32 devices in a mesh: gx: 4 (over y, x), gy: 8 (over z, core).
Axes of the slice: x: 2, y: 2, z: 4, core: 2. Of those that a mesh axis runs over, the one named last changes fastest.
Arguments:
- conserved: float32 [5, 4, 4, 4, 16, 16, 128], P(None, None, None, None, 'gx', 'gy'), as said below
- troubled_list: int32 [16384], P(('gx', 'gy')), may hold values from 0 to 1024, as said below
- widths_x: float32 [16], replicated, may hold values from 1 to 3
- widths_y: float32 [16], replicated, may hold values from 1 to 3
- widths_z: float32 [128], replicated, may hold values from 1 to 3
- speed_x: float32 [16], replicated, may hold values from -0.5 to 0.5
- speed_y: float32 [16], replicated, may hold values from -0.5 to 0.5
- speed_z: float32 [128], replicated, may hold values from -0.5 to 0.5
Outputs:
- advanced: float32 [5, 4, 4, 4, 16, 16, 128], P(None, None, None, None, 'gx', 'gy')
- hessian: float32 [6, 16, 16, 128], P(None, 'gx', 'gy')
The draws below stay inside these ranges and needn't reach their ends.
Inputs may be any that keep to these rules, and one draw needn't show every extreme that they name: `conserved`: density lies between 0.5 and 2 and the pressure computed from the state between 0.5 and 2 at every node. `troubled_list`: in each device's block the first c entries are distinct element indices in increasing order and the rest equal 1024; c is at most 512 and reaches 512 on some device, and the c of all devices sum to exactly 8192.
All inputs are finite; a program needn't handle non-finite values.
Results may differ from the reference program's by a relative error of at most 0.0003.
Values sent between devices are 32-bit elements; how exact they have to be, the bound alone decides.
A program may use at most 64 MiB of HBM per device.

```python
import math
import jax
import jax.numpy as jnp
import numpy as np
from jax import lax

EX = 4
EY = 2
EZ = 128
BAL = 256
NEX = 16
NEY = 16
N_GX = 4
N_GY = 8
DEVICES = 32


def draw_conserved(key, part):
    subkeys = jax.random.split(key, 3)
    grid_shape = (4, 4, 4, NEX, NEY, EZ)
    density = jnp.exp(jax.random.uniform(subkeys[0], grid_shape, jnp.float32, math.log(0.5), math.log(2.0)))
    velocity = jnp.clip(0.4 * jax.random.normal(subkeys[1], (3,) + grid_shape, jnp.float32), -1.5, 1.5)
    pressure = jnp.exp(jax.random.uniform(subkeys[2], grid_shape, jnp.float32, math.log(0.5), math.log(2.0)))
    momentum = density[None] * velocity
    energy = pressure / 0.4 + 0.5 * density * (velocity[0] * velocity[0] + velocity[1] * velocity[1] + velocity[2] * velocity[2])
    return jnp.concatenate([density[None], momentum, energy[None]], axis=0).astype(jnp.float32)


def draw_troubled_list(key, part):
    elements = EX * EY * EZ
    key_order, key_spread, key_pick = jax.random.split(key, 3)
    placing = jax.random.permutation(key_order, DEVICES)
    spreads = jax.random.randint(key_spread, (DEVICES // 2,), 0, BAL + 1).at[0].set(BAL)
    positions = jnp.arange(DEVICES)
    signed = jnp.where(positions % 2 == 0, 1, -1) * spreads[positions // 2]
    counts = jnp.zeros((DEVICES,), jnp.int32).at[placing].set((BAL + signed).astype(jnp.int32))

    def pick_one(device_key, count):
        ranking = jax.random.permutation(device_key, elements)
        element_ids = jnp.arange(elements, dtype=jnp.int32)
        scores = jnp.where(ranking < count, element_ids, elements + element_ids)
        ordered = jnp.sort(scores)[:2 * BAL]
        return jnp.where(ordered < elements, ordered, elements)
    lists = jax.vmap(pick_one)(jax.random.split(key_pick, DEVICES), counts)
    return lists.reshape(-1).astype(jnp.int32)


def setup_inputs(seed: int = 0) -> dict:
    seeds = jax.random.split(jax.random.key(seed), 9)
    return {
        "conserved": draw_conserved(jax.random.fold_in(seeds[8], 71), 0),
        "troubled_list": draw_troubled_list(jax.random.fold_in(seeds[8], 71), 0),
        "widths_x": jnp.clip(jnp.exp(jax.random.uniform(seeds[2], (NEX,), jnp.float32, math.log(1.0), math.log(3.0))), 1.0, 3.0),
        "widths_y": jnp.clip(jnp.exp(jax.random.uniform(seeds[3], (NEY,), jnp.float32, math.log(1.0), math.log(3.0))), 1.0, 3.0),
        "widths_z": jnp.clip(jnp.exp(jax.random.uniform(seeds[4], (EZ,), jnp.float32, math.log(1.0), math.log(3.0))), 1.0, 3.0),
        "speed_x": jnp.clip(jax.random.uniform(seeds[5], (NEX,), jnp.float32, -0.5, 0.5), -0.5, 0.5),
        "speed_y": jnp.clip(jax.random.uniform(seeds[6], (NEY,), jnp.float32, -0.5, 0.5), -0.5, 0.5),
        "speed_z": jnp.clip(jax.random.uniform(seeds[7], (EZ,), jnp.float32, -0.5, 0.5), -0.5, 0.5),
    }


time_step = 0.05
gamma_ratio = 1.4

def lgl_tables():
    nodes = np.array([-1.0, -1.0 / np.sqrt(5.0), 1.0 / np.sqrt(5.0), 1.0])
    weights = np.array([1.0 / 6.0, 5.0 / 6.0, 5.0 / 6.0, 1.0 / 6.0])
    barycentric = np.ones(4)
    for row_a in range(4):
        for row_b in range(4):
            if row_a != row_b:
                barycentric[row_a] = barycentric[row_a] / (nodes[row_a] - nodes[row_b])
    deriv = np.zeros((4, 4))
    for row_a in range(4):
        for row_b in range(4):
            if row_a != row_b:
                deriv[row_a, row_b] = barycentric[row_b] / barycentric[row_a] / (nodes[row_a] - nodes[row_b])
    for row_a in range(4):
        deriv[row_a, row_a] = -np.sum(deriv[row_a])
    return (nodes, weights, deriv)

def euler_flux(conserved, direction, mesh_speed):
    density = conserved[0]
    normal_vel = conserved[direction + 1] / density
    kinetic = 0.5 * (conserved[1] * conserved[1] + conserved[2] * conserved[2] + conserved[3] * conserved[3]) / density
    pressure = (gamma_ratio - 1.0) * (conserved[4] - kinetic)
    relative = normal_vel - mesh_speed
    columns_out = [conserved[component] * relative for component in range(5)]
    columns_out[direction + 1] = columns_out[direction + 1] + pressure
    columns_out[4] = columns_out[4] + pressure * normal_vel
    sound = jnp.sqrt(gamma_ratio * pressure / density)
    return (jnp.stack(columns_out), jnp.abs(relative) + sound)

def rusanov(lower_state, upper_state, direction, mesh_speed):
    flux_low, speed_low = euler_flux(lower_state, direction, mesh_speed)
    flux_high, speed_high = euler_flux(upper_state, direction, mesh_speed)
    return 0.5 * (flux_low + flux_high) - 0.5 * jnp.maximum(speed_low, speed_high) * (upper_state - lower_state)

def face_rates(conserved, x_lower, x_upper, y_lower, y_upper, scale_x, scale_y, scale_z, faces_x, faces_y, faces_z):
    nodes, weights, deriv = lgl_tables()
    tile_x, tile_y, column = (conserved.shape[4], conserved.shape[5], conserved.shape[6])
    deriv_mat = jnp.asarray(deriv, jnp.float32)
    lower_half = jnp.asarray((1.0 - nodes) / 2.0, jnp.float32)
    upper_half = jnp.asarray((1.0 + nodes) / 2.0, jnp.float32)
    first_w = float(weights[0])
    last_w = float(weights[3])
    exact = lax.Precision.HIGHEST
    node_x = (faces_x[None, :-1] * lower_half[:, None] + faces_x[None, 1:] * upper_half[:, None]).reshape(4, 1, 1, tile_x, 1, 1)
    flux_x = euler_flux(conserved, 0, node_x)[0]
    grad_x = jnp.einsum('pa,vabcijk->vpbcijk', deriv_mat, flux_x, precision=exact)
    star_x = rusanov(jnp.concatenate([x_lower, conserved[:, 3]], axis=3), jnp.concatenate([conserved[:, 0], x_upper], axis=3), 0, faces_x.reshape(1, 1, tile_x + 1, 1, 1))
    low_x = star_x[:, :, :, :-1]
    high_x = star_x[:, :, :, 1:]
    blank_x = jnp.zeros_like(low_x)
    dg_x = -scale_x * (grad_x + jnp.stack([-(low_x - flux_x[:, 0]) / first_w, blank_x, blank_x, (high_x - flux_x[:, 3]) / last_w], axis=1))
    fv_x = scale_x * jnp.stack([low_x / first_w, blank_x, blank_x, -high_x / last_w], axis=1)
    node_y = (faces_y[None, :-1] * lower_half[:, None] + faces_y[None, 1:] * upper_half[:, None]).reshape(1, 4, 1, 1, tile_y, 1)
    flux_y = euler_flux(conserved, 1, node_y)[0]
    grad_y = jnp.einsum('pb,vabcijk->vapcijk', deriv_mat, flux_y, precision=exact)
    star_y = rusanov(jnp.concatenate([y_lower, conserved[:, :, 3]], axis=4), jnp.concatenate([conserved[:, :, 0], y_upper], axis=4), 1, faces_y.reshape(1, 1, 1, tile_y + 1, 1))
    low_y = star_y[:, :, :, :, :-1]
    high_y = star_y[:, :, :, :, 1:]
    blank_y = jnp.zeros_like(low_y)
    dg_y = -scale_y * (grad_y + jnp.stack([-(low_y - flux_y[:, :, 0]) / first_w, blank_y, blank_y, (high_y - flux_y[:, :, 3]) / last_w], axis=2))
    fv_y = scale_y * jnp.stack([low_y / first_w, blank_y, blank_y, -high_y / last_w], axis=2)
    next_z = jnp.roll(faces_z, -1)
    node_z = (faces_z[None, :] * lower_half[:, None] + next_z[None, :] * upper_half[:, None]).reshape(1, 1, 4, 1, 1, column)
    flux_z = euler_flux(conserved, 2, node_z)[0]
    grad_z = jnp.einsum('pc,vabcijk->vabpijk', deriv_mat, flux_z, precision=exact)
    star_z = rusanov(jnp.roll(conserved[:, :, :, 3], 1, axis=5), conserved[:, :, :, 0], 2, faces_z.reshape(1, 1, 1, 1, column))
    low_z = star_z
    high_z = jnp.roll(star_z, -1, axis=5)
    blank_z = jnp.zeros_like(low_z)
    dg_z = -scale_z * (grad_z + jnp.stack([-(low_z - flux_z[:, :, :, 0]) / first_w, blank_z, blank_z, (high_z - flux_z[:, :, :, 3]) / last_w], axis=3))
    fv_z = scale_z * jnp.stack([low_z / first_w, blank_z, blank_z, -high_z / last_w], axis=3)
    return (dg_x + dg_y + dg_z, fv_x + fv_y + fv_z)

def fv_interior(conserved, scale_x, scale_y, scale_z, low_x, high_x, low_y, high_y, low_z, high_z):
    nodes, weights, deriv = lgl_tables()
    interfaces_xi = (-5.0 / 6.0, 0.0, 5.0 / 6.0)

    def direction_rate(direction, lower_speed, upper_speed):
        fluxes = []
        for interface in range(3):
            speed_here = lower_speed * ((1.0 - interfaces_xi[interface]) / 2.0) + upper_speed * ((1.0 + interfaces_xi[interface]) / 2.0)
            left_state = lax.index_in_dim(conserved, interface, direction + 1, keepdims=False)
            right_state = lax.index_in_dim(conserved, interface + 1, direction + 1, keepdims=False)
            fluxes.append(rusanov(left_state, right_state, direction, speed_here))
        jumps = jnp.stack([fluxes[0], fluxes[1] - fluxes[0], fluxes[2] - fluxes[1], -fluxes[2]], axis=direction + 1)
        shaped = [1] * conserved.ndim
        shaped[direction + 1] = 4
        return jumps / jnp.asarray(weights, jnp.float32).reshape(shaped)
    return -scale_x * direction_rate(0, low_x, high_x) - scale_y * direction_rate(1, low_y, high_y) - scale_z * direction_rate(2, low_z, high_z)

def corner_hessian(density, inv_x, inv_y, inv_z):
    nodes, weights, deriv = lgl_tables()
    first_order = jnp.asarray(deriv[[0, 3]], jnp.float32)
    second_order = jnp.asarray((deriv @ deriv)[[0, 3]], jnp.float32)
    select_rows = jnp.asarray(np.eye(4)[[0, 3]], jnp.float32)

    def contract(along_a, along_b, along_c):
        return jnp.einsum('pa,qb,rc,abcijk->pqrijk', along_a, along_b, along_c, density, precision=lax.Precision.HIGHEST)
    return jnp.stack([contract(second_order, select_rows, select_rows) * inv_x * inv_x, contract(select_rows, second_order, select_rows) * inv_y * inv_y, contract(select_rows, select_rows, second_order) * inv_z * inv_z, contract(first_order, first_order, select_rows) * inv_x * inv_y, contract(first_order, select_rows, first_order) * inv_x * inv_z, contract(select_rows, first_order, first_order) * inv_y * inv_z])

def reference(conserved, troubled_list, widths_x, widths_y, widths_z, speed_x, speed_y, speed_z):
    count_x = widths_x.shape[0]
    count_y = widths_y.shape[0]
    column = widths_z.shape[0]
    local_count = EX * EY * EZ
    devices = N_GX * N_GY
    listed = troubled_list.reshape(devices, 2 * BAL)
    owners = jnp.broadcast_to(jnp.arange(devices, dtype=jnp.int32)[:, None], listed.shape)
    marks = jnp.zeros((devices, local_count), bool).at[owners, listed].set(True, mode='drop')
    marks = marks.reshape(N_GX, N_GY, EX, EY, EZ).transpose(0, 2, 1, 3, 4).reshape(count_x, count_y, column)
    next_x = jnp.roll(speed_x, -1)
    new_x = widths_x + time_step * (next_x - speed_x)
    new_y = widths_y + time_step * (jnp.roll(speed_y, -1) - speed_y)
    new_z = widths_z + time_step * (jnp.roll(speed_z, -1) - speed_z)
    faces_y = jnp.concatenate([speed_y, speed_y[:1]])
    scale_y = (2.0 / widths_y).reshape(1, count_y, 1)
    scale_z = (2.0 / widths_z).reshape(1, 1, column)
    low_y = speed_y.reshape(1, count_y, 1)
    high_y = faces_y[1:].reshape(1, count_y, 1)
    low_z = speed_z.reshape(1, 1, column)
    high_z = jnp.roll(speed_z, -1).reshape(1, 1, column)

    def slab(index_x):
        current = lax.dynamic_slice_in_dim(conserved, index_x, 1, 4)
        x_lower = lax.dynamic_slice_in_dim(conserved, (index_x + count_x - 1) % count_x, 1, 4)[:, 3]
        x_upper = lax.dynamic_slice_in_dim(conserved, (index_x + 1) % count_x, 1, 4)[:, 0]
        y_lower = current[:, :, 3][:, :, :, :, -1:]
        y_upper = current[:, :, 0][:, :, :, :, 0:1]
        width_here = lax.dynamic_slice_in_dim(widths_x, index_x, 1)
        faces_x = jnp.concatenate([lax.dynamic_slice_in_dim(speed_x, index_x, 1), lax.dynamic_slice_in_dim(next_x, index_x, 1)])
        scale_x = (2.0 / width_here).reshape(1, 1, 1)
        dg_rate, fv_face = face_rates(current, x_lower, x_upper, y_lower, y_upper, scale_x, scale_y, scale_z, faces_x, faces_y, speed_z)
        inner = fv_interior(current, scale_x, scale_y, scale_z, faces_x[0:1].reshape(1, 1, 1), faces_x[1:2].reshape(1, 1, 1), low_y, high_y, low_z, high_z)
        troubled = lax.dynamic_slice_in_dim(marks, index_x, 1, 0)
        rate = jnp.where(troubled, fv_face + inner, dg_rate)
        new_here = lax.dynamic_slice_in_dim(new_x, index_x, 1)
        ratio = width_here.reshape(1, 1, 1) * widths_y.reshape(1, count_y, 1) * widths_z.reshape(1, 1, column) / (new_here.reshape(1, 1, 1) * new_y.reshape(1, count_y, 1) * new_z.reshape(1, 1, column))
        return (ratio * (current + time_step * rate))[:, :, :, :, 0]
    advanced = jnp.moveaxis(lax.map(slab, jnp.arange(count_x, dtype=jnp.int32)), 0, 4)
    inv_x = (2.0 / new_x).reshape(count_x, 1, 1)
    inv_y = (2.0 / new_y).reshape(1, count_y, 1)
    inv_z = (2.0 / new_z).reshape(1, 1, column)
    mass = new_x.reshape(count_x, 1, 1) * new_y.reshape(1, count_y, 1) * new_z.reshape(1, 1, column)
    weighted = corner_hessian(advanced[0], inv_x, inv_y, inv_z) * mass
    totals = jnp.zeros((6, count_x, count_y, column), jnp.float32)
    for side_x in (0, 1):
        for side_y in (0, 1):
            for side_z in (0, 1):
                totals = totals + jnp.roll(weighted[:, side_x, side_y, side_z], (side_x, side_y, side_z), axis=(1, 2, 3))
    denominator = (new_x + jnp.roll(new_x, 1)).reshape(count_x, 1, 1) * (new_y + jnp.roll(new_y, 1)).reshape(1, count_y, 1) * (new_z + jnp.roll(new_z, 1)).reshape(1, 1, column)
    return (advanced, totals / denominator)
```

```python
import functools

import jax
import jax.numpy as jnp
import numpy as np
from jax import lax
from jax.experimental import pallas as pl
from jax.experimental.pallas import tpu as pltpu
from jax.sharding import PartitionSpec as P

MESH = pl.DeviceIdType.MESH
time_step = 0.05
gamma_ratio = 1.4


def lgl_tables():
    nodes = np.array([-1.0, -1.0 / np.sqrt(5.0), 1.0 / np.sqrt(5.0), 1.0])
    weights = np.array([1.0 / 6.0, 5.0 / 6.0, 5.0 / 6.0, 1.0 / 6.0])
    barycentric = np.ones(4)
    for row_a in range(4):
        for row_b in range(4):
            if row_a != row_b:
                barycentric[row_a] = barycentric[row_a] / (nodes[row_a] - nodes[row_b])
    deriv = np.zeros((4, 4))
    for row_a in range(4):
        for row_b in range(4):
            if row_a != row_b:
                deriv[row_a, row_b] = (
                    barycentric[row_b] / barycentric[row_a] / (nodes[row_a] - nodes[row_b])
                )
    for row_a in range(4):
        deriv[row_a, row_a] = -np.sum(deriv[row_a])
    return (nodes, weights, deriv)


NODES, WEIGHTS, DERIV = lgl_tables()
SPEED, INTER, SCALE, FACE = 0, 12, 21, 27
RATIO, MASK, GEO = 33, 34, 35
ALL, DENSITY, REST = (0, 1, 2, 3, 4), (0,), (1, 2, 3, 4)


def primitives(state):
    inverse = 1.0 / state[0]
    square = state[1] * state[1] + state[2] * state[2] + state[3] * state[3]
    pressure = (gamma_ratio - 1.0) * (state[4] - 0.5 * square * inverse)
    ratio = gamma_ratio * pressure * inverse
    return inverse, pressure, ratio * lax.rsqrt(ratio)


def twice_flux(low, p_low, c_low, u_low, high, p_high, c_high, u_high, direction, speed):
    rel_low = u_low - speed
    rel_high = u_high - speed
    fastest = jnp.maximum(jnp.abs(rel_low) + c_low, jnp.abs(rel_high) + c_high)
    left = rel_low + fastest
    right = rel_high - fastest
    flux = [low[v] * left + high[v] * right for v in range(5)]
    flux[direction + 1] = flux[direction + 1] + (p_low + p_high)
    flux[4] = flux[4] + (p_low * u_low + p_high * u_high)
    return flux


def dg_table():
    lifted = DERIV.copy()
    lifted[0, 0] += 1.0 / WEIGHTS[0]
    lifted[3, 3] -= 1.0 / WEIGHTS[3]
    return np.cumsum(2.0 * WEIGHTS[:, None] * lifted, axis=0)


SUBCELL = dg_table()


def dg_fluxes(values):
    outer, inner = values[0] + values[3], values[1] + values[2]
    step = inner - outer
    even = outer + float(0.5 * (SUBCELL[0, 1] + SUBCELL[2, 1])) * step
    middle = outer + float(SUBCELL[1, 1]) * step
    odd = float(0.5 * (SUBCELL[0, 0] - SUBCELL[2, 0])) * (values[0] - values[3])
    odd = odd + float(0.5 * (SUBCELL[0, 1] - SUBCELL[2, 1])) * (values[1] - values[2])
    return even + odd, middle, even - odd


def wave_weights(u_low, c_low, u_high, c_high, speed):
    rel_low = u_low - speed
    rel_high = u_high - speed
    fastest = jnp.maximum(jnp.abs(rel_low) + c_low, jnp.abs(rel_high) + c_high)
    return rel_low + fastest, rel_high - fastest


def kernel(
    tile_x,
    tile_y,
    sizes,
    cons_hbm,
    list_hbm,
    wx_hbm,
    wy_hbm,
    wz_hbm,
    sx_hbm,
    sy_hbm,
    sz_hbm,
    out,
    hess_ref,
    list_ref,
    wx_ref,
    wy_ref,
    wz_ref,
    sx_ref,
    sy_ref,
    sz_ref,
    state,
    inv_s,
    pres_s,
    sound_s,
    zl,
    zst,
    ph,
    geo,
    cs,
    cr,
    xs,
    xr,
    ys,
    yr,
    rxs,
    rxr,
    rys,
    ryr,
    rds,
    rdr,
    io_sem,
    send_sem,
    recv_sem,
):
    size_x, size_y = sizes
    rows = tile_x * tile_y
    lanes = state.shape[-1]
    me_x, me_y = lax.axis_index("gx"), lax.axis_index("gy")
    up_x, down_x = lax.rem(me_x + 1, size_x), lax.rem(me_x + size_x - 1, size_x)
    up_y, down_y = lax.rem(me_y + 1, size_y), lax.rem(me_y + size_y - 1, size_y)

    barrier = pltpu.get_barrier_semaphore()
    partners = ((me_x, down_y), (me_x, up_y), (down_x, me_y), (up_x, me_y))
    for partner in partners:
        pl.semaphore_signal(barrier, inc=1, device_id=partner, device_id_type=MESH)
    small = [
        pltpu.make_async_copy(src, dst, io_sem.at[4 + n])
        for n, (src, dst) in enumerate(
            (
                (wx_hbm, wx_ref),
                (wy_hbm, wy_ref),
                (sx_hbm, sx_ref),
                (sy_hbm, sy_ref),
                (wz_hbm, wz_ref),
                (sz_hbm, sz_ref),
                (list_hbm, list_ref),
            )
        )
    ]
    loads = [pltpu.make_async_copy(cons_hbm.at[:, a], state.at[:, a], io_sem.at[a]) for a in range(4)]
    for a in (0, 3, 1, 2):
        loads[a].start()
    for copy in small:
        copy.start()

    shape = (rows, lanes)
    row = lax.broadcasted_iota(jnp.int32, shape, 0)
    row_i, row_j = row // tile_y, row % tile_y

    def roll_rows(value, shift):
        shift = shift % rows
        return value if shift == 0 else pltpu.roll(value, shift, 0)

    def roll_lanes(value, shift):
        return pltpu.roll(value, shift % lanes, 1)

    def pack_x(q, carry):
        for v in range(5):
            for side, node, first in ((0, 0, 0), (1, 3, rows - tile_y)):
                packed = None
                for c in range(4):
                    part = roll_rows(state[v, node, q, c], tile_y * c - first)
                    packed = part if packed is None else jnp.where(row_i == c, part, packed)
                xs[side, v, q] = packed
        return carry

    def pack_y(q, carry):
        for v in range(5):
            for side, node, first in ((0, 0, 0), (1, 3, tile_y - 1)):
                for group in range(4 // tile_y):
                    packed = None
                    for c in range(tile_y):
                        part = roll_rows(state[v, q, node, group * tile_y + c], c - first)
                        packed = part if packed is None else jnp.where(row_j == c, part, packed)
                    ys[side, v, q, group] = packed
        return carry

    last_i, last_j = tile_x - 1, tile_y - 1
    early = ((0, 0, last_j), (0, 1, rows - 1), (1, 0, rows - tile_y), (1, 1, rows - 1))

    def pack_early(v, carry):
        for slot, (d, side, place) in enumerate(early):
            for group in range(16 // rows):
                packed = None
                for sub in range(rows):
                    q, c = (group * rows + sub) // 4, (group * rows + sub) % 4
                    value = state[v, 3 * side, q, c] if d == 0 else state[v, q, 3 * side, c]
                    part = roll_rows(value, sub - place)
                    packed = part if packed is None else jnp.where(row == sub, part, packed)
                cs[slot, v, group] = packed
        return carry

    def remote(src, dst, slot, device):
        return pltpu.make_async_remote_copy(
            src_ref=src,
            dst_ref=dst,
            send_sem=send_sem.at[slot],
            recv_sem=recv_sem.at[slot],
            device_id=device,
            device_id_type=MESH,
        )

    for a in (0, 3, 1, 2):
        loads[a].wait()
    lax.fori_loop(0, 5, pack_early, 0)
    pl.semaphore_wait(barrier, len(partners))
    heralds = [
        remote(cs.at[2], cr.at[3], 9, (me_x, down_y)),
        remote(cs.at[3], cr.at[2], 10, (me_x, up_y)),
        remote(cs.at[0], cr.at[1], 7, (down_x, me_y)),
        remote(cs.at[1], cr.at[0], 8, (up_x, me_y)),
    ]
    for copy in heralds:
        copy.start()
    faces = [
        remote(ys.at[0], yr.at[1], 2, (me_x, down_y)),
        remote(ys.at[1], yr.at[0], 3, (me_x, up_y)),
        remote(xs.at[0], xr.at[1], 0, (down_x, me_y)),
        remote(xs.at[1], xr.at[0], 1, (up_x, me_y)),
    ]
    lax.fori_loop(0, 4, pack_y, 0)
    faces[0].start()
    faces[1].start()
    lax.fori_loop(0, 4, pack_x, 0)
    faces[2].start()
    faces[3].start()
    for copy in small:
        copy.wait()

    def along(ref, start, total, tile, index):
        values = [ref[lax.rem(start + total + i, total)] for i in range(-1, tile + 1)]

        def pick(offset):
            vector = jnp.full(shape, values[1 + offset], jnp.float32)
            for i in range(1, tile):
                vector = jnp.where(index == i, values[1 + offset + i], vector)
            return vector

        return pick(-1), pick(0), pick(1)

    total_x, total_y = size_x * tile_x, size_y * tile_y
    wx_p, wx, _ = along(wx_ref, me_x * tile_x, total_x, tile_x, row_i)
    wy_p, wy, _ = along(wy_ref, me_y * tile_y, total_y, tile_y, row_j)
    sx_p, sx, sx_n = along(sx_ref, me_x * tile_x, total_x, tile_x, row_i)
    sy_p, sy, sy_n = along(sy_ref, me_y * tile_y, total_y, tile_y, row_j)
    wz = jnp.broadcast_to(wz_ref[...], shape)
    sz = jnp.broadcast_to(sz_ref[...], shape)
    sz_n = roll_lanes(sz, -1)
    nx, ny, nz = (
        wx + time_step * (sx_n - sx),
        wy + time_step * (sy_n - sy),
        wz + time_step * (sz_n - sz),
    )
    px, py = wx_p + time_step * (sx - sx_p), wy_p + time_step * (sy - sy_p)
    pz = roll_lanes(nz, 1)
    mass = nx * ny * nz
    ratio = wx * wy * wz / mass
    geo[RATIO] = ratio
    for d, (width, low, high) in enumerate(((wx, sx, sx_n), (wy, sy, sy_n), (wz, sz, sz_n))):
        for a in range(4):
            geo[SPEED + 4 * d + a] = low * float((1.0 - NODES[a]) / 2.0) + high * float(
                (1.0 + NODES[a]) / 2.0
            )
        for q, xi in enumerate((-5.0 / 6.0, 0.0, 5.0 / 6.0)):
            geo[INTER + 3 * d + q] = low * ((1.0 - xi) / 2.0) + high * ((1.0 + xi) / 2.0)
        geo[FACE + 2 * d] = low
        geo[FACE + 2 * d + 1] = high
        kappa = -time_step * ratio / width
        geo[SCALE + 2 * d] = kappa * float(1.0 / WEIGHTS[0])
        geo[SCALE + 2 * d + 1] = kappa * float(1.0 / WEIGHTS[1])

    entries = list_ref[...]
    count = entries.shape[-1]
    in_row = jnp.where(
        lax.broadcasted_iota(jnp.int32, (rows, count), 0) == entries // lanes, 1.0, 0.0
    )
    in_lane = jnp.where(
        lax.broadcasted_iota(jnp.int32, (lanes, count), 0) == entries % lanes, 1.0, 0.0
    )
    geo[MASK] = lax.dot_general(
        in_row, in_lane, (((1,), (1,)), ((), ())), preferred_element_type=jnp.float32
    )

    def prepare(a, carry):
        for b in range(4):
            for c in range(4):
                inverse, pressure, sound = primitives([state[v, a, b, c] for v in range(5)])
                inv_s[a, b, c] = inverse
                pres_s[a, b, c] = pressure
                sound_s[a, b, c] = sound
            zl[0, a, b] = roll_lanes(state[0, a, b, 3], 1)
            zl[3, a, b] = roll_lanes(state[3, a, b, 3] * inverse, 1)
            zl[5, a, b] = roll_lanes(sound, 1)
        return carry

    lax.fori_loop(0, 4, prepare, 0)

    def interior(d, parts, index, carry):
        first, second = index // 4, index % 4

        def at(n):
            return ((n, first, second), (first, n, second), (first, second, n))[d]

        mask = geo[MASK] > 0.5
        sound = [sound_s[at(n)] for n in range(4)]
        normal = [state[(d + 1,) + at(n)] * inv_s[at(n)] for n in range(4)]
        weights = [
            wave_weights(normal[q], sound[q], normal[q + 1], sound[q + 1], geo[INTER + 3 * d + q])
            for q in range(3)
        ]
        relative = [normal[n] - geo[SPEED + 4 * d + n] for n in range(4)]
        if parts != DENSITY:
            pressure = [pres_s[at(n)] for n in range(4)]
            work = [pressure[n] * normal[n] for n in range(4)]
        if d == 2:
            behind = zl[3, first, second]
            star_left, star_right = wave_weights(
                behind, zl[5, first, second], normal[0], sound[0], geo[FACE + 4]
            )
            if parts != DENSITY:
                push = zl[6, first, second]
        for v in parts:
            value = [state[(v,) + at(n)] for n in range(4)]
            flux = [value[n] * relative[n] for n in range(4)]
            inner = [value[q] * weights[q][0] + value[q + 1] * weights[q][1] for q in range(3)]
            if d == 2:
                if v == 3:
                    rolled = zl[7, first, second]
                else:
                    rolled = zl[v, first, second]
                star = rolled * star_left + value[0] * star_right
            extra = pressure if v == d + 1 else work if v == 4 else None
            if extra is not None:
                flux = [flux[n] + extra[n] for n in range(4)]
                inner = [inner[q] + (extra[q] + extra[q + 1]) for q in range(3)]
            if d == 2:
                if v == 3:
                    star = star + (push + pressure[0])
                if v == 4:
                    star = star + (push * behind + work[0])
                zst[v, first, second] = star
            smooth = dg_fluxes(flux)
            chosen = [jnp.where(mask, inner[q], smooth[q]) for q in range(3)]
            head = chosen[0] - star if d == 2 else chosen[0]
            change = [head, chosen[1] - chosen[0], chosen[2] - chosen[1], -chosen[2]]
            for n in range(4):
                where = (v,) + at(n)
                scale = geo[SCALE + 2 * d + (0 if n in (0, 3) else 1)]
                if d == 0:
                    base = geo[RATIO] * value[n]
                else:
                    base = out[where]
                out[where] = base + scale * change[n]
        return carry

    def above(v, a):
        for b in range(4):
            out[v, a, b, 3] = out[v, a, b, 3] + geo[SCALE + 4] * roll_lanes(zst[v, a, b], -1)

    for d in range(3):
        lax.fori_loop(0, 16, functools.partial(interior, d, DENSITY), 0)
    for a in range(4):
        above(0, a)

    def spots(d, q, c):
        return ((0, q, c), (3, q, c)) if d == 0 else ((q, 0, c), (q, 3, c))

    def inside(d, q, carry):
        shift = (tile_y, 1)[d]
        edge = (row_i, row_j)[d]
        for c in range(4):
            low, high = spots(d, q, c)
            left, right = wave_weights(
                roll_rows(state[(d + 1,) + high] * inv_s[high], shift),
                roll_rows(sound_s[high], shift),
                state[(d + 1,) + low] * inv_s[low],
                sound_s[low],
                geo[FACE + 2 * d],
            )
            star = roll_rows(state[(0,) + high], shift) * left + state[(0,) + low] * right
            star = jnp.where(edge > 0, star, 0.0)
            scale = geo[SCALE + 2 * d]
            out[(0,) + low] = out[(0,) + low] - scale * star
            out[(0,) + high] = out[(0,) + high] + scale * roll_rows(star, -shift)
        return carry

    for d in range(2):
        lax.fori_loop(0, 4, functools.partial(inside, d), 0)

    second = DERIV @ DERIV
    ends = (0, 3)

    def combine(coefficients, values):
        total = None
        for n in range(4):
            if values[n] is not None:
                term = float(coefficients[n]) * values[n]
                total = term if total is None else total + term
        return total

    def columns(density, factors, wanted):
        along_x = {
            (p, b, c): combine(DERIV[p], [density[a][b][c] for a in range(4)])
            for p in ends
            for b in range(4)
            for c in range(4)
            if b in ends or c in ends
        }
        along_y = {
            (a, q, c): combine(DERIV[q], [density[a][b][c] for b in range(4)])
            for q in ends
            for a in ends
            for c in range(4)
        }

        def corner(kind, p, q, r):
            if kind == 0:
                return combine(second[p], [density[a][q][r] for a in range(4)])
            if kind == 1:
                return combine(second[q], [density[p][b][r] for b in range(4)])
            if kind == 2:
                return combine(second[r], [density[p][q][c] for c in range(4)])
            if kind == 3:
                return combine(DERIV[q], [along_x[p, b, r] for b in range(4)])
            if kind == 4:
                return combine(DERIV[r], [along_x[p, q, c] for c in range(4)])
            return combine(DERIV[r], [along_y[p, q, c] for c in range(4)])

        found = []
        for kind in range(6):
            column = {}
            for p, q in wanted:
                low, high = corner(kind, p, q, 0), corner(kind, p, q, 3)
                column[p, q] = factors[kind] * low + roll_lanes(factors[kind] * high, 1)
            found.append(column)
        return found

    def pairs(jx, jy, jz):
        return (jx * jx, jy * jy, jz * jz, jx * jy, jx * jz, jy * jz)

    ix, iy, iz = 2.0 / nx, 2.0 / ny, 2.0 / nz
    factors = [mass * pair for pair in pairs(ix, iy, iz)]

    def up_y_shift(value):
        return jnp.where(row_j == 0, 0.0, roll_rows(value, 1))

    def up_x_shift(value):
        return jnp.where(row_i == 0, 0.0, roll_rows(value, tile_y))

    for copy in heralds:
        copy.wait()
    density = [[[out[0, a, b, c] for c in range(4)] for b in range(4)] for a in range(4)]
    for slot, (d, side, place) in enumerate(early):
        for group in range(16 // rows):
            own = [cs[slot, v, group] for v in range(5)]
            other = [cr[slot, v, group] for v in range(5)]
            low, high = (other, own) if side == 0 else (own, other)
            low_inverse, _, low_sound = primitives(low)
            high_inverse, _, high_sound = primitives(high)
            left, right = wave_weights(
                low[d + 1] * low_inverse,
                low_sound,
                high[d + 1] * high_inverse,
                high_sound,
                geo[FACE + 2 * d + side, place : place + 1],
            )
            scale = geo[SCALE + 2 * d, place : place + 1]
            delta = (scale if side else -scale) * (low[0] * left + high[0] * right)
            for sub in range(rows):
                q, c = (group * rows + sub) // 4, (group * rows + sub) % 4
                a, b = (3 * side, q) if d == 0 else (q, 3 * side)
                part = jnp.where(row == place, roll_rows(delta, place - sub), 0.0)
                density[a][b][c] = density[a][b][c] + part
    for a in range(4):
        for b in range(4):
            if a in ends or b in ends:
                for c in range(4):
                    out[0, a, b, c] = density[a][b][c]

    x_rim = [None] * -(-6 // tile_x)
    y_rim = [None] * -(-6 // tile_y)
    d_rim = None
    for kind, column in enumerate(columns(density, factors, ((0, 3), (3, 0), (3, 3)))):
        high_x = column[3, 0] + up_y_shift(column[3, 3])
        slot, place = kind // tile_x, kind % tile_x
        part = roll_rows(high_x, tile_y * place - (rows - tile_y))
        x_rim[slot] = part if place == 0 else jnp.where(row_i == place, part, x_rim[slot])
        rim = column[0, 3] + up_x_shift(column[3, 3])
        slot, place = kind // tile_y, kind % tile_y
        part = roll_rows(rim, place - (tile_y - 1))
        y_rim[slot] = part if place == 0 else jnp.where(row_j == place, part, y_rim[slot])
        part = roll_rows(column[3, 3], kind - (rows - 1))
        d_rim = part if kind == 0 else jnp.where(row == kind, part, d_rim)
    for slot, value in enumerate(x_rim):
        rxs[slot] = value
    for slot, value in enumerate(y_rim):
        rys[slot] = value
    rds[...] = d_rim
    rims = [
        remote(rds, rdr, 6, (up_x, up_y)),
        remote(rys, ryr, 5, (me_x, up_y)),
        remote(rxs, rxr, 4, (up_x, me_y)),
    ]
    for copy in rims:
        copy.start()

    def behind_rest(a, carry):
        for b in range(4):
            zl[1, a, b] = roll_lanes(state[1, a, b, 3], 1)
            zl[2, a, b] = roll_lanes(state[2, a, b, 3], 1)
            zl[7, a, b] = roll_lanes(state[3, a, b, 3], 1)
            zl[4, a, b] = roll_lanes(state[4, a, b, 3], 1)
            zl[6, a, b] = roll_lanes(pres_s[a, b, 3], 1)
        return carry

    lax.fori_loop(0, 4, behind_rest, 0)
    for d in range(3):
        lax.fori_loop(0, 16, functools.partial(interior, d, REST), 0)

    def above_rest(a, carry):
        for v in REST:
            above(v, a)
        return carry

    lax.fori_loop(0, 4, above_rest, 0)

    def surface(d, q, carry):
        shift = (tile_y, 1)[d]
        edge, across = ((row_i, row_j), (row_j, row_i))[d]
        last, last_across = ((last_i, last_j), (last_j, last_i))[d]
        speed = geo[FACE + 2 * d]
        top_speed = geo[FACE + 2 * d + 1, rows - 1 : rows]
        scale = geo[SCALE + 2 * d]
        tops = []
        for group in range(1 if d == 0 else 4 // tile_y):
            if d == 0:
                own = [xs[1, v, q] for v in range(5)]
                other = [xr[1, v, q] for v in range(5)]
            else:
                own = [ys[1, v, q, group] for v in range(5)]
                other = [yr[1, v, q, group] for v in range(5)]
            own_inverse, own_pressure, own_sound = primitives(own)
            inverse, pressure, sound = primitives(other)
            tops.append(
                twice_flux(
                    own,
                    own_pressure,
                    own_sound,
                    own[d + 1] * own_inverse,
                    other,
                    pressure,
                    sound,
                    other[d + 1] * inverse,
                    d,
                    top_speed,
                )
            )
        for c in range(4):
            low, high = spots(d, q, c)
            own = [state[(v,) + low] for v in range(5)]
            other = []
            for v in range(5):
                if d == 0:
                    halo = roll_rows(xr[0, v, q], -tile_y * c)
                else:
                    halo = roll_rows(yr[0, v, q, c // tile_y], -(c % tile_y))
                moved = roll_rows(state[(v,) + high], shift)
                other.append(jnp.where(edge == 0, halo, moved))
            inverse, pressure, sound = primitives(other)
            star = twice_flux(
                other,
                pressure,
                sound,
                other[d + 1] * inverse,
                own,
                pres_s[low],
                sound_s[low],
                own[d + 1] * inv_s[low],
                d,
                speed,
            )
            for v in range(5):
                if d == 0:
                    top = roll_rows(tops[0][v], rows - tile_y - tile_y * c)
                else:
                    top = roll_rows(tops[c // tile_y][v], tile_y - 1 - c % tile_y)
                if v == 0:
                    late = across < last_across
                    down = jnp.where(jnp.logical_and(edge == 0, late), star[v], 0.0)
                    up = jnp.where(jnp.logical_and(edge == last, late), top, 0.0)
                    ph[d, q, c] = down
                else:
                    down = star[v]
                    up = jnp.where(edge == last, top, roll_rows(star[v], -shift))
                out[(v,) + low] = out[(v,) + low] - scale * down
                out[(v,) + high] = out[(v,) + high] + scale * up
        return carry

    faces[2].wait()
    faces[3].wait()
    lax.fori_loop(0, 4, functools.partial(surface, 0), 0)
    faces[0].wait()
    faces[1].wait()
    lax.fori_loop(0, 4, functools.partial(surface, 1), 0)

    density = [[[out[0, a, b, c] for c in range(4)] for b in range(4)] for a in range(4)]
    for kind, column in enumerate(columns(density, factors, ((0, 0), (0, 3), (3, 0), (3, 3)))):
        low_x = column[0, 0] + up_y_shift(column[0, 3])
        high_x = column[3, 0] + up_y_shift(column[3, 3])
        hess_ref[kind] = low_x + up_x_shift(high_x)

    bottom = row_j == 0
    ghost_x = jnp.where(bottom, nx, px)
    ghost_y = jnp.where(bottom, py, roll_rows(ny, 1))
    ghost = jnp.where(bottom, wx, roll_rows(wy, 1)) * wz * float(-time_step / WEIGHTS[3])
    ghost_factors = [ghost * pair for pair in pairs(2.0 / ghost_x, 2.0 / ghost_y, iz)]
    field = [[[None] * 4 for b in range(4)] for a in range(4)]
    for n in range(4):
        for c in range(4):
            from_x, from_y = roll_rows(ph[0, n, c], 1), ph[1, n, c]
            if n == 3:
                field[3][3][c] = from_x + from_y
            else:
                field[3][n][c] = from_x
                field[n][3][c] = from_y
    for kind, column in enumerate(columns(field, ghost_factors, ((0, 3), (3, 0), (3, 3)))):
        total = hess_ref[kind] + jnp.where(bottom, column[0, 3], column[3, 3])
        total = total + roll_rows(jnp.where(bottom, column[3, 3], 0.0), tile_y)
        hess_ref[kind] = total + roll_rows(jnp.where(bottom, 0.0, column[3, 0]), -1)

    inverse = 1.0 / ((nx + px) * (ny + py) * (nz + pz))
    for copy in rims:
        copy.wait()
    for kind in range(6):
        total = hess_ref[kind]
        from_x = roll_rows(rxr[kind // tile_x], -tile_y * (kind % tile_x))
        total = total + jnp.where(row_i == 0, from_x, 0.0)
        from_y = roll_rows(ryr[kind // tile_y], -(kind % tile_y))
        total = total + jnp.where(row_j == 0, from_y, 0.0)
        total = total + jnp.where(row == 0, roll_rows(rdr[...], -kind), 0.0)
        hess_ref[kind] = total * inverse


def emit(adv_ref, hess_ref, adv_out, hess_out, sem):
    copies = [
        pltpu.make_async_copy(adv_ref, adv_out, sem.at[0]),
        pltpu.make_async_copy(hess_ref, hess_out, sem.at[1]),
    ]
    for copy in copies:
        copy.start()
    for copy in copies:
        copy.wait()


def solution(mesh):
    sizes = (mesh.shape["gx"], mesh.shape["gy"])

    def local(conserved, troubled_list, widths_x, widths_y, widths_z, speed_x, speed_y, speed_z):
        tile_x, tile_y, column = conserved.shape[4:]
        rows = tile_x * tile_y
        f32 = jnp.float32
        vmem = pl.BlockSpec(memory_space=pltpu.VMEM)
        whole = pl.BlockSpec(memory_space=pl.ANY)
        full = (5, 4, 4, 4, rows, column)
        nodal = (4, 4, 4, rows, column)
        x_face = (2, 5, 4, rows, column)
        y_face = (2, 5, 4, 4 // tile_y, rows, column)
        herald = (4, 5, 16 // rows, rows, column)
        x_rim = (-(-6 // tile_x), rows, column)
        y_rim = (-(-6 // tile_y), rows, column)
        advanced, hessian = pl.pallas_call(
            functools.partial(kernel, tile_x, tile_y, sizes),
            out_shape=(
                pltpu.VMEM(full, f32),
                pltpu.VMEM((6, rows, column), f32),
            ),
            in_specs=[whole] * 8,
            out_specs=(vmem, vmem),
            scratch_shapes=[
                pltpu.VMEM((1, troubled_list.shape[0]), jnp.int32),
                pltpu.SMEM(widths_x.shape, f32),
                pltpu.SMEM(widths_y.shape, f32),
                pltpu.VMEM((1, column), f32),
                pltpu.SMEM(speed_x.shape, f32),
                pltpu.SMEM(speed_y.shape, f32),
                pltpu.VMEM((1, column), f32),
                pltpu.VMEM(full, f32),
                pltpu.VMEM(nodal, f32),
                pltpu.VMEM(nodal, f32),
                pltpu.VMEM(nodal, f32),
                pltpu.VMEM((8, 4, 4, rows, column), f32),
                pltpu.VMEM((5, 4, 4, rows, column), f32),
                pltpu.VMEM((2, 4, 4, rows, column), f32),
                pltpu.VMEM((GEO, rows, column), f32),
                pltpu.VMEM(herald, f32),
                pltpu.VMEM(herald, f32),
                pltpu.VMEM(x_face, f32),
                pltpu.VMEM(x_face, f32),
                pltpu.VMEM(y_face, f32),
                pltpu.VMEM(y_face, f32),
                pltpu.VMEM(x_rim, f32),
                pltpu.VMEM(x_rim, f32),
                pltpu.VMEM(y_rim, f32),
                pltpu.VMEM(y_rim, f32),
                pltpu.VMEM((rows, column), f32),
                pltpu.VMEM((rows, column), f32),
                pltpu.SemaphoreType.DMA((11,)),
                pltpu.SemaphoreType.DMA((11,)),
                pltpu.SemaphoreType.DMA((11,)),
            ],
            compiler_params=pltpu.CompilerParams(collective_id=0, has_side_effects=True),
        )(
            conserved.reshape(full),
            troubled_list.reshape(1, -1),
            widths_x,
            widths_y,
            widths_z.reshape(1, -1),
            speed_x,
            speed_y,
            speed_z.reshape(1, -1),
        )
        advanced = pltpu.with_memory_space_constraint(advanced, pltpu.VMEM)
        hessian = pltpu.with_memory_space_constraint(hessian, pltpu.VMEM)
        advanced, hessian = pl.pallas_call(
            emit,
            out_shape=(
                jax.ShapeDtypeStruct(full, f32),
                jax.ShapeDtypeStruct((6, rows, column), f32),
            ),
            in_specs=[whole, whole],
            out_specs=(whole, whole),
            scratch_shapes=[pltpu.SemaphoreType.DMA((2,))],
        )(advanced, hessian)
        return advanced.reshape(conserved.shape), hessian.reshape(6, tile_x, tile_y, column)

    in_specs = (
        P(None, None, None, None, "gx", "gy", None),
        P(("gx", "gy")),
        P(),
        P(),
        P(),
        P(),
        P(),
        P(),
    )
    out_specs = (P(None, None, None, None, "gx", "gy", None), P(None, "gx", "gy", None))
    return jax.shard_map(local, mesh=mesh, in_specs=in_specs, out_specs=out_specs, check_vma=False)
```

```python
import functools

import jax
import jax.numpy as jnp
import numpy as np
from jax import lax
from jax.experimental import pallas as pl
from jax.experimental.pallas import tpu as pltpu
from jax.sharding import PartitionSpec as P

MESH = pl.DeviceIdType.MESH
time_step = 0.05
gamma_ratio = 1.4


def lgl_tables():
    nodes = np.array([-1.0, -1.0 / np.sqrt(5.0), 1.0 / np.sqrt(5.0), 1.0])
    weights = np.array([1.0 / 6.0, 5.0 / 6.0, 5.0 / 6.0, 1.0 / 6.0])
    barycentric = np.ones(4)
    for row_a in range(4):
        for row_b in range(4):
            if row_a != row_b:
                barycentric[row_a] = barycentric[row_a] / (nodes[row_a] - nodes[row_b])
    deriv = np.zeros((4, 4))
    for row_a in range(4):
        for row_b in range(4):
            if row_a != row_b:
                deriv[row_a, row_b] = (
                    barycentric[row_b] / barycentric[row_a] / (nodes[row_a] - nodes[row_b])
                )
    for row_a in range(4):
        deriv[row_a, row_a] = -np.sum(deriv[row_a])
    return (nodes, weights, deriv)


NODES, WEIGHTS, DERIV = lgl_tables()
SPEED, INTER, SCALE, FACE = 0, 12, 21, 27
RATIO, MASK, GEO = 33, 34, 35
ALL, DENSITY, REST = (0, 1, 2, 3, 4), (0,), (1, 2, 3, 4)


def primitives(state):
    inverse = 1.0 / state[0]
    square = state[1] * state[1] + state[2] * state[2] + state[3] * state[3]
    pressure = (gamma_ratio - 1.0) * (state[4] - 0.5 * square * inverse)
    ratio = gamma_ratio * pressure * inverse
    return inverse, pressure, ratio * lax.rsqrt(ratio)


def twice_flux(low, p_low, c_low, u_low, high, p_high, c_high, u_high, direction, speed):
    rel_low = u_low - speed
    rel_high = u_high - speed
    fastest = jnp.maximum(jnp.abs(rel_low) + c_low, jnp.abs(rel_high) + c_high)
    left = rel_low + fastest
    right = rel_high - fastest
    flux = [low[v] * left + high[v] * right for v in range(5)]
    flux[direction + 1] = flux[direction + 1] + (p_low + p_high)
    flux[4] = flux[4] + (p_low * u_low + p_high * u_high)
    return flux


def dg_table():
    lifted = DERIV.copy()
    lifted[0, 0] += 1.0 / WEIGHTS[0]
    lifted[3, 3] -= 1.0 / WEIGHTS[3]
    return np.cumsum(2.0 * WEIGHTS[:, None] * lifted, axis=0)


SUBCELL = dg_table()


def dg_fluxes(values):
    outer, inner = values[0] + values[3], values[1] + values[2]
    step = inner - outer
    even = outer + float(0.5 * (SUBCELL[0, 1] + SUBCELL[2, 1])) * step
    middle = outer + float(SUBCELL[1, 1]) * step
    odd = float(0.5 * (SUBCELL[0, 0] - SUBCELL[2, 0])) * (values[0] - values[3])
    odd = odd + float(0.5 * (SUBCELL[0, 1] - SUBCELL[2, 1])) * (values[1] - values[2])
    return even + odd, middle, even - odd


def wave_weights(u_low, c_low, u_high, c_high, speed):
    rel_low = u_low - speed
    rel_high = u_high - speed
    fastest = jnp.maximum(jnp.abs(rel_low) + c_low, jnp.abs(rel_high) + c_high)
    return rel_low + fastest, rel_high - fastest


def kernel(
    tile_x,
    tile_y,
    sizes,
    cons_hbm,
    list_hbm,
    wx_hbm,
    wy_hbm,
    wz_hbm,
    sx_hbm,
    sy_hbm,
    sz_hbm,
    out,
    hess_ref,
    list_ref,
    wx_ref,
    wy_ref,
    wz_ref,
    sx_ref,
    sy_ref,
    sz_ref,
    state,
    inv_s,
    pres_s,
    sound_s,
    zl,
    zst,
    ph,
    geo,
    cs,
    cr,
    lxs,
    lxr,
    lys,
    lyr,
    xs,
    xr,
    ys,
    yr,
    rxs,
    rxr,
    rys,
    ryr,
    rds,
    rdr,
    io_sem,
    send_sem,
    recv_sem,
):
    size_x, size_y = sizes
    rows = tile_x * tile_y
    lanes = state.shape[-1]
    me_x, me_y = lax.axis_index("gx"), lax.axis_index("gy")
    up_x, down_x = lax.rem(me_x + 1, size_x), lax.rem(me_x + size_x - 1, size_x)
    up_y, down_y = lax.rem(me_y + 1, size_y), lax.rem(me_y + size_y - 1, size_y)

    barrier = pltpu.get_barrier_semaphore()
    partners = ((me_x, down_y), (me_x, up_y), (down_x, me_y), (up_x, me_y), (down_x, down_y))
    for partner in partners:
        pl.semaphore_signal(barrier, inc=1, device_id=partner, device_id_type=MESH)
    small = [
        pltpu.make_async_copy(src, dst, io_sem.at[4 + n])
        for n, (src, dst) in enumerate(
            (
                (wx_hbm, wx_ref),
                (wy_hbm, wy_ref),
                (sx_hbm, sx_ref),
                (sy_hbm, sy_ref),
                (wz_hbm, wz_ref),
                (sz_hbm, sz_ref),
                (list_hbm, list_ref),
            )
        )
    ]
    loads = [pltpu.make_async_copy(cons_hbm.at[:, a], state.at[:, a], io_sem.at[a]) for a in range(4)]
    for a in (0, 3, 1, 2):
        loads[a].start()
    for copy in small:
        copy.start()

    shape = (rows, lanes)
    row = lax.broadcasted_iota(jnp.int32, shape, 0)
    row_i, row_j = row // tile_y, row % tile_y

    def roll_rows(value, shift):
        shift = shift % rows
        return value if shift == 0 else pltpu.roll(value, shift, 0)

    def roll_lanes(value, shift):
        return pltpu.roll(value, shift % lanes, 1)

    def pack_x(q, carry):
        for v in range(5):
            for side, node, first in ((0, 0, 0), (1, 3, rows - tile_y)):
                packed = None
                for c in range(4):
                    part = roll_rows(state[v, node, q, c], tile_y * c - first)
                    packed = part if packed is None else jnp.where(row_i == c, part, packed)
                xs[side, v, q] = packed
        return carry

    def pack_y(q, carry):
        for v in range(5):
            for side, node, first in ((0, 0, 0), (1, 3, tile_y - 1)):
                for group in range(4 // tile_y):
                    packed = None
                    for c in range(tile_y):
                        part = roll_rows(state[v, q, node, group * tile_y + c], c - first)
                        packed = part if packed is None else jnp.where(row_j == c, part, packed)
                    ys[side, v, q, group] = packed
        return carry

    last_i, last_j = tile_x - 1, tile_y - 1
    early = ((0, 0, last_j), (0, 1, rows - 1), (1, 0, rows - tile_y), (1, 1, rows - 1))

    def early_node(d, group, sub):
        if d == 0:
            return group * tile_y + sub % tile_y, sub // tile_y
        return (group * rows + sub) // 4, sub % 4

    def pack_early(v, carry):
        for slot, (d, side, place) in enumerate(early):
            for group in range(16 // rows):
                packed = None
                for sub in range(rows):
                    q, c = early_node(d, group, sub)
                    value = state[v, 3 * side, q, c] if d == 0 else state[v, q, 3 * side, c]
                    part = roll_rows(value, sub - place)
                    packed = part if packed is None else jnp.where(row == sub, part, packed)
                cs[slot, v, group] = packed
        return carry

    def remote(src, dst, slot, device):
        return pltpu.make_async_remote_copy(
            src_ref=src,
            dst_ref=dst,
            send_sem=send_sem.at[slot],
            recv_sem=recv_sem.at[slot],
            device_id=device,
            device_id_type=MESH,
        )

    for copy in small:
        copy.wait()

    def along(ref, start, total, tile, index):
        values = [ref[lax.rem(start + total + i, total)] for i in range(-1, tile + 1)]

        def pick(offset):
            vector = jnp.full(shape, values[1 + offset], jnp.float32)
            for i in range(1, tile):
                vector = jnp.where(index == i, values[1 + offset + i], vector)
            return vector

        return values, pick(-1), pick(0), pick(1)

    total_x, total_y = size_x * tile_x, size_y * tile_y
    wx_all, wx_p, wx, _ = along(wx_ref, me_x * tile_x, total_x, tile_x, row_i)
    wy_all, wy_p, wy, _ = along(wy_ref, me_y * tile_y, total_y, tile_y, row_j)
    sx_all, sx_p, sx, sx_n = along(sx_ref, me_x * tile_x, total_x, tile_x, row_i)
    sy_all, sy_p, sy, sy_n = along(sy_ref, me_y * tile_y, total_y, tile_y, row_j)
    nx_all = [wx_all[i] + time_step * (sx_all[i + 1] - sx_all[i]) for i in range(tile_x + 1)]
    ny_all = [wy_all[i] + time_step * (sy_all[i + 1] - sy_all[i]) for i in range(tile_y + 1)]
    wz = jnp.broadcast_to(wz_ref[...], shape)
    sz = jnp.broadcast_to(sz_ref[...], shape)
    sz_n = roll_lanes(sz, -1)
    nx, ny, nz = (
        wx + time_step * (sx_n - sx),
        wy + time_step * (sy_n - sy),
        wz + time_step * (sz_n - sz),
    )
    px, py = wx_p + time_step * (sx - sx_p), wy_p + time_step * (sy - sy_p)
    pz = roll_lanes(nz, 1)
    mass = nx * ny * nz
    ratio = wx * wy * wz / mass
    geo[RATIO] = ratio
    for d, (width, low, high) in enumerate(((wx, sx, sx_n), (wy, sy, sy_n), (wz, sz, sz_n))):
        for a in range(4):
            geo[SPEED + 4 * d + a] = low * float((1.0 - NODES[a]) / 2.0) + high * float(
                (1.0 + NODES[a]) / 2.0
            )
        for q, xi in enumerate((-5.0 / 6.0, 0.0, 5.0 / 6.0)):
            geo[INTER + 3 * d + q] = low * ((1.0 - xi) / 2.0) + high * ((1.0 + xi) / 2.0)
        geo[FACE + 2 * d] = low
        geo[FACE + 2 * d + 1] = high
        kappa = -time_step * ratio / width
        geo[SCALE + 2 * d] = kappa * float(1.0 / WEIGHTS[0])
        geo[SCALE + 2 * d + 1] = kappa * float(1.0 / WEIGHTS[1])

    entries = list_ref[...]
    count = entries.shape[-1]
    in_row = jnp.where(
        lax.broadcasted_iota(jnp.int32, (rows, count), 0) == entries // lanes, 1.0, 0.0
    )
    in_lane = jnp.where(
        lax.broadcasted_iota(jnp.int32, (lanes, count), 0) == entries % lanes, 1.0, 0.0
    )
    geo[MASK] = lax.dot_general(
        in_row, in_lane, (((1,), (1,)), ((), ())), preferred_element_type=jnp.float32
    )

    def prepare(a, carry):
        for b in range(4):
            for c in range(4):
                inverse, pressure, sound = primitives([state[v, a, b, c] for v in range(5)])
                inv_s[a, b, c] = inverse
                pres_s[a, b, c] = pressure
                sound_s[a, b, c] = sound
            zl[0, a, b] = roll_lanes(state[0, a, b, 3], 1)
            zl[3, a, b] = roll_lanes(state[3, a, b, 3] * inverse, 1)
            zl[5, a, b] = roll_lanes(sound, 1)
        return carry


    def interior(d, parts, index, carry):
        first, second = index // 4, index % 4

        def at(n):
            return ((n, first, second), (first, n, second), (first, second, n))[d]

        mask = geo[MASK] > 0.5
        sound = [sound_s[at(n)] for n in range(4)]
        normal = [state[(d + 1,) + at(n)] * inv_s[at(n)] for n in range(4)]
        weights = [
            wave_weights(normal[q], sound[q], normal[q + 1], sound[q + 1], geo[INTER + 3 * d + q])
            for q in range(3)
        ]
        relative = [normal[n] - geo[SPEED + 4 * d + n] for n in range(4)]
        if parts != DENSITY:
            pressure = [pres_s[at(n)] for n in range(4)]
            work = [pressure[n] * normal[n] for n in range(4)]
        if d == 2:
            behind = zl[3, first, second]
            star_left, star_right = wave_weights(
                behind, zl[5, first, second], normal[0], sound[0], geo[FACE + 4]
            )
            if parts != DENSITY:
                push = zl[6, first, second]
        for v in parts:
            value = [state[(v,) + at(n)] for n in range(4)]
            flux = [value[n] * relative[n] for n in range(4)]
            inner = [value[q] * weights[q][0] + value[q + 1] * weights[q][1] for q in range(3)]
            if d == 2:
                if v == 3:
                    rolled = zl[7, first, second]
                else:
                    rolled = zl[v, first, second]
                star = rolled * star_left + value[0] * star_right
            extra = pressure if v == d + 1 else work if v == 4 else None
            if extra is not None:
                flux = [flux[n] + extra[n] for n in range(4)]
                inner = [inner[q] + (extra[q] + extra[q + 1]) for q in range(3)]
            if d == 2:
                if v == 3:
                    star = star + (push + pressure[0])
                if v == 4:
                    star = star + (push * behind + work[0])
                zst[v, first, second] = star
            smooth = dg_fluxes(flux)
            chosen = [jnp.where(mask, inner[q], smooth[q]) for q in range(3)]
            head = chosen[0] - star if d == 2 else chosen[0]
            change = [head, chosen[1] - chosen[0], chosen[2] - chosen[1], -chosen[2]]
            for n in range(4):
                where = (v,) + at(n)
                scale = geo[SCALE + 2 * d + (0 if n in (0, 3) else 1)]
                if d == 0:
                    base = geo[RATIO] * value[n]
                else:
                    base = out[where]
                out[where] = base + scale * change[n]
        return carry

    def above(v, a):
        for b in range(4):
            out[v, a, b, 3] = out[v, a, b, 3] + geo[SCALE + 4] * roll_lanes(zst[v, a, b], -1)


    def spots(d, q, c):
        return ((0, q, c), (3, q, c)) if d == 0 else ((q, 0, c), (q, 3, c))

    def inside(d, q, carry):
        shift = (tile_y, 1)[d]
        edge = (row_i, row_j)[d]
        for c in range(4):
            low, high = spots(d, q, c)
            left, right = wave_weights(
                roll_rows(state[(d + 1,) + high] * inv_s[high], shift),
                roll_rows(sound_s[high], shift),
                state[(d + 1,) + low] * inv_s[low],
                sound_s[low],
                geo[FACE + 2 * d],
            )
            star = roll_rows(state[(0,) + high], shift) * left + state[(0,) + low] * right
            star = jnp.where(edge > 0, star, 0.0)
            scale = geo[SCALE + 2 * d]
            out[(0,) + low] = out[(0,) + low] - scale * star
            out[(0,) + high] = out[(0,) + high] + scale * roll_rows(star, -shift)
        return carry


    def first_density():
        lax.fori_loop(0, 4, prepare, 0)
        for d in range(3):
            lax.fori_loop(0, 16, functools.partial(interior, d, DENSITY), 0)
        for a in range(4):
            above(0, a)
        for d in range(2):
            lax.fori_loop(0, 4, functools.partial(inside, d), 0)

    ring_end = jnp.logical_or(me_x == size_x - 1, me_y == size_y - 1)
    for a in (0, 3, 1, 2):
        loads[a].wait()
    lax.fori_loop(0, 5, pack_early, 0)
    pl.when(jnp.logical_not(ring_end))(first_density)
    pl.semaphore_wait(barrier, len(partners))
    heralds = [
        remote(cs.at[2], cr.at[3], 9, (me_x, down_y)),
        remote(cs.at[3], cr.at[2], 10, (me_x, up_y)),
        remote(cs.at[0], cr.at[1], 7, (down_x, me_y)),
        remote(cs.at[1], cr.at[0], 8, (up_x, me_y)),
    ]
    for copy in heralds:
        copy.start()
    faces = [
        remote(lys.at[0], lyr.at[1], 2, (me_x, down_y)),
        remote(lys.at[1], lyr.at[0], 3, (me_x, up_y)),
        remote(lxs.at[0], lxr.at[1], 0, (down_x, me_y)),
        remote(lxs.at[1], lxr.at[0], 1, (up_x, me_y)),
    ]
    halves = 4 // tile_y
    groups = 4 * halves
    kept = groups - groups // tile_x
    free_y, free_x = row_i == last_i, row_j == last_j

    def group_of(ref, side, v, k):
        return ref[side, v, k // halves, k % halves]

    def squeeze_y(v, carry):
        for side in range(2):
            for k in range(kept):
                source, piece = kept + k // last_i, k % last_i
                moved = roll_rows(group_of(ys, side, v, source), rows - tile_y - piece * tile_y)
                lys[side, v, k] = jnp.where(free_y, moved, group_of(ys, side, v, k))
        return carry

    def squeeze_x(v, carry):
        for side in range(2):
            for k in range(4 // tile_y):
                moved = roll_rows(xs[side, v, tile_y * k + 1], last_j)
                lxs[side, v, k] = jnp.where(free_x, moved, xs[side, v, tile_y * k])
        return carry

    lax.fori_loop(0, 4, pack_y, 0)
    lax.fori_loop(0, 5, squeeze_y, 0)
    faces[0].start()
    faces[1].start()
    lax.fori_loop(0, 4, pack_x, 0)
    lax.fori_loop(0, 5, squeeze_x, 0)
    faces[2].start()
    faces[3].start()

    pl.when(ring_end)(first_density)

    second = DERIV @ DERIV
    ends = (0, 3)

    def combine(coefficients, values):
        total = None
        for n in range(4):
            if values[n] is not None:
                term = float(coefficients[n]) * values[n]
                total = term if total is None else total + term
        return total

    def columns(density, factors, wanted):
        along_x = {
            (p, b, c): combine(DERIV[p], [density[a][b][c] for a in range(4)])
            for p in ends
            for b in range(4)
            for c in range(4)
            if b in ends or c in ends
        }
        along_y = {
            (a, q, c): combine(DERIV[q], [density[a][b][c] for b in range(4)])
            for q in ends
            for a in ends
            for c in range(4)
        }

        def corner(kind, p, q, r):
            if kind == 0:
                return combine(second[p], [density[a][q][r] for a in range(4)])
            if kind == 1:
                return combine(second[q], [density[p][b][r] for b in range(4)])
            if kind == 2:
                return combine(second[r], [density[p][q][c] for c in range(4)])
            if kind == 3:
                return combine(DERIV[q], [along_x[p, b, r] for b in range(4)])
            if kind == 4:
                return combine(DERIV[r], [along_x[p, q, c] for c in range(4)])
            return combine(DERIV[r], [along_y[p, q, c] for c in range(4)])

        found = []
        for kind in range(6):
            column = {}
            for p, q in wanted:
                low, high = corner(kind, p, q, 0), corner(kind, p, q, 3)
                column[p, q] = factors[kind] * low + roll_lanes(factors[kind] * high, 1)
            found.append(column)
        return found

    def pairs(jx, jy, jz):
        return (jx * jx, jy * jy, jz * jz, jx * jy, jx * jz, jy * jz)

    ix, iy, iz = 2.0 / nx, 2.0 / ny, 2.0 / nz
    factors = [mass * pair for pair in pairs(ix, iy, iz)]

    def up_y_shift(value):
        return jnp.where(row_j == 0, 0.0, roll_rows(value, 1))

    def up_x_shift(value):
        return jnp.where(row_i == 0, 0.0, roll_rows(value, tile_y))

    def column_rims(found, spread):
        x_rim = [None] * -(-6 // tile_x)
        y_rim = [None] * -(-6 // tile_y)
        d_rim = None
        for kind, column in enumerate(found):
            high_x, rim, far = spread(column)
            slot, place = kind // tile_x, kind % tile_x
            part = roll_rows(high_x, tile_y * place - (rows - tile_y))
            x_rim[slot] = part if place == 0 else jnp.where(row_i == place, part, x_rim[slot])
            slot, place = kind // tile_y, kind % tile_y
            part = roll_rows(rim, place - (tile_y - 1))
            y_rim[slot] = part if place == 0 else jnp.where(row_j == place, part, y_rim[slot])
            if far is not None:
                part = roll_rows(far, kind - (rows - 1))
                d_rim = part if kind == 0 else jnp.where(row == kind, part, d_rim)
        return x_rim, y_rim, d_rim

    def whole_rims(column):
        high_x = column[3, 0] + up_y_shift(column[3, 3])
        return high_x, column[0, 3] + up_x_shift(column[3, 3]), column[3, 3]

    three = ((0, 3), (3, 0), (3, 3))
    density = [[[out[0, a, b, c] for c in range(4)] for b in range(4)] for a in range(4)]
    x_rim, y_rim, d_rim = column_rims(columns(density, factors, three), whole_rims)
    for slot, value in enumerate(x_rim):
        rxs[slot] = value
    for slot, value in enumerate(y_rim):
        rys[slot] = value
    rds[...] = d_rim
    rims = [
        remote(rds, rdr, 6, (up_x, up_y)),
        remote(rys, ryr, 5, (me_x, up_y)),
        remote(rxs, rxr, 4, (up_x, me_y)),
    ]
    rims[0].start()

    def behind_rest(a, carry):
        for b in range(4):
            zl[1, a, b] = roll_lanes(state[1, a, b, 3], 1)
            zl[2, a, b] = roll_lanes(state[2, a, b, 3], 1)
            zl[7, a, b] = roll_lanes(state[3, a, b, 3], 1)
            zl[4, a, b] = roll_lanes(state[4, a, b, 3], 1)
            zl[6, a, b] = roll_lanes(pres_s[a, b, 3], 1)
        return carry

    def above_rest(a, carry):
        for v in REST:
            above(v, a)
        return carry

    def rest():
        lax.fori_loop(0, 4, behind_rest, 0)
        for d in range(3):
            lax.fori_loop(0, 16, functools.partial(interior, d, REST), 0)
        lax.fori_loop(0, 4, above_rest, 0)

    pl.when(jnp.logical_not(ring_end))(rest)

    row_up_x, row_low_x, row_under_x = 3, last_j, last_j - 1
    row_up_y, row_low_y, row_under_y = rows - 1, rows - tile_y, rows - tile_y - 1
    is_x = row <= row_up_x
    lower = jnp.logical_or(row == row_low_x, row == row_low_y)
    part_x = jnp.where(row == row_under_x, nx_all[0], jnp.where(row == row_low_x, nx_all[1], nx_all[tile_x]))
    part_y = jnp.where(row == row_under_y, ny_all[0], jnp.where(row == row_low_y, ny_all[1], ny_all[tile_y]))
    across = jnp.where(is_x, wy_all[tile_y], wx_all[tile_x])
    part = jnp.where(lower, 1.0, -1.0) * across * wz * float(time_step / WEIGHTS[3])
    part_factors = [part * pair for pair in pairs(2.0 / part_x, 2.0 / part_y, iz)]

    for copy in heralds:
        copy.wait()
    stars = []
    for slot, (d, side, place) in enumerate(early):
        stars.append([])
        for group in range(16 // rows):
            own = [cs[slot, v, group] for v in range(5)]
            other = [cr[slot, v, group] for v in range(5)]
            low, high = (other, own) if side == 0 else (own, other)
            low_inverse, _, low_sound = primitives(low)
            high_inverse, _, high_sound = primitives(high)
            left, right = wave_weights(
                low[d + 1] * low_inverse,
                low_sound,
                high[d + 1] * high_inverse,
                high_sound,
                geo[FACE + 2 * d + side, place : place + 1],
            )
            stars[slot].append(low[0] * left + high[0] * right)
    field = [[[None] * 4 for b in range(4)] for a in range(4)]

    def put(a, b, c, value):
        old = field[a][b][c]
        field[a][b][c] = value if old is None else old + value

    for group in range(16 // rows):
        for sub in range(rows):
            q, c = early_node(0, group, sub)
            under = roll_rows(stars[0][group], row_under_x - sub)
            upper = roll_rows(stars[1][group], row_up_x - sub)
            value = jnp.where(row == row_up_x, upper, 0.0)
            put(3, q, c, jnp.where(row == row_under_x, under, value))
            low = roll_rows(stars[0][group], row_low_x - sub)
            put(0, q, c, jnp.where(row == row_low_x, low, 0.0))
            q, c = early_node(1, group, sub)
            under = roll_rows(stars[2][group], row_under_y - sub)
            upper = roll_rows(stars[3][group], row_up_y - sub)
            value = jnp.where(row == row_up_y, upper, 0.0)
            put(q, 3, c, jnp.where(row == row_under_y, under, value))
            low = roll_rows(stars[2][group], row_low_y - sub)
            put(q, 0, c, jnp.where(row == row_low_y, low, 0.0))

    def part_rims(column):
        high_x = column[3, 0] + roll_rows(column[3, 3], 1)
        near = jnp.where(row == last_j, column[0, 3] + roll_rows(column[3, 3], 1), 0.0)
        near = jnp.where(row == last_j + tile_y, roll_rows(column[3, 3], tile_y), near)
        return high_x, jnp.where(row == rows - 1, roll_rows(column[0, 3], rows - 1 - row_up_x), near), None

    x_rim, y_rim, _ = column_rims(columns(field, part_factors, three), part_rims)
    for slot, value in enumerate(y_rim):
        rys[slot] = rys[slot] + value
    rims[1].start()
    for slot, value in enumerate(x_rim):
        rxs[slot] = rxs[slot] + value
    rims[2].start()
    pl.when(ring_end)(rest)

    def surface(d, q, carry):
        shift = (tile_y, 1)[d]
        edge, last = ((row_i, last_i), (row_j, last_j))[d]
        speed = geo[FACE + 2 * d]
        top_speed = geo[FACE + 2 * d + 1, rows - 1 : rows]
        scale = geo[SCALE + 2 * d]
        tops = []
        for group in range(1 if d == 0 else 4 // tile_y):
            if d == 0:
                own = [xs[1, v, q] for v in range(5)]
                other = [xr[1, v, q] for v in range(5)]
            else:
                own = [ys[1, v, q, group] for v in range(5)]
                other = [yr[1, v, q, group] for v in range(5)]
            own_inverse, own_pressure, own_sound = primitives(own)
            inverse, pressure, sound = primitives(other)
            tops.append(
                twice_flux(
                    own,
                    own_pressure,
                    own_sound,
                    own[d + 1] * own_inverse,
                    other,
                    pressure,
                    sound,
                    other[d + 1] * inverse,
                    d,
                    top_speed,
                )
            )
        for c in range(4):
            low, high = spots(d, q, c)
            own = [state[(v,) + low] for v in range(5)]
            other = []
            for v in range(5):
                if d == 0:
                    halo = roll_rows(xr[0, v, q], -tile_y * c)
                else:
                    halo = roll_rows(yr[0, v, q, c // tile_y], -(c % tile_y))
                moved = roll_rows(state[(v,) + high], shift)
                other.append(jnp.where(edge == 0, halo, moved))
            inverse, pressure, sound = primitives(other)
            star = twice_flux(
                other,
                pressure,
                sound,
                other[d + 1] * inverse,
                own,
                pres_s[low],
                sound_s[low],
                own[d + 1] * inv_s[low],
                d,
                speed,
            )
            for v in range(5):
                if d == 0:
                    top = roll_rows(tops[0][v], rows - tile_y - tile_y * c)
                else:
                    top = roll_rows(tops[c // tile_y][v], tile_y - 1 - c % tile_y)
                if v == 0:
                    down = jnp.where(edge == 0, star[v], 0.0)
                    up = jnp.where(edge == last, top, 0.0)
                    ph[d, q, c] = down
                else:
                    down = star[v]
                    up = jnp.where(edge == last, top, roll_rows(star[v], -shift))
                out[(v,) + low] = out[(v,) + low] - scale * down
                out[(v,) + high] = out[(v,) + high] + scale * up
        return carry

    def spread_x(v, carry):
        for side in range(2):
            for q in range(4):
                k = q // tile_y
                late, first = lxr[side, v, k], cr[side, v, k]
                if q % tile_y == 0:
                    first = roll_rows(first, last_j)
                else:
                    late = roll_rows(late, -last_j)
                xr[side, v, q] = jnp.where(free_x, first, late)
        return carry

    def spread_y(v, carry):
        for side in range(2):
            for k in range(groups):
                if k < kept:
                    value = lyr[side, v, k]
                else:
                    value = None
                    for piece in range(last_i):
                        part = lyr[side, v, (k - kept) * last_i + piece]
                        part = roll_rows(part, piece * tile_y - (rows - tile_y))
                        value = part if value is None else jnp.where(row_i == piece, part, value)
                first = cr[2 + side, v, k // tile_x]
                first = roll_rows(first, rows - tile_y - (k % tile_x) * tile_y)
                yr[side, v, k // halves, k % halves] = jnp.where(free_y, first, value)
        return carry

    faces[2].wait()
    faces[3].wait()
    lax.fori_loop(0, 5, spread_x, 0)
    lax.fori_loop(0, 4, functools.partial(surface, 0), 0)
    faces[0].wait()
    faces[1].wait()
    lax.fori_loop(0, 5, spread_y, 0)
    lax.fori_loop(0, 4, functools.partial(surface, 1), 0)

    density = [[[out[0, a, b, c] for c in range(4)] for b in range(4)] for a in range(4)]
    for kind, column in enumerate(columns(density, factors, ((0, 0), (0, 3), (3, 0), (3, 3)))):
        low_x = column[0, 0] + up_y_shift(column[0, 3])
        high_x = column[3, 0] + up_y_shift(column[3, 3])
        hess_ref[kind] = low_x + up_x_shift(high_x)

    bottom = row_j == 0
    side_y, side_w = jnp.full(shape, ny_all[1], jnp.float32), jnp.full(shape, wy_all[1], jnp.float32)
    for n in range(1, tile_y):
        side_y = jnp.where(row_i == n, ny_all[1 + n], side_y)
        side_w = jnp.where(row_i == n, wy_all[1 + n], side_w)
    ghost_x = jnp.where(bottom, nx, nx_all[0])
    ghost_y = jnp.where(bottom, py, side_y)
    ghost = jnp.where(bottom, wx, side_w) * wz * float(-time_step / WEIGHTS[3])
    ghost_factors = [ghost * pair for pair in pairs(2.0 / ghost_x, 2.0 / ghost_y, iz)]
    field = [[[None] * 4 for b in range(4)] for a in range(4)]
    for n in range(4):
        for c in range(4):
            from_x = jnp.zeros(shape, jnp.float32)
            for m in range(tile_y):
                place = m * tile_y + last_j
                from_x = jnp.where(row == place, roll_rows(ph[0, n, c], place - m), from_x)
            put(3, n, c, from_x)
            put(n, 3, c, ph[1, n, c])
    for kind, column in enumerate(columns(field, ghost_factors, three)):
        total = hess_ref[kind] + jnp.where(bottom, column[0, 3], 0.0)
        total = total + jnp.where(bottom, up_x_shift(column[3, 3]), 0.0)
        for m in range(tile_y):
            place = m * tile_y + last_j
            total = total + jnp.where(row == m, roll_rows(column[3, 0], m - place), 0.0)
            if m < last_j:
                total = total + jnp.where(row == m + 1, roll_rows(column[3, 3], m + 1 - place), 0.0)
        hess_ref[kind] = total

    inverse = 1.0 / ((nx + px) * (ny + py) * (nz + pz))
    for copy in rims:
        copy.wait()
    for kind in range(6):
        total = hess_ref[kind]
        from_x = roll_rows(rxr[kind // tile_x], -tile_y * (kind % tile_x))
        total = total + jnp.where(row_i == 0, from_x, 0.0)
        from_y = roll_rows(ryr[kind // tile_y], -(kind % tile_y))
        total = total + jnp.where(row_j == 0, from_y, 0.0)
        total = total + jnp.where(row == 0, roll_rows(rdr[...], -kind), 0.0)
        hess_ref[kind] = total * inverse


def emit(adv_ref, hess_ref, adv_out, hess_out, sem):
    copies = [
        pltpu.make_async_copy(adv_ref, adv_out, sem.at[0]),
        pltpu.make_async_copy(hess_ref, hess_out, sem.at[1]),
    ]
    for copy in copies:
        copy.start()
    for copy in copies:
        copy.wait()


def solution(mesh):
    sizes = (mesh.shape["gx"], mesh.shape["gy"])

    def local(conserved, troubled_list, widths_x, widths_y, widths_z, speed_x, speed_y, speed_z):
        tile_x, tile_y, column = conserved.shape[4:]
        rows = tile_x * tile_y
        f32 = jnp.float32
        vmem = pl.BlockSpec(memory_space=pltpu.VMEM)
        whole = pl.BlockSpec(memory_space=pl.ANY)
        full = (5, 4, 4, 4, rows, column)
        nodal = (4, 4, 4, rows, column)
        x_face = (2, 5, 4, rows, column)
        y_face = (2, 5, 4, 4 // tile_y, rows, column)
        groups = 4 * (4 // tile_y)
        x_late = (2, 5, 4 // tile_y, rows, column)
        y_late = (2, 5, groups - groups // tile_x, rows, column)
        herald = (4, 5, 16 // rows, rows, column)
        x_rim = (-(-6 // tile_x), rows, column)
        y_rim = (-(-6 // tile_y), rows, column)
        advanced, hessian = pl.pallas_call(
            functools.partial(kernel, tile_x, tile_y, sizes),
            out_shape=(
                pltpu.VMEM(full, f32),
                pltpu.VMEM((6, rows, column), f32),
            ),
            in_specs=[whole] * 8,
            out_specs=(vmem, vmem),
            scratch_shapes=[
                pltpu.VMEM((1, troubled_list.shape[0]), jnp.int32),
                pltpu.SMEM(widths_x.shape, f32),
                pltpu.SMEM(widths_y.shape, f32),
                pltpu.VMEM((1, column), f32),
                pltpu.SMEM(speed_x.shape, f32),
                pltpu.SMEM(speed_y.shape, f32),
                pltpu.VMEM((1, column), f32),
                pltpu.VMEM(full, f32),
                pltpu.VMEM(nodal, f32),
                pltpu.VMEM(nodal, f32),
                pltpu.VMEM(nodal, f32),
                pltpu.VMEM((8, 4, 4, rows, column), f32),
                pltpu.VMEM((5, 4, 4, rows, column), f32),
                pltpu.VMEM((2, 4, 4, rows, column), f32),
                pltpu.VMEM((GEO, rows, column), f32),
                pltpu.VMEM(herald, f32),
                pltpu.VMEM(herald, f32),
                pltpu.VMEM(x_late, f32),
                pltpu.VMEM(x_late, f32),
                pltpu.VMEM(y_late, f32),
                pltpu.VMEM(y_late, f32),
                pltpu.VMEM(x_face, f32),
                pltpu.VMEM(x_face, f32),
                pltpu.VMEM(y_face, f32),
                pltpu.VMEM(y_face, f32),
                pltpu.VMEM(x_rim, f32),
                pltpu.VMEM(x_rim, f32),
                pltpu.VMEM(y_rim, f32),
                pltpu.VMEM(y_rim, f32),
                pltpu.VMEM((rows, column), f32),
                pltpu.VMEM((rows, column), f32),
                pltpu.SemaphoreType.DMA((11,)),
                pltpu.SemaphoreType.DMA((11,)),
                pltpu.SemaphoreType.DMA((11,)),
            ],
            compiler_params=pltpu.CompilerParams(collective_id=0, has_side_effects=True),
        )(
            conserved.reshape(full),
            troubled_list.reshape(1, -1),
            widths_x,
            widths_y,
            widths_z.reshape(1, -1),
            speed_x,
            speed_y,
            speed_z.reshape(1, -1),
        )
        advanced = pltpu.with_memory_space_constraint(advanced, pltpu.VMEM)
        hessian = pltpu.with_memory_space_constraint(hessian, pltpu.VMEM)
        advanced, hessian = pl.pallas_call(
            emit,
            out_shape=(
                jax.ShapeDtypeStruct(full, f32),
                jax.ShapeDtypeStruct((6, rows, column), f32),
            ),
            in_specs=[whole, whole],
            out_specs=(whole, whole),
            scratch_shapes=[pltpu.SemaphoreType.DMA((2,))],
        )(advanced, hessian)
        return advanced.reshape(conserved.shape), hessian.reshape(6, tile_x, tile_y, column)

    in_specs = (
        P(None, None, None, None, "gx", "gy", None),
        P(("gx", "gy")),
        P(),
        P(),
        P(),
        P(),
        P(),
        P(),
    )
    out_specs = (P(None, None, None, None, "gx", "gy", None), P(None, "gx", "gy", None))
    return jax.shard_map(local, mesh=mesh, in_specs=in_specs, out_specs=out_specs, check_vma=False)
```

```python
import functools

import jax
import jax.numpy as jnp
import numpy as np
from jax import lax
from jax.experimental import pallas as pl
from jax.experimental.pallas import tpu as pltpu
from jax.sharding import PartitionSpec as P

MESH = pl.DeviceIdType.MESH
time_step = 0.05
gamma_ratio = 1.4


def lgl_tables():
    nodes = np.array([-1.0, -1.0 / np.sqrt(5.0), 1.0 / np.sqrt(5.0), 1.0])
    weights = np.array([1.0 / 6.0, 5.0 / 6.0, 5.0 / 6.0, 1.0 / 6.0])
    barycentric = np.ones(4)
    for row_a in range(4):
        for row_b in range(4):
            if row_a != row_b:
                barycentric[row_a] = barycentric[row_a] / (nodes[row_a] - nodes[row_b])
    deriv = np.zeros((4, 4))
    for row_a in range(4):
        for row_b in range(4):
            if row_a != row_b:
                deriv[row_a, row_b] = (
                    barycentric[row_b] / barycentric[row_a] / (nodes[row_a] - nodes[row_b])
                )
    for row_a in range(4):
        deriv[row_a, row_a] = -np.sum(deriv[row_a])
    return (nodes, weights, deriv)


NODES, WEIGHTS, DERIV = lgl_tables()
SPEED, INTER, SCALE, FACE = 0, 12, 21, 27
RATIO, MASK, GEO = 33, 34, 35
ALL, DENSITY, REST = (0, 1, 2, 3, 4), (0,), (1, 2, 3, 4)


def primitives(state):
    inverse = 1.0 / state[0]
    square = state[1] * state[1] + state[2] * state[2] + state[3] * state[3]
    pressure = (gamma_ratio - 1.0) * (state[4] - 0.5 * square * inverse)
    ratio = gamma_ratio * pressure * inverse
    return inverse, pressure, ratio * lax.rsqrt(ratio)


def twice_flux(low, p_low, c_low, u_low, high, p_high, c_high, u_high, direction, speed):
    rel_low = u_low - speed
    rel_high = u_high - speed
    fastest = jnp.maximum(jnp.abs(rel_low) + c_low, jnp.abs(rel_high) + c_high)
    left = rel_low + fastest
    right = rel_high - fastest
    flux = [low[v] * left + high[v] * right for v in range(5)]
    flux[direction + 1] = flux[direction + 1] + (p_low + p_high)
    flux[4] = flux[4] + (p_low * u_low + p_high * u_high)
    return flux


def dg_table():
    lifted = DERIV.copy()
    lifted[0, 0] += 1.0 / WEIGHTS[0]
    lifted[3, 3] -= 1.0 / WEIGHTS[3]
    return np.cumsum(2.0 * WEIGHTS[:, None] * lifted, axis=0)


SUBCELL = dg_table()


def dg_fluxes(values):
    outer, inner = values[0] + values[3], values[1] + values[2]
    step = inner - outer
    even = outer + float(0.5 * (SUBCELL[0, 1] + SUBCELL[2, 1])) * step
    middle = outer + float(SUBCELL[1, 1]) * step
    odd = float(0.5 * (SUBCELL[0, 0] - SUBCELL[2, 0])) * (values[0] - values[3])
    odd = odd + float(0.5 * (SUBCELL[0, 1] - SUBCELL[2, 1])) * (values[1] - values[2])
    return even + odd, middle, even - odd


def wave_weights(u_low, c_low, u_high, c_high, speed):
    rel_low = u_low - speed
    rel_high = u_high - speed
    fastest = jnp.maximum(jnp.abs(rel_low) + c_low, jnp.abs(rel_high) + c_high)
    return rel_low + fastest, rel_high - fastest


def kernel(
    tile_x,
    tile_y,
    sizes,
    cons_hbm,
    list_hbm,
    wx_hbm,
    wy_hbm,
    wz_hbm,
    sx_hbm,
    sy_hbm,
    sz_hbm,
    out,
    hess_ref,
    list_ref,
    wx_ref,
    wy_ref,
    wz_ref,
    sx_ref,
    sy_ref,
    sz_ref,
    state,
    inv_s,
    pres_s,
    sound_s,
    zl,
    zst,
    ph,
    geo,
    cs,
    cr,
    lxs,
    lxr,
    lys,
    lyr,
    xs,
    xr,
    ys,
    yr,
    rxs,
    rxr,
    rys,
    ryr,
    rds,
    rdr,
    io_sem,
    send_sem,
    recv_sem,
):
    size_x, size_y = sizes
    rows = tile_x * tile_y
    lanes = state.shape[-1]
    me_x, me_y = lax.axis_index("gx"), lax.axis_index("gy")
    up_x, down_x = lax.rem(me_x + 1, size_x), lax.rem(me_x + size_x - 1, size_x)
    up_y, down_y = lax.rem(me_y + 1, size_y), lax.rem(me_y + size_y - 1, size_y)

    barrier = pltpu.get_barrier_semaphore()
    partners = ((me_x, down_y), (me_x, up_y), (down_x, me_y), (up_x, me_y), (down_x, down_y))
    for partner in partners:
        pl.semaphore_signal(barrier, inc=1, device_id=partner, device_id_type=MESH)
    small = [
        pltpu.make_async_copy(src, dst, io_sem.at[4 + n])
        for n, (src, dst) in enumerate(
            (
                (wx_hbm, wx_ref),
                (wy_hbm, wy_ref),
                (sx_hbm, sx_ref),
                (sy_hbm, sy_ref),
                (wz_hbm, wz_ref),
                (sz_hbm, sz_ref),
                (list_hbm, list_ref),
            )
        )
    ]
    loads = [pltpu.make_async_copy(cons_hbm.at[:, a], state.at[:, a], io_sem.at[a]) for a in range(4)]
    for a in (0, 3, 1, 2):
        loads[a].start()
    for copy in small:
        copy.start()

    shape = (rows, lanes)
    row = lax.broadcasted_iota(jnp.int32, shape, 0)
    row_i, row_j = row // tile_y, row % tile_y

    def roll_rows(value, shift):
        shift = shift % rows
        return value if shift == 0 else pltpu.roll(value, shift, 0)

    def roll_lanes(value, shift):
        return pltpu.roll(value, shift % lanes, 1)

    def pack_x(q, carry):
        for v in range(5):
            for side, node, first in ((0, 0, 0), (1, 3, rows - tile_y)):
                packed = None
                for c in range(4):
                    part = roll_rows(state[v, node, q, c], tile_y * c - first)
                    packed = part if packed is None else jnp.where(row_i == c, part, packed)
                xs[side, v, q] = packed
        return carry

    def pack_y(q, carry):
        for v in range(5):
            for side, node, first in ((0, 0, 0), (1, 3, tile_y - 1)):
                for group in range(4 // tile_y):
                    packed = None
                    for c in range(tile_y):
                        part = roll_rows(state[v, q, node, group * tile_y + c], c - first)
                        packed = part if packed is None else jnp.where(row_j == c, part, packed)
                    ys[side, v, q, group] = packed
        return carry

    last_i, last_j = tile_x - 1, tile_y - 1
    early = ((0, 0, last_j), (0, 1, rows - 1), (1, 0, rows - tile_y), (1, 1, rows - 1))

    def early_node(d, group, sub):
        if d == 0:
            return group * tile_y + sub % tile_y, sub // tile_y
        return (group * rows + sub) // 4, sub % 4

    def pack_early(v, carry):
        for slot, (d, side, place) in enumerate(early):
            for group in range(16 // rows):
                packed = None
                for sub in range(rows):
                    q, c = early_node(d, group, sub)
                    value = state[v, 3 * side, q, c] if d == 0 else state[v, q, 3 * side, c]
                    part = roll_rows(value, sub - place)
                    packed = part if packed is None else jnp.where(row == sub, part, packed)
                cs[slot, v, group] = packed
        return carry

    def remote(src, dst, slot, device):
        return pltpu.make_async_remote_copy(
            src_ref=src,
            dst_ref=dst,
            send_sem=send_sem.at[slot],
            recv_sem=recv_sem.at[slot],
            device_id=device,
            device_id_type=MESH,
        )

    for copy in small:
        copy.wait()

    def along(ref, start, total, tile, index):
        values = [ref[lax.rem(start + total + i, total)] for i in range(-1, tile + 1)]

        def pick(offset):
            vector = jnp.full(shape, values[1 + offset], jnp.float32)
            for i in range(1, tile):
                vector = jnp.where(index == i, values[1 + offset + i], vector)
            return vector

        return values, pick(-1), pick(0), pick(1)

    total_x, total_y = size_x * tile_x, size_y * tile_y
    wx_all, wx_p, wx, _ = along(wx_ref, me_x * tile_x, total_x, tile_x, row_i)
    wy_all, wy_p, wy, _ = along(wy_ref, me_y * tile_y, total_y, tile_y, row_j)
    sx_all, sx_p, sx, sx_n = along(sx_ref, me_x * tile_x, total_x, tile_x, row_i)
    sy_all, sy_p, sy, sy_n = along(sy_ref, me_y * tile_y, total_y, tile_y, row_j)
    nx_all = [wx_all[i] + time_step * (sx_all[i + 1] - sx_all[i]) for i in range(tile_x + 1)]
    ny_all = [wy_all[i] + time_step * (sy_all[i + 1] - sy_all[i]) for i in range(tile_y + 1)]
    wz = jnp.broadcast_to(wz_ref[...], shape)
    sz = jnp.broadcast_to(sz_ref[...], shape)
    sz_n = roll_lanes(sz, -1)
    nx, ny, nz = (
        wx + time_step * (sx_n - sx),
        wy + time_step * (sy_n - sy),
        wz + time_step * (sz_n - sz),
    )
    px, py = wx_p + time_step * (sx - sx_p), wy_p + time_step * (sy - sy_p)
    pz = roll_lanes(nz, 1)
    mass = nx * ny * nz
    ratio = wx * wy * wz / mass
    geo[RATIO] = ratio
    for d, (width, low, high) in enumerate(((wx, sx, sx_n), (wy, sy, sy_n), (wz, sz, sz_n))):
        for a in range(4):
            geo[SPEED + 4 * d + a] = low * float((1.0 - NODES[a]) / 2.0) + high * float(
                (1.0 + NODES[a]) / 2.0
            )
        for q, xi in enumerate((-5.0 / 6.0, 0.0, 5.0 / 6.0)):
            geo[INTER + 3 * d + q] = low * ((1.0 - xi) / 2.0) + high * ((1.0 + xi) / 2.0)
        geo[FACE + 2 * d] = low
        geo[FACE + 2 * d + 1] = high
        kappa = -time_step * ratio / width
        geo[SCALE + 2 * d] = kappa * float(1.0 / WEIGHTS[0])
        geo[SCALE + 2 * d + 1] = kappa * float(1.0 / WEIGHTS[1])

    entries = list_ref[...]
    count = entries.shape[-1]
    in_row = jnp.where(
        lax.broadcasted_iota(jnp.int32, (rows, count), 0) == entries // lanes, 1.0, 0.0
    )
    in_lane = jnp.where(
        lax.broadcasted_iota(jnp.int32, (lanes, count), 0) == entries % lanes, 1.0, 0.0
    )
    geo[MASK] = lax.dot_general(
        in_row, in_lane, (((1,), (1,)), ((), ())), preferred_element_type=jnp.float32
    )

    def prepare(a, carry):
        for b in range(4):
            for c in range(4):
                inverse, pressure, sound = primitives([state[v, a, b, c] for v in range(5)])
                inv_s[a, b, c] = inverse
                pres_s[a, b, c] = pressure
                sound_s[a, b, c] = sound
            zl[0, a, b] = roll_lanes(state[0, a, b, 3], 1)
            zl[3, a, b] = roll_lanes(state[3, a, b, 3] * inverse, 1)
            zl[5, a, b] = roll_lanes(sound, 1)
        return carry


    def interior(d, parts, index, carry):
        first, second = index // 4, index % 4

        def at(n):
            return ((n, first, second), (first, n, second), (first, second, n))[d]

        mask = geo[MASK] > 0.5
        sound = [sound_s[at(n)] for n in range(4)]
        normal = [state[(d + 1,) + at(n)] * inv_s[at(n)] for n in range(4)]
        weights = [
            wave_weights(normal[q], sound[q], normal[q + 1], sound[q + 1], geo[INTER + 3 * d + q])
            for q in range(3)
        ]
        relative = [normal[n] - geo[SPEED + 4 * d + n] for n in range(4)]
        if parts != DENSITY:
            pressure = [pres_s[at(n)] for n in range(4)]
            work = [pressure[n] * normal[n] for n in range(4)]
        if d == 2:
            behind = zl[3, first, second]
            star_left, star_right = wave_weights(
                behind, zl[5, first, second], normal[0], sound[0], geo[FACE + 4]
            )
            if parts != DENSITY:
                push = zl[6, first, second]
        for v in parts:
            value = [state[(v,) + at(n)] for n in range(4)]
            flux = [value[n] * relative[n] for n in range(4)]
            inner = [value[q] * weights[q][0] + value[q + 1] * weights[q][1] for q in range(3)]
            if d == 2:
                if v == 3:
                    rolled = zl[7, first, second]
                else:
                    rolled = zl[v, first, second]
                star = rolled * star_left + value[0] * star_right
            extra = pressure if v == d + 1 else work if v == 4 else None
            if extra is not None:
                flux = [flux[n] + extra[n] for n in range(4)]
                inner = [inner[q] + (extra[q] + extra[q + 1]) for q in range(3)]
            if d == 2:
                if v == 3:
                    star = star + (push + pressure[0])
                if v == 4:
                    star = star + (push * behind + work[0])
                zst[v, first, second] = star
            smooth = dg_fluxes(flux)
            chosen = [jnp.where(mask, inner[q], smooth[q]) for q in range(3)]
            head = chosen[0] - star if d == 2 else chosen[0]
            change = [head, chosen[1] - chosen[0], chosen[2] - chosen[1], -chosen[2]]
            for n in range(4):
                where = (v,) + at(n)
                scale = geo[SCALE + 2 * d + (0 if n in (0, 3) else 1)]
                if d == 0:
                    base = geo[RATIO] * value[n]
                else:
                    base = out[where]
                out[where] = base + scale * change[n]
        return carry

    def above(v, a):
        for b in range(4):
            out[v, a, b, 3] = out[v, a, b, 3] + geo[SCALE + 4] * roll_lanes(zst[v, a, b], -1)


    def spots(d, q, c):
        return ((0, q, c), (3, q, c)) if d == 0 else ((q, 0, c), (q, 3, c))

    def inside(d, q, carry):
        shift = (tile_y, 1)[d]
        edge = (row_i, row_j)[d]
        for c in range(4):
            low, high = spots(d, q, c)
            left, right = wave_weights(
                roll_rows(state[(d + 1,) + high] * inv_s[high], shift),
                roll_rows(sound_s[high], shift),
                state[(d + 1,) + low] * inv_s[low],
                sound_s[low],
                geo[FACE + 2 * d],
            )
            star = roll_rows(state[(0,) + high], shift) * left + state[(0,) + low] * right
            star = jnp.where(edge > 0, star, 0.0)
            scale = geo[SCALE + 2 * d]
            out[(0,) + low] = out[(0,) + low] - scale * star
            out[(0,) + high] = out[(0,) + high] + scale * roll_rows(star, -shift)
        return carry


    def first_density():
        lax.fori_loop(0, 4, prepare, 0)
        for d in range(3):
            lax.fori_loop(0, 16, functools.partial(interior, d, DENSITY), 0)
        for a in range(4):
            above(0, a)
        for d in range(2):
            lax.fori_loop(0, 4, functools.partial(inside, d), 0)

    ring_end = jnp.logical_or(me_x == size_x - 1, me_y == size_y - 1)
    for a in (0, 3, 1, 2):
        loads[a].wait()
    lax.fori_loop(0, 5, pack_early, 0)
    pl.when(jnp.logical_not(ring_end))(first_density)
    pl.semaphore_wait(barrier, len(partners))
    heralds = [
        remote(cs.at[2], cr.at[3], 9, (me_x, down_y)),
        remote(cs.at[3], cr.at[2], 10, (me_x, up_y)),
        remote(cs.at[0], cr.at[1], 7, (down_x, me_y)),
        remote(cs.at[1], cr.at[0], 8, (up_x, me_y)),
    ]
    for copy in heralds:
        copy.start()
    faces = [
        remote(lys.at[0], lyr.at[1], 2, (me_x, down_y)),
        remote(lys.at[1], lyr.at[0], 3, (me_x, up_y)),
        remote(lxs.at[0], lxr.at[1], 0, (down_x, me_y)),
        remote(lxs.at[1], lxr.at[0], 1, (up_x, me_y)),
    ]
    halves = 4 // tile_y
    groups = 4 * halves
    kept = groups - groups // tile_x
    free_y, free_x = row_i == last_i, row_j == last_j

    def group_of(ref, side, v, k):
        return ref[side, v, k // halves, k % halves]

    def squeeze_y(v, carry):
        for side in range(2):
            for k in range(kept):
                source, piece = kept + k // last_i, k % last_i
                moved = roll_rows(group_of(ys, side, v, source), rows - tile_y - piece * tile_y)
                lys[side, v, k] = jnp.where(free_y, moved, group_of(ys, side, v, k))
        return carry

    def squeeze_x(v, carry):
        for side in range(2):
            for k in range(4 // tile_y):
                moved = roll_rows(xs[side, v, tile_y * k + 1], last_j)
                lxs[side, v, k] = jnp.where(free_x, moved, xs[side, v, tile_y * k])
        return carry

    def send_y():
        lax.fori_loop(0, 4, pack_y, 0)
        lax.fori_loop(0, 5, squeeze_y, 0)
        faces[0].start()
        faces[1].start()

    held_back = jnp.logical_and(me_x == size_x - 1, me_y != size_y - 1)
    pl.when(jnp.logical_not(held_back))(send_y)
    lax.fori_loop(0, 4, pack_x, 0)
    lax.fori_loop(0, 5, squeeze_x, 0)
    faces[2].start()
    faces[3].start()

    pl.when(ring_end)(first_density)

    second = DERIV @ DERIV
    ends = (0, 3)

    def combine(coefficients, values):
        total = None
        for n in range(4):
            if values[n] is not None:
                term = float(coefficients[n]) * values[n]
                total = term if total is None else total + term
        return total

    def columns(density, factors, wanted):
        along_x = {
            (p, b, c): combine(DERIV[p], [density[a][b][c] for a in range(4)])
            for p in ends
            for b in range(4)
            for c in range(4)
            if b in ends or c in ends
        }
        along_y = {
            (a, q, c): combine(DERIV[q], [density[a][b][c] for b in range(4)])
            for q in ends
            for a in ends
            for c in range(4)
        }

        def corner(kind, p, q, r):
            if kind == 0:
                return combine(second[p], [density[a][q][r] for a in range(4)])
            if kind == 1:
                return combine(second[q], [density[p][b][r] for b in range(4)])
            if kind == 2:
                return combine(second[r], [density[p][q][c] for c in range(4)])
            if kind == 3:
                return combine(DERIV[q], [along_x[p, b, r] for b in range(4)])
            if kind == 4:
                return combine(DERIV[r], [along_x[p, q, c] for c in range(4)])
            return combine(DERIV[r], [along_y[p, q, c] for c in range(4)])

        found = []
        for kind in range(6):
            column = {}
            for p, q in wanted:
                low, high = corner(kind, p, q, 0), corner(kind, p, q, 3)
                column[p, q] = factors[kind] * low + roll_lanes(factors[kind] * high, 1)
            found.append(column)
        return found

    def pairs(jx, jy, jz):
        return (jx * jx, jy * jy, jz * jz, jx * jy, jx * jz, jy * jz)

    ix, iy, iz = 2.0 / nx, 2.0 / ny, 2.0 / nz
    factors = [mass * pair for pair in pairs(ix, iy, iz)]

    def up_y_shift(value):
        return jnp.where(row_j == 0, 0.0, roll_rows(value, 1))

    def up_x_shift(value):
        return jnp.where(row_i == 0, 0.0, roll_rows(value, tile_y))

    three = ((0, 3), (3, 0), (3, 3))
    density = [[[out[0, a, b, c] for c in range(4)] for b in range(4)] for a in range(4)]
    x_rim, y_rim = [None] * -(-6 // tile_x), [None] * -(-6 // tile_y)
    d_rim = None
    for kind, column in enumerate(columns(density, factors, three)):
        high_x = column[3, 0] + up_y_shift(column[3, 3])
        slot, place = kind // tile_x, kind % tile_x
        part = roll_rows(high_x, tile_y * place - (rows - tile_y))
        x_rim[slot] = part if place == 0 else jnp.where(row_i == place, part, x_rim[slot])
        rim = column[0, 3] + up_x_shift(column[3, 3])
        slot, place = kind // tile_y, kind % tile_y
        part = roll_rows(rim, place - last_j)
        y_rim[slot] = part if place == 0 else jnp.where(row_j == place, part, y_rim[slot])
        part = roll_rows(column[3, 3], kind - (rows - 1))
        d_rim = part if kind == 0 else jnp.where(row == kind, part, d_rim)
    for slot, value in enumerate(x_rim):
        rxs[slot] = value
    for slot, value in enumerate(y_rim):
        rys[slot] = value
    rds[...] = d_rim
    rims = [
        remote(rds, rdr, 6, (up_x, up_y)),
        remote(rys, ryr, 5, (me_x, up_y)),
        remote(rxs, rxr, 4, (up_x, me_y)),
    ]
    rims[0].start()
    pl.when(held_back)(send_y)

    def behind_rest(a, carry):
        for b in range(4):
            zl[1, a, b] = roll_lanes(state[1, a, b, 3], 1)
            zl[2, a, b] = roll_lanes(state[2, a, b, 3], 1)
            zl[7, a, b] = roll_lanes(state[3, a, b, 3], 1)
            zl[4, a, b] = roll_lanes(state[4, a, b, 3], 1)
            zl[6, a, b] = roll_lanes(pres_s[a, b, 3], 1)
        return carry

    def above_rest(a, carry):
        for v in REST:
            above(v, a)
        return carry

    def rest():
        lax.fori_loop(0, 4, behind_rest, 0)
        for d in range(3):
            lax.fori_loop(0, 16, functools.partial(interior, d, REST), 0)
        lax.fori_loop(0, 4, above_rest, 0)

    pl.when(jnp.logical_not(ring_end))(rest)

    row_up_x, row_low_x, row_under_x = 3, last_j, last_j - 1
    row_up_y, row_low_y, row_under_y = rows - 1, rows - tile_y, rows - tile_y - 1
    is_x = row <= row_up_x
    lower = jnp.logical_or(row == row_low_x, row == row_low_y)
    part_x = jnp.where(row == row_under_x, nx_all[0], jnp.where(row == row_low_x, nx_all[1], nx_all[tile_x]))
    part_y = jnp.where(row == row_under_y, ny_all[0], jnp.where(row == row_low_y, ny_all[1], ny_all[tile_y]))
    across = jnp.where(is_x, wy_all[tile_y], wx_all[tile_x])
    part = jnp.where(lower, 1.0, -1.0) * across * wz * float(time_step / WEIGHTS[3])
    part_factors = [part * pair for pair in pairs(2.0 / part_x, 2.0 / part_y, iz)]

    def face_stars(slot):
        d, side, place = early[slot]
        found = []
        for group in range(16 // rows):
            own = [cs[slot, v, group] for v in range(5)]
            other = [cr[slot, v, group] for v in range(5)]
            low, high = (other, own) if side == 0 else (own, other)
            low_inverse, _, low_sound = primitives(low)
            high_inverse, _, high_sound = primitives(high)
            left, right = wave_weights(
                low[d + 1] * low_inverse,
                low_sound,
                high[d + 1] * high_inverse,
                high_sound,
                geo[FACE + 2 * d + side, place : place + 1],
            )
            found.append(low[0] * left + high[0] * right)
        return found

    def put(field, a, b, c, value):
        old = field[a][b][c]
        field[a][b][c] = value if old is None else old + value

    def part_field(d):
        field = [[[None] * 4 for b in range(4)] for a in range(4)]
        lows, ups = face_stars(2 * d), face_stars(2 * d + 1)
        up_row, low_row = (row_up_x, row_up_y)[d], (row_low_x, row_low_y)[d]
        under_row = (row_under_x, row_under_y)[d]
        for group in range(16 // rows):
            for sub in range(rows):
                q, c = early_node(d, group, sub)
                top, floor = ((3, q, c), (0, q, c)) if d == 0 else ((q, 3, c), (q, 0, c))
                value = jnp.where(row == up_row, roll_rows(ups[group], up_row - sub), 0.0)
                below = roll_rows(lows[group], under_row - sub)
                put(field, *top, jnp.where(row == under_row, below, value))
                low = roll_rows(lows[group], low_row - sub)
                put(field, *floor, jnp.where(row == low_row, low, 0.0))
        return field

    def y_part():
        heralds[2].wait()
        heralds[3].wait()
        y_rim = [None] * -(-6 // tile_y)
        for kind, column in enumerate(columns(part_field(0), part_factors, ((0, 3), (3, 3)))):
            near = jnp.where(row == last_j, column[0, 3] + roll_rows(column[3, 3], 1), 0.0)
            near = jnp.where(row == last_j + tile_y, roll_rows(column[3, 3], tile_y), near)
            rim = jnp.where(row == rows - 1, roll_rows(column[0, 3], rows - 1 - row_up_x), near)
            slot, place = kind // tile_y, kind % tile_y
            part = roll_rows(rim, place - last_j)
            y_rim[slot] = part if place == 0 else jnp.where(row_j == place, part, y_rim[slot])
        for slot, value in enumerate(y_rim):
            rys[slot] = rys[slot] + value
        rims[1].start()

    def x_part():
        heralds[0].wait()
        heralds[1].wait()
        x_rim = [None] * -(-6 // tile_x)
        for kind, column in enumerate(columns(part_field(1), part_factors, ((3, 0), (3, 3)))):
            high_x = column[3, 0] + roll_rows(column[3, 3], 1)
            slot, place = kind // tile_x, kind % tile_x
            part = roll_rows(high_x, tile_y * place - (rows - tile_y))
            x_rim[slot] = part if place == 0 else jnp.where(row_i == place, part, x_rim[slot])
        for slot, value in enumerate(x_rim):
            rxs[slot] = rxs[slot] + value
        rims[2].start()

    first_x = me_x == size_x - 1
    pl.when(first_x)(x_part)
    y_part()
    pl.when(jnp.logical_not(first_x))(x_part)
    pl.when(ring_end)(rest)

    def surface(d, q, carry):
        shift = (tile_y, 1)[d]
        edge, last = ((row_i, last_i), (row_j, last_j))[d]
        speed = geo[FACE + 2 * d]
        top_speed = geo[FACE + 2 * d + 1, rows - 1 : rows]
        scale = geo[SCALE + 2 * d]
        tops = []
        for group in range(1 if d == 0 else 4 // tile_y):
            if d == 0:
                own = [xs[1, v, q] for v in range(5)]
                other = [xr[1, v, q] for v in range(5)]
            else:
                own = [ys[1, v, q, group] for v in range(5)]
                other = [yr[1, v, q, group] for v in range(5)]
            own_inverse, own_pressure, own_sound = primitives(own)
            inverse, pressure, sound = primitives(other)
            tops.append(
                twice_flux(
                    own,
                    own_pressure,
                    own_sound,
                    own[d + 1] * own_inverse,
                    other,
                    pressure,
                    sound,
                    other[d + 1] * inverse,
                    d,
                    top_speed,
                )
            )
        for c in range(4):
            low, high = spots(d, q, c)
            own = [state[(v,) + low] for v in range(5)]
            other = []
            for v in range(5):
                if d == 0:
                    halo = roll_rows(xr[0, v, q], -tile_y * c)
                else:
                    halo = roll_rows(yr[0, v, q, c // tile_y], -(c % tile_y))
                moved = roll_rows(state[(v,) + high], shift)
                other.append(jnp.where(edge == 0, halo, moved))
            inverse, pressure, sound = primitives(other)
            star = twice_flux(
                other,
                pressure,
                sound,
                other[d + 1] * inverse,
                own,
                pres_s[low],
                sound_s[low],
                own[d + 1] * inv_s[low],
                d,
                speed,
            )
            for v in range(5):
                if d == 0:
                    top = roll_rows(tops[0][v], rows - tile_y - tile_y * c)
                else:
                    top = roll_rows(tops[c // tile_y][v], tile_y - 1 - c % tile_y)
                if v == 0:
                    down = jnp.where(edge == 0, star[v], 0.0)
                    up = jnp.where(edge == last, top, 0.0)
                    ph[d, q, c] = down
                else:
                    down = star[v]
                    up = jnp.where(edge == last, top, roll_rows(star[v], -shift))
                out[(v,) + low] = out[(v,) + low] - scale * down
                out[(v,) + high] = out[(v,) + high] + scale * up
        return carry

    def spread_x(v, carry):
        for side in range(2):
            for q in range(4):
                k = q // tile_y
                late, first = lxr[side, v, k], cr[side, v, k]
                if q % tile_y == 0:
                    first = roll_rows(first, last_j)
                else:
                    late = roll_rows(late, -last_j)
                xr[side, v, q] = jnp.where(free_x, first, late)
        return carry

    def spread_y(v, carry):
        for side in range(2):
            for k in range(groups):
                if k < kept:
                    value = lyr[side, v, k]
                else:
                    value = None
                    for piece in range(last_i):
                        part = lyr[side, v, (k - kept) * last_i + piece]
                        part = roll_rows(part, piece * tile_y - (rows - tile_y))
                        value = part if value is None else jnp.where(row_i == piece, part, value)
                first = cr[2 + side, v, k // tile_x]
                first = roll_rows(first, rows - tile_y - (k % tile_x) * tile_y)
                yr[side, v, k // halves, k % halves] = jnp.where(free_y, first, value)
        return carry

    faces[2].wait()
    faces[3].wait()
    lax.fori_loop(0, 5, spread_x, 0)
    lax.fori_loop(0, 4, functools.partial(surface, 0), 0)
    faces[0].wait()
    faces[1].wait()
    lax.fori_loop(0, 5, spread_y, 0)
    lax.fori_loop(0, 4, functools.partial(surface, 1), 0)

    density = [[[out[0, a, b, c] for c in range(4)] for b in range(4)] for a in range(4)]
    for kind, column in enumerate(columns(density, factors, ((0, 0), (0, 3), (3, 0), (3, 3)))):
        low_x = column[0, 0] + up_y_shift(column[0, 3])
        high_x = column[3, 0] + up_y_shift(column[3, 3])
        hess_ref[kind] = low_x + up_x_shift(high_x)

    bottom = row_j == 0
    side_y, side_w = jnp.full(shape, ny_all[1], jnp.float32), jnp.full(shape, wy_all[1], jnp.float32)
    for n in range(1, tile_y):
        side_y = jnp.where(row_i == n, ny_all[1 + n], side_y)
        side_w = jnp.where(row_i == n, wy_all[1 + n], side_w)
    ghost_x = jnp.where(bottom, nx, nx_all[0])
    ghost_y = jnp.where(bottom, py, side_y)
    ghost = jnp.where(bottom, wx, side_w) * wz * float(-time_step / WEIGHTS[3])
    ghost_factors = [ghost * pair for pair in pairs(2.0 / ghost_x, 2.0 / ghost_y, iz)]
    field = [[[None] * 4 for b in range(4)] for a in range(4)]
    for n in range(4):
        for c in range(4):
            from_x = jnp.zeros(shape, jnp.float32)
            for m in range(tile_y):
                place = m * tile_y + last_j
                from_x = jnp.where(row == place, roll_rows(ph[0, n, c], place - m), from_x)
            put(field, 3, n, c, from_x)
            put(field, n, 3, c, ph[1, n, c])
    for kind, column in enumerate(columns(field, ghost_factors, three)):
        total = hess_ref[kind] + jnp.where(bottom, column[0, 3], 0.0)
        total = total + jnp.where(bottom, up_x_shift(column[3, 3]), 0.0)
        for m in range(tile_y):
            place = m * tile_y + last_j
            total = total + jnp.where(row == m, roll_rows(column[3, 0], m - place), 0.0)
            if m < last_j:
                total = total + jnp.where(row == m + 1, roll_rows(column[3, 3], m + 1 - place), 0.0)
        hess_ref[kind] = total

    inverse = 1.0 / ((nx + px) * (ny + py) * (nz + pz))
    for copy in rims:
        copy.wait()
    for kind in range(6):
        total = hess_ref[kind]
        from_x = roll_rows(rxr[kind // tile_x], -tile_y * (kind % tile_x))
        total = total + jnp.where(row_i == 0, from_x, 0.0)
        from_y = roll_rows(ryr[kind // tile_y], -(kind % tile_y))
        total = total + jnp.where(row_j == 0, from_y, 0.0)
        total = total + jnp.where(row == 0, roll_rows(rdr[...], -kind), 0.0)
        hess_ref[kind] = total * inverse


def emit(adv_ref, hess_ref, adv_out, hess_out, sem):
    copies = [
        pltpu.make_async_copy(adv_ref, adv_out, sem.at[0]),
        pltpu.make_async_copy(hess_ref, hess_out, sem.at[1]),
    ]
    for copy in copies:
        copy.start()
    for copy in copies:
        copy.wait()


def solution(mesh):
    sizes = (mesh.shape["gx"], mesh.shape["gy"])

    def local(conserved, troubled_list, widths_x, widths_y, widths_z, speed_x, speed_y, speed_z):
        tile_x, tile_y, column = conserved.shape[4:]
        rows = tile_x * tile_y
        f32 = jnp.float32
        vmem = pl.BlockSpec(memory_space=pltpu.VMEM)
        whole = pl.BlockSpec(memory_space=pl.ANY)
        full = (5, 4, 4, 4, rows, column)
        nodal = (4, 4, 4, rows, column)
        x_face = (2, 5, 4, rows, column)
        y_face = (2, 5, 4, 4 // tile_y, rows, column)
        groups = 4 * (4 // tile_y)
        x_late = (2, 5, 4 // tile_y, rows, column)
        y_late = (2, 5, groups - groups // tile_x, rows, column)
        herald = (4, 5, 16 // rows, rows, column)
        x_rim = (-(-6 // tile_x), rows, column)
        y_rim = (-(-6 // tile_y), rows, column)
        advanced, hessian = pl.pallas_call(
            functools.partial(kernel, tile_x, tile_y, sizes),
            out_shape=(
                pltpu.VMEM(full, f32),
                pltpu.VMEM((6, rows, column), f32),
            ),
            in_specs=[whole] * 8,
            out_specs=(vmem, vmem),
            scratch_shapes=[
                pltpu.VMEM((1, troubled_list.shape[0]), jnp.int32),
                pltpu.SMEM(widths_x.shape, f32),
                pltpu.SMEM(widths_y.shape, f32),
                pltpu.VMEM((1, column), f32),
                pltpu.SMEM(speed_x.shape, f32),
                pltpu.SMEM(speed_y.shape, f32),
                pltpu.VMEM((1, column), f32),
                pltpu.VMEM(full, f32),
                pltpu.VMEM(nodal, f32),
                pltpu.VMEM(nodal, f32),
                pltpu.VMEM(nodal, f32),
                pltpu.VMEM((8, 4, 4, rows, column), f32),
                pltpu.VMEM((5, 4, 4, rows, column), f32),
                pltpu.VMEM((2, 4, 4, rows, column), f32),
                pltpu.VMEM((GEO, rows, column), f32),
                pltpu.VMEM(herald, f32),
                pltpu.VMEM(herald, f32),
                pltpu.VMEM(x_late, f32),
                pltpu.VMEM(x_late, f32),
                pltpu.VMEM(y_late, f32),
                pltpu.VMEM(y_late, f32),
                pltpu.VMEM(x_face, f32),
                pltpu.VMEM(x_face, f32),
                pltpu.VMEM(y_face, f32),
                pltpu.VMEM(y_face, f32),
                pltpu.VMEM(x_rim, f32),
                pltpu.VMEM(x_rim, f32),
                pltpu.VMEM(y_rim, f32),
                pltpu.VMEM(y_rim, f32),
                pltpu.VMEM((rows, column), f32),
                pltpu.VMEM((rows, column), f32),
                pltpu.SemaphoreType.DMA((11,)),
                pltpu.SemaphoreType.DMA((11,)),
                pltpu.SemaphoreType.DMA((11,)),
            ],
            compiler_params=pltpu.CompilerParams(collective_id=0, has_side_effects=True),
        )(
            conserved.reshape(full),
            troubled_list.reshape(1, -1),
            widths_x,
            widths_y,
            widths_z.reshape(1, -1),
            speed_x,
            speed_y,
            speed_z.reshape(1, -1),
        )
        advanced = pltpu.with_memory_space_constraint(advanced, pltpu.VMEM)
        hessian = pltpu.with_memory_space_constraint(hessian, pltpu.VMEM)
        advanced, hessian = pl.pallas_call(
            emit,
            out_shape=(
                jax.ShapeDtypeStruct(full, f32),
                jax.ShapeDtypeStruct((6, rows, column), f32),
            ),
            in_specs=[whole, whole],
            out_specs=(whole, whole),
            scratch_shapes=[pltpu.SemaphoreType.DMA((2,))],
        )(advanced, hessian)
        return advanced.reshape(conserved.shape), hessian.reshape(6, tile_x, tile_y, column)

    in_specs = (
        P(None, None, None, None, "gx", "gy", None),
        P(("gx", "gy")),
        P(),
        P(),
        P(),
        P(),
        P(),
        P(),
    )
    out_specs = (P(None, None, None, None, "gx", "gy", None), P(None, "gx", "gy", None))
    return jax.shard_map(local, mesh=mesh, in_specs=in_specs, out_specs=out_specs, check_vma=False)
```

```python
import functools

import jax
import jax.numpy as jnp
import numpy as np
from jax import lax
from jax.experimental import pallas as pl
from jax.experimental.pallas import tpu as pltpu
from jax.sharding import PartitionSpec as P

MESH = pl.DeviceIdType.MESH
time_step = 0.05
gamma_ratio = 1.4


def lgl_tables():
    nodes = np.array([-1.0, -1.0 / np.sqrt(5.0), 1.0 / np.sqrt(5.0), 1.0])
    weights = np.array([1.0 / 6.0, 5.0 / 6.0, 5.0 / 6.0, 1.0 / 6.0])
    barycentric = np.ones(4)
    for row_a in range(4):
        for row_b in range(4):
            if row_a != row_b:
                barycentric[row_a] = barycentric[row_a] / (nodes[row_a] - nodes[row_b])
    deriv = np.zeros((4, 4))
    for row_a in range(4):
        for row_b in range(4):
            if row_a != row_b:
                deriv[row_a, row_b] = (
                    barycentric[row_b] / barycentric[row_a] / (nodes[row_a] - nodes[row_b])
                )
    for row_a in range(4):
        deriv[row_a, row_a] = -np.sum(deriv[row_a])
    return (nodes, weights, deriv)


NODES, WEIGHTS, DERIV = lgl_tables()
SPEED, INTER, SCALE, FACE = 0, 12, 21, 27
RATIO, MASK, GEO = 33, 34, 35
ALL, DENSITY, REST = (0, 1, 2, 3, 4), (0,), (1, 2, 3, 4)


def primitives(state):
    inverse = 1.0 / state[0]
    square = state[1] * state[1] + state[2] * state[2] + state[3] * state[3]
    pressure = (gamma_ratio - 1.0) * (state[4] - 0.5 * square * inverse)
    ratio = gamma_ratio * pressure * inverse
    return inverse, pressure, ratio * lax.rsqrt(ratio)


def twice_flux(low, p_low, c_low, u_low, high, p_high, c_high, u_high, direction, speed):
    rel_low = u_low - speed
    rel_high = u_high - speed
    fastest = jnp.maximum(jnp.abs(rel_low) + c_low, jnp.abs(rel_high) + c_high)
    left = rel_low + fastest
    right = rel_high - fastest
    flux = [low[v] * left + high[v] * right for v in range(5)]
    flux[direction + 1] = flux[direction + 1] + (p_low + p_high)
    flux[4] = flux[4] + (p_low * u_low + p_high * u_high)
    return flux


def dg_table():
    lifted = DERIV.copy()
    lifted[0, 0] += 1.0 / WEIGHTS[0]
    lifted[3, 3] -= 1.0 / WEIGHTS[3]
    return np.cumsum(2.0 * WEIGHTS[:, None] * lifted, axis=0)


SUBCELL = dg_table()


def dg_fluxes(values):
    outer, inner = values[0] + values[3], values[1] + values[2]
    step = inner - outer
    even = outer + float(0.5 * (SUBCELL[0, 1] + SUBCELL[2, 1])) * step
    middle = outer + float(SUBCELL[1, 1]) * step
    odd = float(0.5 * (SUBCELL[0, 0] - SUBCELL[2, 0])) * (values[0] - values[3])
    odd = odd + float(0.5 * (SUBCELL[0, 1] - SUBCELL[2, 1])) * (values[1] - values[2])
    return even + odd, middle, even - odd


def wave_weights(u_low, c_low, u_high, c_high, speed):
    rel_low = u_low - speed
    rel_high = u_high - speed
    fastest = jnp.maximum(jnp.abs(rel_low) + c_low, jnp.abs(rel_high) + c_high)
    return rel_low + fastest, rel_high - fastest


def kernel(
    tile_x,
    tile_y,
    sizes,
    cons_hbm,
    rows_hbm,
    list_hbm,
    wx_hbm,
    wy_hbm,
    wz_hbm,
    sx_hbm,
    sy_hbm,
    sz_hbm,
    out,
    hess_ref,
    list_ref,
    wx_ref,
    wy_ref,
    wz_ref,
    sx_ref,
    sy_ref,
    sz_ref,
    state,
    inv_s,
    pres_s,
    sound_s,
    zl,
    zst,
    ph,
    geo,
    cs,
    cr,
    theirs,
    lxs,
    lxr,
    lys,
    lyr,
    xs,
    xr,
    ys,
    yr,
    rxs,
    rxr,
    rys,
    ryr,
    rds,
    rdr,
    io_sem,
    send_sem,
    recv_sem,
):
    size_x, size_y = sizes
    rows = tile_x * tile_y
    lanes = state.shape[-1]
    me_x, me_y = lax.axis_index("gx"), lax.axis_index("gy")
    up_x, down_x = lax.rem(me_x + 1, size_x), lax.rem(me_x + size_x - 1, size_x)
    up_y, down_y = lax.rem(me_y + 1, size_y), lax.rem(me_y + size_y - 1, size_y)

    barrier = pltpu.get_barrier_semaphore()
    partners = ((me_x, down_y), (me_x, up_y), (down_x, me_y), (up_x, me_y), (down_x, down_y))
    for partner in partners:
        pl.semaphore_signal(barrier, inc=1, device_id=partner, device_id_type=MESH)
    small = [
        pltpu.make_async_copy(src, dst, io_sem.at[4 + n])
        for n, (src, dst) in enumerate(
            (
                (wx_hbm, wx_ref),
                (wy_hbm, wy_ref),
                (sx_hbm, sx_ref),
                (sy_hbm, sy_ref),
                (wz_hbm, wz_ref),
                (sz_hbm, sz_ref),
                (list_hbm, list_ref),
            )
        )
    ]
    last_i, last_j = tile_x - 1, tile_y - 1
    early = ((0, 0, last_j), (0, 1, rows - 1), (1, 0, rows - tile_y), (1, 1, rows - 1))

    picks = []
    for slot, (d, side, place) in enumerate(early):
        view = rows_hbm.at[:, 3 * side, :, :, place] if d == 0 else rows_hbm.at[:, :, 3 * side, :, place]
        picks.append(pltpu.make_async_copy(view, cs.at[slot], io_sem.at[11 + slot]))
    for slot in (3, 1, 2, 0):
        picks[slot].start()
    loads = [pltpu.make_async_copy(cons_hbm.at[:, a], state.at[:, a], io_sem.at[a]) for a in range(4)]
    for a in (0, 3, 1, 2):
        loads[a].start()
    for copy in small:
        copy.start()

    shape = (rows, lanes)
    row = lax.broadcasted_iota(jnp.int32, shape, 0)
    row_i, row_j = row // tile_y, row % tile_y

    def roll_rows(value, shift):
        shift = shift % rows
        return value if shift == 0 else pltpu.roll(value, shift, 0)

    def roll_lanes(value, shift):
        return pltpu.roll(value, shift % lanes, 1)

    def pack_x(q, carry):
        for v in range(5):
            for side, node, first in ((0, 0, 0), (1, 3, rows - tile_y)):
                packed = None
                for c in range(4):
                    part = roll_rows(state[v, node, q, c], tile_y * c - first)
                    packed = part if packed is None else jnp.where(row_i == c, part, packed)
                xs[side, v, q] = packed
        return carry

    def pack_y(q, carry):
        for v in range(5):
            for side, node, first in ((0, 0, 0), (1, 3, tile_y - 1)):
                for group in range(4 // tile_y):
                    packed = None
                    for c in range(tile_y):
                        part = roll_rows(state[v, q, node, group * tile_y + c], c - first)
                        packed = part if packed is None else jnp.where(row_j == c, part, packed)
                    ys[side, v, q, group] = packed
        return carry

    def early_node(group, sub):
        return (group * rows + sub) // 4, sub % 4

    def packed_rows(ref, slot, v, group):
        return ref[slot, v, group * (rows // 4) : (group + 1) * (rows // 4)].reshape(shape)

    def remote(src, dst, slot, device):
        return pltpu.make_async_remote_copy(
            src_ref=src,
            dst_ref=dst,
            send_sem=send_sem.at[slot],
            recv_sem=recv_sem.at[slot],
            device_id=device,
            device_id_type=MESH,
        )

    ring_end = jnp.logical_or(me_x == size_x - 1, me_y == size_y - 1)
    heralds = [
        remote(cs.at[2], cr.at[3], 9, (me_x, down_y)),
        remote(cs.at[3], cr.at[2], 10, (me_x, up_y)),
        remote(cs.at[0], cr.at[1], 7, (down_x, me_y)),
        remote(cs.at[1], cr.at[0], 8, (up_x, me_y)),
    ]

    def send_early():
        pl.semaphore_wait(barrier, len(partners))
        for slot, copy in ((3, heralds[1]), (1, heralds[3]), (2, heralds[0]), (0, heralds[2])):
            picks[slot].wait()
            copy.start()

    work_first = me_y == 0
    pl.when(jnp.logical_not(work_first))(send_early)
    for copy in small:
        copy.wait()

    def along(ref, start, total, tile, index):
        values = [ref[lax.rem(start + total + i, total)] for i in range(-1, tile + 1)]

        def pick(offset):
            vector = jnp.full(shape, values[1 + offset], jnp.float32)
            for i in range(1, tile):
                vector = jnp.where(index == i, values[1 + offset + i], vector)
            return vector

        return values, pick(-1), pick(0), pick(1)

    total_x, total_y = size_x * tile_x, size_y * tile_y
    wx_all, wx_p, wx, _ = along(wx_ref, me_x * tile_x, total_x, tile_x, row_i)
    wy_all, wy_p, wy, _ = along(wy_ref, me_y * tile_y, total_y, tile_y, row_j)
    sx_all, sx_p, sx, sx_n = along(sx_ref, me_x * tile_x, total_x, tile_x, row_i)
    sy_all, sy_p, sy, sy_n = along(sy_ref, me_y * tile_y, total_y, tile_y, row_j)
    nx_all = [wx_all[i] + time_step * (sx_all[i + 1] - sx_all[i]) for i in range(tile_x + 1)]
    ny_all = [wy_all[i] + time_step * (sy_all[i + 1] - sy_all[i]) for i in range(tile_y + 1)]
    wz = jnp.broadcast_to(wz_ref[...], shape)
    sz = jnp.broadcast_to(sz_ref[...], shape)
    sz_n = roll_lanes(sz, -1)
    nx, ny, nz = (
        wx + time_step * (sx_n - sx),
        wy + time_step * (sy_n - sy),
        wz + time_step * (sz_n - sz),
    )
    px, py = wx_p + time_step * (sx - sx_p), wy_p + time_step * (sy - sy_p)
    pz = roll_lanes(nz, 1)
    mass = nx * ny * nz
    ratio = wx * wy * wz / mass
    geo[RATIO] = ratio
    for d, (width, low, high) in enumerate(((wx, sx, sx_n), (wy, sy, sy_n), (wz, sz, sz_n))):
        for a in range(4):
            geo[SPEED + 4 * d + a] = low * float((1.0 - NODES[a]) / 2.0) + high * float(
                (1.0 + NODES[a]) / 2.0
            )
        for q, xi in enumerate((-5.0 / 6.0, 0.0, 5.0 / 6.0)):
            geo[INTER + 3 * d + q] = low * ((1.0 - xi) / 2.0) + high * ((1.0 + xi) / 2.0)
        geo[FACE + 2 * d] = low
        geo[FACE + 2 * d + 1] = high
        kappa = -time_step * ratio / width
        geo[SCALE + 2 * d] = kappa * float(1.0 / WEIGHTS[0])
        geo[SCALE + 2 * d + 1] = kappa * float(1.0 / WEIGHTS[1])

    entries = list_ref[...]
    count = entries.shape[-1]
    in_row = jnp.where(
        lax.broadcasted_iota(jnp.int32, (rows, count), 0) == entries // lanes, 1.0, 0.0
    )
    in_lane = jnp.where(
        lax.broadcasted_iota(jnp.int32, (lanes, count), 0) == entries % lanes, 1.0, 0.0
    )
    geo[MASK] = lax.dot_general(
        in_row, in_lane, (((1,), (1,)), ((), ())), preferred_element_type=jnp.float32
    )

    def prepare(a, carry):
        for b in range(4):
            for c in range(4):
                inverse, pressure, sound = primitives([state[v, a, b, c] for v in range(5)])
                inv_s[a, b, c] = inverse
                pres_s[a, b, c] = pressure
                sound_s[a, b, c] = sound
            zl[0, a, b] = roll_lanes(state[0, a, b, 3], 1)
            zl[3, a, b] = roll_lanes(state[3, a, b, 3] * inverse, 1)
            zl[5, a, b] = roll_lanes(sound, 1)
        return carry


    def interior(d, parts, first, second):
        def at(n):
            return ((n, first, second), (first, n, second), (first, second, n))[d]

        mask = geo[MASK] > 0.5
        sound = [sound_s[at(n)] for n in range(4)]
        normal = [state[(d + 1,) + at(n)] * inv_s[at(n)] for n in range(4)]
        weights = [
            wave_weights(normal[q], sound[q], normal[q + 1], sound[q + 1], geo[INTER + 3 * d + q])
            for q in range(3)
        ]
        relative = [normal[n] - geo[SPEED + 4 * d + n] for n in range(4)]
        if parts != DENSITY:
            pressure = [pres_s[at(n)] for n in range(4)]
            work = [pressure[n] * normal[n] for n in range(4)]
        if d == 2:
            behind = zl[3, first, second]
            star_left, star_right = wave_weights(
                behind, zl[5, first, second], normal[0], sound[0], geo[FACE + 4]
            )
            if parts != DENSITY:
                push = zl[6, first, second]
        for v in parts:
            value = [state[(v,) + at(n)] for n in range(4)]
            flux = [value[n] * relative[n] for n in range(4)]
            inner = [value[q] * weights[q][0] + value[q + 1] * weights[q][1] for q in range(3)]
            if d == 2:
                if v == 3:
                    rolled = zl[7, first, second]
                else:
                    rolled = zl[v, first, second]
                star = rolled * star_left + value[0] * star_right
            extra = pressure if v == d + 1 else work if v == 4 else None
            if extra is not None:
                flux = [flux[n] + extra[n] for n in range(4)]
                inner = [inner[q] + (extra[q] + extra[q + 1]) for q in range(3)]
            if d == 2:
                if v == 3:
                    star = star + (push + pressure[0])
                if v == 4:
                    star = star + (push * behind + work[0])
                zst[v, first, second] = star
            smooth = dg_fluxes(flux)
            chosen = [jnp.where(mask, inner[q], smooth[q]) for q in range(3)]
            head = chosen[0] - star if d == 2 else chosen[0]
            change = [head, chosen[1] - chosen[0], chosen[2] - chosen[1], -chosen[2]]
            for n in range(4):
                where = (v,) + at(n)
                scale = geo[SCALE + 2 * d + (0 if n in (0, 3) else 1)]
                if d == 0:
                    base = geo[RATIO] * value[n]
                else:
                    base = out[where]
                out[where] = base + scale * change[n]

    def lines(d, parts, width):
        def body(index, carry):
            for step in range(width):
                interior(d, parts, index // (4 // width), index % (4 // width) * width + step)
            return carry

        lax.fori_loop(0, 16 // width, body, 0)

    def above(v, a):
        for b in range(4):
            out[v, a, b, 3] = out[v, a, b, 3] + geo[SCALE + 4] * roll_lanes(zst[v, a, b], -1)


    def spots(d, q, c):
        return ((0, q, c), (3, q, c)) if d == 0 else ((q, 0, c), (q, 3, c))

    def inside(d, q, carry):
        shift = (tile_y, 1)[d]
        edge = (row_i, row_j)[d]
        for c in range(4):
            low, high = spots(d, q, c)
            left, right = wave_weights(
                roll_rows(state[(d + 1,) + high] * inv_s[high], shift),
                roll_rows(sound_s[high], shift),
                state[(d + 1,) + low] * inv_s[low],
                sound_s[low],
                geo[FACE + 2 * d],
            )
            star = roll_rows(state[(0,) + high], shift) * left + state[(0,) + low] * right
            star = jnp.where(edge > 0, star, 0.0)
            scale = geo[SCALE + 2 * d]
            out[(0,) + low] = out[(0,) + low] - scale * star
            out[(0,) + high] = out[(0,) + high] + scale * roll_rows(star, -shift)
        return carry


    def first_density():
        lax.fori_loop(0, 4, prepare, 0)
        for d in range(3):
            lines(d, DENSITY, 4)
        for a in range(4):
            above(0, a)
        for d in range(2):
            lax.fori_loop(0, 4, functools.partial(inside, d), 0)

    for a in (0, 3, 1, 2):
        loads[a].wait()

    @pl.when(work_first)
    def _():
        first_density()
        send_early()

    faces = [
        remote(lys.at[0], lyr.at[1], 2, (me_x, down_y)),
        remote(lys.at[1], lyr.at[0], 3, (me_x, up_y)),
        remote(lxs.at[0], lxr.at[1], 0, (down_x, me_y)),
        remote(lxs.at[1], lxr.at[0], 1, (up_x, me_y)),
    ]
    halves = 4 // tile_y
    groups = 4 * halves
    kept = groups - groups // tile_x
    free_y, free_x = row_i == last_i, row_j == last_j

    def group_of(ref, side, v, k):
        return ref[side, v, k // halves, k % halves]

    def squeeze_y(v, carry):
        for side in range(2):
            for k in range(kept):
                source, piece = kept + k // last_i, k % last_i
                moved = roll_rows(group_of(ys, side, v, source), rows - tile_y - piece * tile_y)
                lys[side, v, k] = jnp.where(free_y, moved, group_of(ys, side, v, k))
        return carry

    def squeeze_x(v, carry):
        for side in range(2):
            for k in range(4 // tile_y):
                moved = roll_rows(xs[side, v, tile_y * k + 1], last_j)
                lxs[side, v, k] = jnp.where(free_x, moved, xs[side, v, tile_y * k])
        return carry

    def send_y():
        lax.fori_loop(0, 4, pack_y, 0)
        lax.fori_loop(0, 5, squeeze_y, 0)
        faces[0].start()
        faces[1].start()

    held_back = jnp.logical_and(me_x == size_x - 1, me_y != size_y - 1)
    pl.when(jnp.logical_not(held_back))(send_y)
    lax.fori_loop(0, 4, pack_x, 0)
    lax.fori_loop(0, 5, squeeze_x, 0)
    faces[2].start()
    faces[3].start()

    pl.when(jnp.logical_not(work_first))(first_density)

    second = DERIV @ DERIV
    ends = (0, 3)

    def combine(coefficients, values):
        total = None
        for n in range(4):
            if values[n] is not None:
                term = float(coefficients[n]) * values[n]
                total = term if total is None else total + term
        return total

    def columns(density, factors, wanted):
        along_x = {
            (p, b, c): combine(DERIV[p], [density[a][b][c] for a in range(4)])
            for p in ends
            for b in range(4)
            for c in range(4)
            if b in ends or c in ends
        }
        along_y = {
            (a, q, c): combine(DERIV[q], [density[a][b][c] for b in range(4)])
            for q in ends
            for a in ends
            for c in range(4)
        }

        def corner(kind, p, q, r):
            if kind == 0:
                return combine(second[p], [density[a][q][r] for a in range(4)])
            if kind == 1:
                return combine(second[q], [density[p][b][r] for b in range(4)])
            if kind == 2:
                return combine(second[r], [density[p][q][c] for c in range(4)])
            if kind == 3:
                return combine(DERIV[q], [along_x[p, b, r] for b in range(4)])
            if kind == 4:
                return combine(DERIV[r], [along_x[p, q, c] for c in range(4)])
            return combine(DERIV[r], [along_y[p, q, c] for c in range(4)])

        found = []
        for kind in range(6):
            column = {}
            for p, q in wanted:
                low, high = corner(kind, p, q, 0), corner(kind, p, q, 3)
                column[p, q] = factors[kind] * low + roll_lanes(factors[kind] * high, 1)
            found.append(column)
        return found

    def pairs(jx, jy, jz):
        return (jx * jx, jy * jy, jz * jz, jx * jy, jx * jz, jy * jz)

    ix, iy, iz = 2.0 / nx, 2.0 / ny, 2.0 / nz
    factors = [mass * pair for pair in pairs(ix, iy, iz)]

    def up_y_shift(value):
        return jnp.where(row_j == 0, 0.0, roll_rows(value, 1))

    def up_x_shift(value):
        return jnp.where(row_i == 0, 0.0, roll_rows(value, tile_y))

    three = ((0, 3), (3, 0), (3, 3))
    density = [[[out[0, a, b, c] for c in range(4)] for b in range(4)] for a in range(4)]
    x_rim, y_rim = [None] * -(-6 // tile_x), [None] * -(-6 // tile_y)
    d_rim = None
    for kind, column in enumerate(columns(density, factors, three)):
        high_x = column[3, 0] + up_y_shift(column[3, 3])
        slot, place = kind // tile_x, kind % tile_x
        part = roll_rows(high_x, tile_y * place - (rows - tile_y))
        x_rim[slot] = part if place == 0 else jnp.where(row_i == place, part, x_rim[slot])
        rim = column[0, 3] + up_x_shift(column[3, 3])
        slot, place = kind // tile_y, kind % tile_y
        part = roll_rows(rim, place - last_j)
        y_rim[slot] = part if place == 0 else jnp.where(row_j == place, part, y_rim[slot])
        part = roll_rows(column[3, 3], kind - (rows - 1))
        d_rim = part if kind == 0 else jnp.where(row == kind, part, d_rim)
    for slot, value in enumerate(x_rim):
        rxs[slot] = value
    for slot, value in enumerate(y_rim):
        rys[slot] = value
    rds[...] = d_rim
    rims = [
        remote(rds, rdr, 6, (up_x, up_y)),
        remote(rys, ryr, 5, (me_x, up_y)),
        remote(rxs, rxr, 4, (up_x, me_y)),
    ]
    rims[0].start()
    pl.when(held_back)(send_y)

    def behind_rest(a, carry):
        for b in range(4):
            zl[1, a, b] = roll_lanes(state[1, a, b, 3], 1)
            zl[2, a, b] = roll_lanes(state[2, a, b, 3], 1)
            zl[7, a, b] = roll_lanes(state[3, a, b, 3], 1)
            zl[4, a, b] = roll_lanes(state[4, a, b, 3], 1)
            zl[6, a, b] = roll_lanes(pres_s[a, b, 3], 1)
        return carry

    def above_rest(a, carry):
        for v in REST:
            above(v, a)
        return carry

    def rest():
        lax.fori_loop(0, 4, behind_rest, 0)
        for d in range(3):
            lines(d, REST, 2)
        lax.fori_loop(0, 4, above_rest, 0)

    pl.when(jnp.logical_not(ring_end))(rest)

    row_up_x, row_low_x, row_under_x = 3, last_j, last_j - 1
    row_up_y, row_low_y, row_under_y = rows - 1, rows - tile_y, rows - tile_y - 1
    is_x = row <= row_up_x
    lower = jnp.logical_or(row == row_low_x, row == row_low_y)
    part_x = jnp.where(row == row_under_x, nx_all[0], jnp.where(row == row_low_x, nx_all[1], nx_all[tile_x]))
    part_y = jnp.where(row == row_under_y, ny_all[0], jnp.where(row == row_low_y, ny_all[1], ny_all[tile_y]))
    across = jnp.where(is_x, wy_all[tile_y], wx_all[tile_x])
    part = jnp.where(lower, 1.0, -1.0) * across * wz * float(time_step / WEIGHTS[3])
    part_factors = [part * pair for pair in pairs(2.0 / part_x, 2.0 / part_y, iz)]

    def face_stars(slot):
        d, side, place = early[slot]
        found = []
        for group in range(16 // rows):
            own = [packed_rows(cs, slot, v, group) for v in range(5)]
            other = [packed_rows(cr, slot, v, group) for v in range(5)]
            for v in range(5):
                theirs[slot, v, group] = other[v]
            low, high = (other, own) if side == 0 else (own, other)
            low_inverse, _, low_sound = primitives(low)
            high_inverse, _, high_sound = primitives(high)
            left, right = wave_weights(
                low[d + 1] * low_inverse,
                low_sound,
                high[d + 1] * high_inverse,
                high_sound,
                geo[FACE + 2 * d + side, place : place + 1],
            )
            found.append(low[0] * left + high[0] * right)
        return found

    def put(field, a, b, c, value):
        old = field[a][b][c]
        field[a][b][c] = value if old is None else old + value

    def part_field(d):
        field = [[[None] * 4 for b in range(4)] for a in range(4)]
        lows, ups = face_stars(2 * d), face_stars(2 * d + 1)
        up_row, low_row = (row_up_x, row_up_y)[d], (row_low_x, row_low_y)[d]
        under_row = (row_under_x, row_under_y)[d]
        for group in range(16 // rows):
            for sub in range(rows):
                q, c = early_node(group, sub)
                top, floor = ((3, q, c), (0, q, c)) if d == 0 else ((q, 3, c), (q, 0, c))
                value = jnp.where(row == up_row, roll_rows(ups[group], up_row - sub), 0.0)
                below = roll_rows(lows[group], under_row - sub)
                put(field, *top, jnp.where(row == under_row, below, value))
                low = roll_rows(lows[group], low_row - sub)
                put(field, *floor, jnp.where(row == low_row, low, 0.0))
        return field

    def y_part():
        heralds[2].wait()
        heralds[3].wait()
        y_rim = [None] * -(-6 // tile_y)
        for kind, column in enumerate(columns(part_field(0), part_factors, ((0, 3), (3, 3)))):
            near = jnp.where(row == last_j, column[0, 3] + roll_rows(column[3, 3], 1), 0.0)
            near = jnp.where(row == last_j + tile_y, roll_rows(column[3, 3], tile_y), near)
            rim = jnp.where(row == rows - 1, roll_rows(column[0, 3], rows - 1 - row_up_x), near)
            slot, place = kind // tile_y, kind % tile_y
            part = roll_rows(rim, place - last_j)
            y_rim[slot] = part if place == 0 else jnp.where(row_j == place, part, y_rim[slot])
        for slot, value in enumerate(y_rim):
            rys[slot] = rys[slot] + value
        rims[1].start()

    def x_part():
        heralds[0].wait()
        heralds[1].wait()
        x_rim = [None] * -(-6 // tile_x)
        for kind, column in enumerate(columns(part_field(1), part_factors, ((3, 0), (3, 3)))):
            high_x = column[3, 0] + roll_rows(column[3, 3], 1)
            slot, place = kind // tile_x, kind % tile_x
            part = roll_rows(high_x, tile_y * place - (rows - tile_y))
            x_rim[slot] = part if place == 0 else jnp.where(row_i == place, part, x_rim[slot])
        for slot, value in enumerate(x_rim):
            rxs[slot] = rxs[slot] + value
        rims[2].start()

    first_x = me_x == size_x - 1
    pl.when(first_x)(x_part)
    y_part()
    pl.when(jnp.logical_not(first_x))(x_part)
    pl.when(ring_end)(rest)

    def surface(d, q, carry):
        shift = (tile_y, 1)[d]
        edge, last = ((row_i, last_i), (row_j, last_j))[d]
        speed = geo[FACE + 2 * d]
        top_speed = geo[FACE + 2 * d + 1, rows - 1 : rows]
        scale = geo[SCALE + 2 * d]
        tops = []
        for group in range(1 if d == 0 else 4 // tile_y):
            if d == 0:
                own = [xs[1, v, q] for v in range(5)]
                other = [xr[1, v, q] for v in range(5)]
            else:
                own = [ys[1, v, q, group] for v in range(5)]
                other = [yr[1, v, q, group] for v in range(5)]
            own_inverse, own_pressure, own_sound = primitives(own)
            inverse, pressure, sound = primitives(other)
            tops.append(
                twice_flux(
                    own,
                    own_pressure,
                    own_sound,
                    own[d + 1] * own_inverse,
                    other,
                    pressure,
                    sound,
                    other[d + 1] * inverse,
                    d,
                    top_speed,
                )
            )
        for c in range(4):
            low, high = spots(d, q, c)
            own = [state[(v,) + low] for v in range(5)]
            other = []
            for v in range(5):
                if d == 0:
                    halo = roll_rows(xr[0, v, q], -tile_y * c)
                else:
                    halo = roll_rows(yr[0, v, q, c // tile_y], -(c % tile_y))
                moved = roll_rows(state[(v,) + high], shift)
                other.append(jnp.where(edge == 0, halo, moved))
            inverse, pressure, sound = primitives(other)
            star = twice_flux(
                other,
                pressure,
                sound,
                other[d + 1] * inverse,
                own,
                pres_s[low],
                sound_s[low],
                own[d + 1] * inv_s[low],
                d,
                speed,
            )
            for v in range(5):
                if d == 0:
                    top = roll_rows(tops[0][v], rows - tile_y - tile_y * c)
                else:
                    top = roll_rows(tops[c // tile_y][v], tile_y - 1 - c % tile_y)
                if v == 0:
                    down = jnp.where(edge == 0, star[v], 0.0)
                    up = jnp.where(edge == last, top, 0.0)
                    ph[d, q, c] = down
                else:
                    down = star[v]
                    up = jnp.where(edge == last, top, roll_rows(star[v], -shift))
                out[(v,) + low] = out[(v,) + low] - scale * down
                out[(v,) + high] = out[(v,) + high] + scale * up
        return carry

    def spread_x(v, carry):
        for side in range(2):
            for q in range(4):
                k = q // tile_y
                value = lxr[side, v, k]
                if q % tile_y:
                    value = roll_rows(value, -last_j)
                for c in range(4):
                    place, sub = tile_y * c + last_j, (q * 4 + c) % rows
                    first = roll_rows(theirs[side, v, q * 4 // rows], place - sub)
                    value = jnp.where(row == place, first, value)
                xr[side, v, q] = value
        return carry

    def spread_y(v, carry):
        for side in range(2):
            for k in range(groups):
                if k < kept:
                    value = lyr[side, v, k]
                else:
                    value = None
                    for piece in range(last_i):
                        part = lyr[side, v, (k - kept) * last_i + piece]
                        part = roll_rows(part, piece * tile_y - (rows - tile_y))
                        value = part if value is None else jnp.where(row_i == piece, part, value)
                first = theirs[2 + side, v, k // tile_x]
                first = roll_rows(first, rows - tile_y - (k % tile_x) * tile_y)
                yr[side, v, k // halves, k % halves] = jnp.where(free_y, first, value)
        return carry

    faces[2].wait()
    faces[3].wait()
    lax.fori_loop(0, 5, spread_x, 0)
    lax.fori_loop(0, 4, functools.partial(surface, 0), 0)
    faces[0].wait()
    faces[1].wait()
    lax.fori_loop(0, 5, spread_y, 0)
    lax.fori_loop(0, 4, functools.partial(surface, 1), 0)

    density = [[[out[0, a, b, c] for c in range(4)] for b in range(4)] for a in range(4)]
    for kind, column in enumerate(columns(density, factors, ((0, 0), (0, 3), (3, 0), (3, 3)))):
        low_x = column[0, 0] + up_y_shift(column[0, 3])
        high_x = column[3, 0] + up_y_shift(column[3, 3])
        hess_ref[kind] = low_x + up_x_shift(high_x)

    bottom = row_j == 0
    side_y, side_w = jnp.full(shape, ny_all[1], jnp.float32), jnp.full(shape, wy_all[1], jnp.float32)
    for n in range(1, tile_y):
        side_y = jnp.where(row_i == n, ny_all[1 + n], side_y)
        side_w = jnp.where(row_i == n, wy_all[1 + n], side_w)
    ghost_x = jnp.where(bottom, nx, nx_all[0])
    ghost_y = jnp.where(bottom, py, side_y)
    ghost = jnp.where(bottom, wx, side_w) * wz * float(-time_step / WEIGHTS[3])
    ghost_factors = [ghost * pair for pair in pairs(2.0 / ghost_x, 2.0 / ghost_y, iz)]
    field = [[[None] * 4 for b in range(4)] for a in range(4)]
    for n in range(4):
        for c in range(4):
            from_x = jnp.zeros(shape, jnp.float32)
            for m in range(tile_y):
                place = m * tile_y + last_j
                from_x = jnp.where(row == place, roll_rows(ph[0, n, c], place - m), from_x)
            put(field, 3, n, c, from_x)
            put(field, n, 3, c, ph[1, n, c])
    for kind, column in enumerate(columns(field, ghost_factors, three)):
        total = hess_ref[kind] + jnp.where(bottom, column[0, 3], 0.0)
        total = total + jnp.where(bottom, up_x_shift(column[3, 3]), 0.0)
        for m in range(tile_y):
            place = m * tile_y + last_j
            total = total + jnp.where(row == m, roll_rows(column[3, 0], m - place), 0.0)
            if m < last_j:
                total = total + jnp.where(row == m + 1, roll_rows(column[3, 3], m + 1 - place), 0.0)
        hess_ref[kind] = total

    inverse = 1.0 / ((nx + px) * (ny + py) * (nz + pz))
    for copy in rims:
        copy.wait()
    for kind in range(6):
        total = hess_ref[kind]
        from_x = roll_rows(rxr[kind // tile_x], -tile_y * (kind % tile_x))
        total = total + jnp.where(row_i == 0, from_x, 0.0)
        from_y = roll_rows(ryr[kind // tile_y], -(kind % tile_y))
        total = total + jnp.where(row_j == 0, from_y, 0.0)
        total = total + jnp.where(row == 0, roll_rows(rdr[...], -kind), 0.0)
        hess_ref[kind] = total * inverse


def emit(adv_ref, hess_ref, adv_out, hess_out, sem):
    copies = [
        pltpu.make_async_copy(adv_ref, adv_out, sem.at[0]),
        pltpu.make_async_copy(hess_ref, hess_out, sem.at[1]),
    ]
    for copy in copies:
        copy.start()
    for copy in copies:
        copy.wait()


def solution(mesh):
    sizes = (mesh.shape["gx"], mesh.shape["gy"])

    def local(conserved, troubled_list, widths_x, widths_y, widths_z, speed_x, speed_y, speed_z):
        tile_x, tile_y, column = conserved.shape[4:]
        rows = tile_x * tile_y
        f32 = jnp.float32
        vmem = pl.BlockSpec(memory_space=pltpu.VMEM)
        whole = pl.BlockSpec(memory_space=pl.ANY)
        full = (5, 4, 4, 4, rows, column)
        nodal = (4, 4, 4, rows, column)
        x_face = (2, 5, 4, rows, column)
        y_face = (2, 5, 4, 4 // tile_y, rows, column)
        groups = 4 * (4 // tile_y)
        x_late = (2, 5, 4 // tile_y, rows, column)
        y_late = (2, 5, groups - groups // tile_x, rows, column)
        herald = (4, 5, 16 // rows, rows, column)
        x_rim = (-(-6 // tile_x), rows, column)
        y_rim = (-(-6 // tile_y), rows, column)
        advanced, hessian = pl.pallas_call(
            functools.partial(kernel, tile_x, tile_y, sizes),
            out_shape=(
                pltpu.VMEM(full, f32),
                pltpu.VMEM((6, rows, column), f32),
            ),
            in_specs=[whole] * 9,
            out_specs=(vmem, vmem),
            scratch_shapes=[
                pltpu.VMEM((1, troubled_list.shape[0]), jnp.int32),
                pltpu.SMEM(widths_x.shape, f32),
                pltpu.SMEM(widths_y.shape, f32),
                pltpu.VMEM((1, column), f32),
                pltpu.SMEM(speed_x.shape, f32),
                pltpu.SMEM(speed_y.shape, f32),
                pltpu.VMEM((1, column), f32),
                pltpu.VMEM(full, f32),
                pltpu.VMEM(nodal, f32),
                pltpu.VMEM(nodal, f32),
                pltpu.VMEM(nodal, f32),
                pltpu.VMEM((8, 4, 4, rows, column), f32),
                pltpu.VMEM((5, 4, 4, rows, column), f32),
                pltpu.VMEM((2, 4, 4, rows, column), f32),
                pltpu.VMEM((GEO, rows, column), f32),
                pltpu.VMEM((4, 5, 4, 4, 1, column), f32),
                pltpu.VMEM((4, 5, 4, 4, 1, column), f32),
                pltpu.VMEM(herald, f32),
                pltpu.VMEM(x_late, f32),
                pltpu.VMEM(x_late, f32),
                pltpu.VMEM(y_late, f32),
                pltpu.VMEM(y_late, f32),
                pltpu.VMEM(x_face, f32),
                pltpu.VMEM(x_face, f32),
                pltpu.VMEM(y_face, f32),
                pltpu.VMEM(y_face, f32),
                pltpu.VMEM(x_rim, f32),
                pltpu.VMEM(x_rim, f32),
                pltpu.VMEM(y_rim, f32),
                pltpu.VMEM(y_rim, f32),
                pltpu.VMEM((rows, column), f32),
                pltpu.VMEM((rows, column), f32),
                pltpu.SemaphoreType.DMA((15,)),
                pltpu.SemaphoreType.DMA((11,)),
                pltpu.SemaphoreType.DMA((11,)),
            ],
            compiler_params=pltpu.CompilerParams(collective_id=0, has_side_effects=True),
        )(
            conserved.reshape(full),
            conserved.reshape(full[:5] + (1, column)),
            troubled_list.reshape(1, -1),
            widths_x,
            widths_y,
            widths_z.reshape(1, -1),
            speed_x,
            speed_y,
            speed_z.reshape(1, -1),
        )
        advanced = pltpu.with_memory_space_constraint(advanced, pltpu.VMEM)
        hessian = pltpu.with_memory_space_constraint(hessian, pltpu.VMEM)
        advanced, hessian = pl.pallas_call(
            emit,
            out_shape=(
                jax.ShapeDtypeStruct(full, f32),
                jax.ShapeDtypeStruct((6, rows, column), f32),
            ),
            in_specs=[whole, whole],
            out_specs=(whole, whole),
            scratch_shapes=[pltpu.SemaphoreType.DMA((2,))],
        )(advanced, hessian)
        return advanced.reshape(conserved.shape), hessian.reshape(6, tile_x, tile_y, column)

    in_specs = (
        P(None, None, None, None, "gx", "gy", None),
        P(("gx", "gy")),
        P(),
        P(),
        P(),
        P(),
        P(),
        P(),
    )
    out_specs = (P(None, None, None, None, "gx", "gy", None), P(None, "gx", "gy", None))
    return jax.shard_map(local, mesh=mesh, in_specs=in_specs, out_specs=out_specs, check_vma=False)
```

```python
import functools

import jax
import jax.numpy as jnp
import numpy as np
from jax import lax
from jax.experimental import pallas as pl
from jax.experimental.pallas import tpu as pltpu
from jax.sharding import PartitionSpec as P

MESH = pl.DeviceIdType.MESH
time_step = 0.05
gamma_ratio = 1.4


def lgl_tables():
    nodes = np.array([-1.0, -1.0 / np.sqrt(5.0), 1.0 / np.sqrt(5.0), 1.0])
    weights = np.array([1.0 / 6.0, 5.0 / 6.0, 5.0 / 6.0, 1.0 / 6.0])
    barycentric = np.ones(4)
    for row_a in range(4):
        for row_b in range(4):
            if row_a != row_b:
                barycentric[row_a] = barycentric[row_a] / (nodes[row_a] - nodes[row_b])
    deriv = np.zeros((4, 4))
    for row_a in range(4):
        for row_b in range(4):
            if row_a != row_b:
                deriv[row_a, row_b] = (
                    barycentric[row_b] / barycentric[row_a] / (nodes[row_a] - nodes[row_b])
                )
    for row_a in range(4):
        deriv[row_a, row_a] = -np.sum(deriv[row_a])
    return (nodes, weights, deriv)


NODES, WEIGHTS, DERIV = lgl_tables()
SPEED, INTER, SCALE, FACE = 0, 12, 21, 27
RATIO, MASK, GEO = 33, 34, 35
ALL, DENSITY, REST = (0, 1, 2, 3, 4), (0,), (1, 2, 3, 4)


def primitives(state):
    inverse = 1.0 / state[0]
    square = state[1] * state[1] + state[2] * state[2] + state[3] * state[3]
    pressure = (gamma_ratio - 1.0) * (state[4] - 0.5 * square * inverse)
    ratio = gamma_ratio * pressure * inverse
    return inverse, pressure, ratio * lax.rsqrt(ratio)


def twice_flux(low, p_low, c_low, u_low, high, p_high, c_high, u_high, direction, speed):
    rel_low = u_low - speed
    rel_high = u_high - speed
    fastest = jnp.maximum(jnp.abs(rel_low) + c_low, jnp.abs(rel_high) + c_high)
    left = rel_low + fastest
    right = rel_high - fastest
    flux = [low[v] * left + high[v] * right for v in range(5)]
    flux[direction + 1] = flux[direction + 1] + (p_low + p_high)
    flux[4] = flux[4] + (p_low * u_low + p_high * u_high)
    return flux


def dg_table():
    lifted = DERIV.copy()
    lifted[0, 0] += 1.0 / WEIGHTS[0]
    lifted[3, 3] -= 1.0 / WEIGHTS[3]
    return np.cumsum(2.0 * WEIGHTS[:, None] * lifted, axis=0)


SUBCELL = dg_table()


def dg_fluxes(values):
    outer, inner = values[0] + values[3], values[1] + values[2]
    step = inner - outer
    even = outer + float(0.5 * (SUBCELL[0, 1] + SUBCELL[2, 1])) * step
    middle = outer + float(SUBCELL[1, 1]) * step
    odd = float(0.5 * (SUBCELL[0, 0] - SUBCELL[2, 0])) * (values[0] - values[3])
    odd = odd + float(0.5 * (SUBCELL[0, 1] - SUBCELL[2, 1])) * (values[1] - values[2])
    return even + odd, middle, even - odd


def wave_weights(u_low, c_low, u_high, c_high, speed):
    rel_low = u_low - speed
    rel_high = u_high - speed
    fastest = jnp.maximum(jnp.abs(rel_low) + c_low, jnp.abs(rel_high) + c_high)
    return rel_low + fastest, rel_high - fastest


def kernel(
    tile_x,
    tile_y,
    sizes,
    cons_hbm,
    rows_hbm,
    list_hbm,
    wx_hbm,
    wy_hbm,
    wz_hbm,
    sx_hbm,
    sy_hbm,
    sz_hbm,
    out,
    hess_ref,
    list_ref,
    wx_ref,
    wy_ref,
    wz_ref,
    sx_ref,
    sy_ref,
    sz_ref,
    state,
    inv_s,
    pres_s,
    sound_s,
    zl,
    zst,
    ph,
    geo,
    cs,
    cr,
    theirs,
    lxs,
    lxr,
    lys,
    lyr,
    xs,
    xr,
    ys,
    yr,
    rxs,
    rxr,
    rys,
    ryr,
    rds,
    rdr,
    io_sem,
    send_sem,
    recv_sem,
):
    size_x, size_y = sizes
    rows = tile_x * tile_y
    lanes = state.shape[-1]
    me_x, me_y = lax.axis_index("gx"), lax.axis_index("gy")
    up_x, down_x = lax.rem(me_x + 1, size_x), lax.rem(me_x + size_x - 1, size_x)
    up_y, down_y = lax.rem(me_y + 1, size_y), lax.rem(me_y + size_y - 1, size_y)

    barrier = pltpu.get_barrier_semaphore()
    partners = ((me_x, down_y), (me_x, up_y), (down_x, me_y), (up_x, me_y), (down_x, down_y))
    for partner in partners:
        pl.semaphore_signal(barrier, inc=1, device_id=partner, device_id_type=MESH)
    small = [
        pltpu.make_async_copy(src, dst, io_sem.at[4 + n])
        for n, (src, dst) in enumerate(
            (
                (wx_hbm, wx_ref),
                (wy_hbm, wy_ref),
                (sx_hbm, sx_ref),
                (sy_hbm, sy_ref),
                (wz_hbm, wz_ref),
                (sz_hbm, sz_ref),
                (list_hbm, list_ref),
            )
        )
    ]
    last_i, last_j = tile_x - 1, tile_y - 1
    early = ((0, 0, last_j), (0, 1, rows - 1), (1, 0, rows - tile_y), (1, 1, rows - 1))

    picks = []
    for slot, (d, side, place) in enumerate(early):
        view = rows_hbm.at[:, 3 * side, :, :, place] if d == 0 else rows_hbm.at[:, :, 3 * side, :, place]
        picks.append(pltpu.make_async_copy(view, cs.at[slot], io_sem.at[11 + slot]))
    for slot in (3, 1):
        picks[slot].start()
    loads = [pltpu.make_async_copy(cons_hbm.at[:, a], state.at[:, a], io_sem.at[a]) for a in range(4)]
    for a in (0, 3, 1, 2):
        loads[a].start()
    for slot in (2, 0):
        picks[slot].start()
    for copy in small:
        copy.start()

    shape = (rows, lanes)
    row = lax.broadcasted_iota(jnp.int32, shape, 0)
    row_i, row_j = row // tile_y, row % tile_y

    def roll_rows(value, shift):
        shift = shift % rows
        return value if shift == 0 else pltpu.roll(value, shift, 0)

    def roll_lanes(value, shift):
        return pltpu.roll(value, shift % lanes, 1)

    def pack_x(q, carry):
        for v in range(5):
            for side, node, first in ((0, 0, 0), (1, 3, rows - tile_y)):
                packed = None
                for c in range(4):
                    part = roll_rows(state[v, node, q, c], tile_y * c - first)
                    packed = part if packed is None else jnp.where(row_i == c, part, packed)
                xs[side, v, q] = packed
        return carry

    def pack_y(q, carry):
        for v in range(5):
            for side, node, first in ((0, 0, 0), (1, 3, tile_y - 1)):
                for group in range(4 // tile_y):
                    packed = None
                    for c in range(tile_y):
                        part = roll_rows(state[v, q, node, group * tile_y + c], c - first)
                        packed = part if packed is None else jnp.where(row_j == c, part, packed)
                    ys[side, v, q, group] = packed
        return carry

    def early_node(group, sub):
        return (group * rows + sub) // 4, sub % 4

    def packed_rows(ref, slot, v, group):
        return ref[slot, v, group * (rows // 4) : (group + 1) * (rows // 4)].reshape(shape)

    def remote(src, dst, slot, device):
        return pltpu.make_async_remote_copy(
            src_ref=src,
            dst_ref=dst,
            send_sem=send_sem.at[slot],
            recv_sem=recv_sem.at[slot],
            device_id=device,
            device_id_type=MESH,
        )

    ring_end = jnp.logical_or(me_x == size_x - 1, me_y == size_y - 1)
    heralds = [
        remote(cs.at[2], cr.at[3], 9, (me_x, down_y)),
        remote(cs.at[3], cr.at[2], 10, (me_x, up_y)),
        remote(cs.at[0], cr.at[1], 7, (down_x, me_y)),
        remote(cs.at[1], cr.at[0], 8, (up_x, me_y)),
    ]

    def send_early():
        pl.semaphore_wait(barrier, len(partners))
        for slot, copy in ((3, heralds[1]), (1, heralds[3]), (2, heralds[0]), (0, heralds[2])):
            picks[slot].wait()
            copy.start()

    work_first = jnp.logical_and(me_y == 0, me_x != size_x - 1)
    pack_first = jnp.logical_and(me_y == size_y - 1, me_x != size_x - 1)
    pl.when(jnp.logical_not(jnp.logical_or(work_first, pack_first)))(send_early)
    for copy in small:
        copy.wait()

    def along(ref, start, total, tile, index):
        values = [ref[lax.rem(start + total + i, total)] for i in range(-1, tile + 1)]

        def pick(offset):
            vector = jnp.full(shape, values[1 + offset], jnp.float32)
            for i in range(1, tile):
                vector = jnp.where(index == i, values[1 + offset + i], vector)
            return vector

        return values, pick(-1), pick(0), pick(1)

    total_x, total_y = size_x * tile_x, size_y * tile_y
    wx_all, wx_p, wx, _ = along(wx_ref, me_x * tile_x, total_x, tile_x, row_i)
    wy_all, wy_p, wy, _ = along(wy_ref, me_y * tile_y, total_y, tile_y, row_j)
    sx_all, sx_p, sx, sx_n = along(sx_ref, me_x * tile_x, total_x, tile_x, row_i)
    sy_all, sy_p, sy, sy_n = along(sy_ref, me_y * tile_y, total_y, tile_y, row_j)
    nx_all = [wx_all[i] + time_step * (sx_all[i + 1] - sx_all[i]) for i in range(tile_x + 1)]
    ny_all = [wy_all[i] + time_step * (sy_all[i + 1] - sy_all[i]) for i in range(tile_y + 1)]
    wz = jnp.broadcast_to(wz_ref[...], shape)
    sz = jnp.broadcast_to(sz_ref[...], shape)
    sz_n = roll_lanes(sz, -1)
    nx, ny, nz = (
        wx + time_step * (sx_n - sx),
        wy + time_step * (sy_n - sy),
        wz + time_step * (sz_n - sz),
    )
    px, py = wx_p + time_step * (sx - sx_p), wy_p + time_step * (sy - sy_p)
    pz = roll_lanes(nz, 1)
    mass = nx * ny * nz
    ratio = wx * wy * wz / mass
    geo[RATIO] = ratio
    for d, (width, low, high) in enumerate(((wx, sx, sx_n), (wy, sy, sy_n), (wz, sz, sz_n))):
        for a in range(4):
            geo[SPEED + 4 * d + a] = low * float((1.0 - NODES[a]) / 2.0) + high * float(
                (1.0 + NODES[a]) / 2.0
            )
        for q, xi in enumerate((-5.0 / 6.0, 0.0, 5.0 / 6.0)):
            geo[INTER + 3 * d + q] = low * ((1.0 - xi) / 2.0) + high * ((1.0 + xi) / 2.0)
        geo[FACE + 2 * d] = low
        geo[FACE + 2 * d + 1] = high
        kappa = -time_step * ratio / width
        geo[SCALE + 2 * d] = kappa * float(1.0 / WEIGHTS[0])
        geo[SCALE + 2 * d + 1] = kappa * float(1.0 / WEIGHTS[1])

    entries = list_ref[...]
    count = entries.shape[-1]
    in_row = jnp.where(
        lax.broadcasted_iota(jnp.int32, (rows, count), 0) == entries // lanes, 1.0, 0.0
    )
    in_lane = jnp.where(
        lax.broadcasted_iota(jnp.int32, (lanes, count), 0) == entries % lanes, 1.0, 0.0
    )
    geo[MASK] = lax.dot_general(
        in_row, in_lane, (((1,), (1,)), ((), ())), preferred_element_type=jnp.float32
    )

    def prepare(a, carry):
        for b in range(4):
            for c in range(4):
                inverse, pressure, sound = primitives([state[v, a, b, c] for v in range(5)])
                inv_s[a, b, c] = inverse
                pres_s[a, b, c] = pressure
                sound_s[a, b, c] = sound
            zl[0, a, b] = roll_lanes(state[0, a, b, 3], 1)
            zl[3, a, b] = roll_lanes(state[3, a, b, 3] * inverse, 1)
            zl[5, a, b] = roll_lanes(sound, 1)
        return carry


    def interior(d, parts, first, second):
        def at(n):
            return ((n, first, second), (first, n, second), (first, second, n))[d]

        mask = geo[MASK] > 0.5
        sound = [sound_s[at(n)] for n in range(4)]
        normal = [state[(d + 1,) + at(n)] * inv_s[at(n)] for n in range(4)]
        weights = [
            wave_weights(normal[q], sound[q], normal[q + 1], sound[q + 1], geo[INTER + 3 * d + q])
            for q in range(3)
        ]
        relative = [normal[n] - geo[SPEED + 4 * d + n] for n in range(4)]
        if parts != DENSITY:
            pressure = [pres_s[at(n)] for n in range(4)]
            work = [pressure[n] * normal[n] for n in range(4)]
        if d == 2:
            behind = zl[3, first, second]
            star_left, star_right = wave_weights(
                behind, zl[5, first, second], normal[0], sound[0], geo[FACE + 4]
            )
            if parts != DENSITY:
                push = zl[6, first, second]
        for v in parts:
            value = [state[(v,) + at(n)] for n in range(4)]
            flux = [value[n] * relative[n] for n in range(4)]
            inner = [value[q] * weights[q][0] + value[q + 1] * weights[q][1] for q in range(3)]
            if d == 2:
                if v == 3:
                    rolled = zl[7, first, second]
                else:
                    rolled = zl[v, first, second]
                star = rolled * star_left + value[0] * star_right
            extra = pressure if v == d + 1 else work if v == 4 else None
            if extra is not None:
                flux = [flux[n] + extra[n] for n in range(4)]
                inner = [inner[q] + (extra[q] + extra[q + 1]) for q in range(3)]
            if d == 2:
                if v == 3:
                    star = star + (push + pressure[0])
                if v == 4:
                    star = star + (push * behind + work[0])
                zst[v, first, second] = star
            smooth = dg_fluxes(flux)
            chosen = [jnp.where(mask, inner[q], smooth[q]) for q in range(3)]
            head = chosen[0] - star if d == 2 else chosen[0]
            change = [head, chosen[1] - chosen[0], chosen[2] - chosen[1], -chosen[2]]
            for n in range(4):
                where = (v,) + at(n)
                scale = geo[SCALE + 2 * d + (0 if n in (0, 3) else 1)]
                if d == 0:
                    base = geo[RATIO] * value[n]
                else:
                    base = out[where]
                out[where] = base + scale * change[n]

    def lines(d, parts, width):
        def body(index, carry):
            for step in range(width):
                interior(d, parts, index // (4 // width), index % (4 // width) * width + step)
            return carry

        lax.fori_loop(0, 16 // width, body, 0)

    def above(v, a):
        for b in range(4):
            out[v, a, b, 3] = out[v, a, b, 3] + geo[SCALE + 4] * roll_lanes(zst[v, a, b], -1)


    def spots(d, q, c):
        return ((0, q, c), (3, q, c)) if d == 0 else ((q, 0, c), (q, 3, c))

    def inside(d, q, carry):
        shift = (tile_y, 1)[d]
        edge = (row_i, row_j)[d]
        for c in range(4):
            low, high = spots(d, q, c)
            left, right = wave_weights(
                roll_rows(state[(d + 1,) + high] * inv_s[high], shift),
                roll_rows(sound_s[high], shift),
                state[(d + 1,) + low] * inv_s[low],
                sound_s[low],
                geo[FACE + 2 * d],
            )
            star = roll_rows(state[(0,) + high], shift) * left + state[(0,) + low] * right
            star = jnp.where(edge > 0, star, 0.0)
            scale = geo[SCALE + 2 * d]
            out[(0,) + low] = out[(0,) + low] - scale * star
            out[(0,) + high] = out[(0,) + high] + scale * roll_rows(star, -shift)
        return carry


    def first_density():
        lax.fori_loop(0, 4, prepare, 0)
        for d in range(3):
            lines(d, DENSITY, 4)
        for a in range(4):
            above(0, a)
        for d in range(2):
            lax.fori_loop(0, 4, functools.partial(inside, d), 0)

    for a in (0, 3, 1, 2):
        loads[a].wait()

    faces = [
        remote(lys.at[0], lyr.at[1], 2, (me_x, down_y)),
        remote(lys.at[1], lyr.at[0], 3, (me_x, up_y)),
        remote(lxs.at[0], lxr.at[1], 0, (down_x, me_y)),
        remote(lxs.at[1], lxr.at[0], 1, (up_x, me_y)),
    ]
    halves = 4 // tile_y
    groups = 4 * halves
    kept = groups - groups // tile_x
    free_y, free_x = row_i == last_i, row_j == last_j

    def group_of(ref, side, v, k):
        return ref[side, v, k // halves, k % halves]

    def squeeze_y(v, carry):
        for side in range(2):
            for k in range(kept):
                source, piece = kept + k // last_i, k % last_i
                moved = roll_rows(group_of(ys, side, v, source), rows - tile_y - piece * tile_y)
                lys[side, v, k] = jnp.where(free_y, moved, group_of(ys, side, v, k))
        return carry

    def squeeze_x(v, carry):
        for side in range(2):
            for k in range(4 // tile_y):
                moved = roll_rows(xs[side, v, tile_y * k + 1], last_j)
                lxs[side, v, k] = jnp.where(free_x, moved, xs[side, v, tile_y * k])
        return carry

    pl.when(work_first)(first_density)
    lax.fori_loop(0, 4, pack_y, 0)
    lax.fori_loop(0, 5, squeeze_y, 0)
    lax.fori_loop(0, 4, pack_x, 0)
    lax.fori_loop(0, 5, squeeze_x, 0)
    pl.when(jnp.logical_or(work_first, pack_first))(send_early)

    def send_y():
        faces[0].start()
        faces[1].start()

    held_back = jnp.logical_and(me_x == size_x - 1, me_y != size_y - 1)
    pl.when(jnp.logical_not(held_back))(send_y)
    faces[2].start()
    faces[3].start()

    pl.when(jnp.logical_not(work_first))(first_density)

    second = DERIV @ DERIV
    ends = (0, 3)

    def combine(coefficients, values):
        total = None
        for n in range(4):
            if values[n] is not None:
                term = float(coefficients[n]) * values[n]
                total = term if total is None else total + term
        return total

    def columns(density, factors, wanted):
        along_x = {
            (p, b, c): combine(DERIV[p], [density[a][b][c] for a in range(4)])
            for p in ends
            for b in range(4)
            for c in range(4)
            if b in ends or c in ends
        }
        along_y = {
            (a, q, c): combine(DERIV[q], [density[a][b][c] for b in range(4)])
            for q in ends
            for a in ends
            for c in range(4)
        }

        def corner(kind, p, q, r):
            if kind == 0:
                return combine(second[p], [density[a][q][r] for a in range(4)])
            if kind == 1:
                return combine(second[q], [density[p][b][r] for b in range(4)])
            if kind == 2:
                return combine(second[r], [density[p][q][c] for c in range(4)])
            if kind == 3:
                return combine(DERIV[q], [along_x[p, b, r] for b in range(4)])
            if kind == 4:
                return combine(DERIV[r], [along_x[p, q, c] for c in range(4)])
            return combine(DERIV[r], [along_y[p, q, c] for c in range(4)])

        found = []
        for kind in range(6):
            column = {}
            for p, q in wanted:
                low, high = corner(kind, p, q, 0), corner(kind, p, q, 3)
                column[p, q] = factors[kind] * low + roll_lanes(factors[kind] * high, 1)
            found.append(column)
        return found

    def pairs(jx, jy, jz):
        return (jx * jx, jy * jy, jz * jz, jx * jy, jx * jz, jy * jz)

    ix, iy, iz = 2.0 / nx, 2.0 / ny, 2.0 / nz
    factors = [mass * pair for pair in pairs(ix, iy, iz)]

    def up_y_shift(value):
        return jnp.where(row_j == 0, 0.0, roll_rows(value, 1))

    def up_x_shift(value):
        return jnp.where(row_i == 0, 0.0, roll_rows(value, tile_y))

    three = ((0, 3), (3, 0), (3, 3))
    density = [[[out[0, a, b, c] for c in range(4)] for b in range(4)] for a in range(4)]
    x_rim, y_rim = [None] * -(-6 // tile_x), [None] * -(-6 // tile_y)
    d_rim = None
    for kind, column in enumerate(columns(density, factors, three)):
        high_x = column[3, 0] + up_y_shift(column[3, 3])
        slot, place = kind // tile_x, kind % tile_x
        part = roll_rows(high_x, tile_y * place - (rows - tile_y))
        x_rim[slot] = part if place == 0 else jnp.where(row_i == place, part, x_rim[slot])
        rim = column[0, 3] + up_x_shift(column[3, 3])
        slot, place = kind // tile_y, kind % tile_y
        part = roll_rows(rim, place - last_j)
        y_rim[slot] = part if place == 0 else jnp.where(row_j == place, part, y_rim[slot])
        part = roll_rows(column[3, 3], kind - (rows - 1))
        d_rim = part if kind == 0 else jnp.where(row == kind, part, d_rim)
    for slot, value in enumerate(x_rim):
        rxs[slot] = value
    for slot, value in enumerate(y_rim):
        rys[slot] = value
    rds[...] = d_rim
    rims = [
        remote(rds, rdr, 6, (up_x, up_y)),
        remote(rys, ryr, 5, (me_x, up_y)),
        remote(rxs, rxr, 4, (up_x, me_y)),
    ]
    rims[0].start()
    pl.when(held_back)(send_y)

    def behind_rest(a, carry):
        for b in range(4):
            zl[1, a, b] = roll_lanes(state[1, a, b, 3], 1)
            zl[2, a, b] = roll_lanes(state[2, a, b, 3], 1)
            zl[7, a, b] = roll_lanes(state[3, a, b, 3], 1)
            zl[4, a, b] = roll_lanes(state[4, a, b, 3], 1)
            zl[6, a, b] = roll_lanes(pres_s[a, b, 3], 1)
        return carry

    def above_rest(a, carry):
        for v in REST:
            above(v, a)
        return carry

    def rest():
        lax.fori_loop(0, 4, behind_rest, 0)
        for d in range(3):
            lines(d, REST, 2)
        lax.fori_loop(0, 4, above_rest, 0)

    pl.when(jnp.logical_not(ring_end))(rest)

    row_up_x, row_low_x, row_under_x = 3, last_j, last_j - 1
    row_up_y, row_low_y, row_under_y = rows - 1, rows - tile_y, rows - tile_y - 1
    is_x = row <= row_up_x
    lower = jnp.logical_or(row == row_low_x, row == row_low_y)
    part_x = jnp.where(row == row_under_x, nx_all[0], jnp.where(row == row_low_x, nx_all[1], nx_all[tile_x]))
    part_y = jnp.where(row == row_under_y, ny_all[0], jnp.where(row == row_low_y, ny_all[1], ny_all[tile_y]))
    across = jnp.where(is_x, wy_all[tile_y], wx_all[tile_x])
    part = jnp.where(lower, 1.0, -1.0) * across * wz * float(time_step / WEIGHTS[3])
    part_factors = [part * pair for pair in pairs(2.0 / part_x, 2.0 / part_y, iz)]

    def waves(ref, slot, group, keep):
        d = early[slot][0]
        fields = [packed_rows(ref, slot, v, group) for v in range(5)]
        if keep:
            for v in range(5):
                theirs[slot, v, group] = fields[v]
        inverse, _, sound = primitives(fields)
        return fields[0], fields[d + 1] * inverse, sound

    def own_waves(d):
        return [[waves(cs, 2 * d + side, group, False) for group in range(16 // rows)] for side in range(2)]

    def face_stars(slot, mine):
        d, side, place = early[slot]
        found = []
        for group in range(16 // rows):
            own, other = mine[side][group], waves(cr, slot, group, True)
            low, high = (other, own) if side == 0 else (own, other)
            speed = geo[FACE + 2 * d + side, place : place + 1]
            left, right = wave_weights(low[1], low[2], high[1], high[2], speed)
            found.append(low[0] * left + high[0] * right)
        return found

    def put(field, a, b, c, value):
        old = field[a][b][c]
        field[a][b][c] = value if old is None else old + value

    def part_field(d, mine):
        field = [[[None] * 4 for b in range(4)] for a in range(4)]
        lows, ups = face_stars(2 * d, mine), face_stars(2 * d + 1, mine)
        up_row, low_row = (row_up_x, row_up_y)[d], (row_low_x, row_low_y)[d]
        under_row = (row_under_x, row_under_y)[d]
        for group in range(16 // rows):
            for sub in range(rows):
                q, c = early_node(group, sub)
                top, floor = ((3, q, c), (0, q, c)) if d == 0 else ((q, 3, c), (q, 0, c))
                value = jnp.where(row == up_row, roll_rows(ups[group], up_row - sub), 0.0)
                below = roll_rows(lows[group], under_row - sub)
                put(field, *top, jnp.where(row == under_row, below, value))
                low = roll_rows(lows[group], low_row - sub)
                put(field, *floor, jnp.where(row == low_row, low, 0.0))
        return field

    def y_part():
        mine = own_waves(0)
        heralds[2].wait()
        heralds[3].wait()
        y_rim = [None] * -(-6 // tile_y)
        for kind, column in enumerate(columns(part_field(0, mine), part_factors, ((0, 3), (3, 3)))):
            near = jnp.where(row == last_j, column[0, 3] + roll_rows(column[3, 3], 1), 0.0)
            near = jnp.where(row == last_j + tile_y, roll_rows(column[3, 3], tile_y), near)
            rim = jnp.where(row == rows - 1, roll_rows(column[0, 3], rows - 1 - row_up_x), near)
            slot, place = kind // tile_y, kind % tile_y
            part = roll_rows(rim, place - last_j)
            y_rim[slot] = part if place == 0 else jnp.where(row_j == place, part, y_rim[slot])
        for slot, value in enumerate(y_rim):
            rys[slot] = rys[slot] + value
        rims[1].start()

    def x_part():
        mine = own_waves(1)
        heralds[0].wait()
        heralds[1].wait()
        x_rim = [None] * -(-6 // tile_x)
        for kind, column in enumerate(columns(part_field(1, mine), part_factors, ((3, 0), (3, 3)))):
            high_x = column[3, 0] + roll_rows(column[3, 3], 1)
            slot, place = kind // tile_x, kind % tile_x
            part = roll_rows(high_x, tile_y * place - (rows - tile_y))
            x_rim[slot] = part if place == 0 else jnp.where(row_i == place, part, x_rim[slot])
        for slot, value in enumerate(x_rim):
            rxs[slot] = rxs[slot] + value
        rims[2].start()

    first_x = me_x == size_x - 1
    pl.when(first_x)(x_part)
    y_part()
    pl.when(jnp.logical_not(first_x))(x_part)
    pl.when(ring_end)(rest)

    def surface(d, q, carry):
        shift = (tile_y, 1)[d]
        edge, last = ((row_i, last_i), (row_j, last_j))[d]
        speed = geo[FACE + 2 * d]
        top_speed = geo[FACE + 2 * d + 1, rows - 1 : rows]
        scale = geo[SCALE + 2 * d]
        tops = []
        for group in range(1 if d == 0 else 4 // tile_y):
            if d == 0:
                own = [xs[1, v, q] for v in range(5)]
                other = [xr[1, v, q] for v in range(5)]
            else:
                own = [ys[1, v, q, group] for v in range(5)]
                other = [yr[1, v, q, group] for v in range(5)]
            own_inverse, own_pressure, own_sound = primitives(own)
            inverse, pressure, sound = primitives(other)
            tops.append(
                twice_flux(
                    own,
                    own_pressure,
                    own_sound,
                    own[d + 1] * own_inverse,
                    other,
                    pressure,
                    sound,
                    other[d + 1] * inverse,
                    d,
                    top_speed,
                )
            )
        for c in range(4):
            low, high = spots(d, q, c)
            own = [state[(v,) + low] for v in range(5)]
            other = []
            for v in range(5):
                if d == 0:
                    halo = roll_rows(xr[0, v, q], -tile_y * c)
                else:
                    halo = roll_rows(yr[0, v, q, c // tile_y], -(c % tile_y))
                moved = roll_rows(state[(v,) + high], shift)
                other.append(jnp.where(edge == 0, halo, moved))
            inverse, pressure, sound = primitives(other)
            star = twice_flux(
                other,
                pressure,
                sound,
                other[d + 1] * inverse,
                own,
                pres_s[low],
                sound_s[low],
                own[d + 1] * inv_s[low],
                d,
                speed,
            )
            for v in range(5):
                if d == 0:
                    top = roll_rows(tops[0][v], rows - tile_y - tile_y * c)
                else:
                    top = roll_rows(tops[c // tile_y][v], tile_y - 1 - c % tile_y)
                if v == 0:
                    down = jnp.where(edge == 0, star[v], 0.0)
                    up = jnp.where(edge == last, top, 0.0)
                    ph[d, q, c] = down
                else:
                    down = star[v]
                    up = jnp.where(edge == last, top, roll_rows(star[v], -shift))
                out[(v,) + low] = out[(v,) + low] - scale * down
                out[(v,) + high] = out[(v,) + high] + scale * up
        return carry

    def spread_x(v, carry):
        for side in range(2):
            for q in range(4):
                k = q // tile_y
                value = lxr[side, v, k]
                if q % tile_y:
                    value = roll_rows(value, -last_j)
                for c in range(4):
                    place, sub = tile_y * c + last_j, (q * 4 + c) % rows
                    first = roll_rows(theirs[side, v, q * 4 // rows], place - sub)
                    value = jnp.where(row == place, first, value)
                xr[side, v, q] = value
        return carry

    def spread_y(v, carry):
        for side in range(2):
            for k in range(groups):
                if k < kept:
                    value = lyr[side, v, k]
                else:
                    value = None
                    for piece in range(last_i):
                        part = lyr[side, v, (k - kept) * last_i + piece]
                        part = roll_rows(part, piece * tile_y - (rows - tile_y))
                        value = part if value is None else jnp.where(row_i == piece, part, value)
                first = theirs[2 + side, v, k // tile_x]
                first = roll_rows(first, rows - tile_y - (k % tile_x) * tile_y)
                yr[side, v, k // halves, k % halves] = jnp.where(free_y, first, value)
        return carry

    faces[2].wait()
    faces[3].wait()
    lax.fori_loop(0, 5, spread_x, 0)
    lax.fori_loop(0, 4, functools.partial(surface, 0), 0)
    faces[0].wait()
    faces[1].wait()
    lax.fori_loop(0, 5, spread_y, 0)
    lax.fori_loop(0, 4, functools.partial(surface, 1), 0)

    density = [[[out[0, a, b, c] for c in range(4)] for b in range(4)] for a in range(4)]
    for kind, column in enumerate(columns(density, factors, ((0, 0), (0, 3), (3, 0), (3, 3)))):
        low_x = column[0, 0] + up_y_shift(column[0, 3])
        high_x = column[3, 0] + up_y_shift(column[3, 3])
        hess_ref[kind] = low_x + up_x_shift(high_x)

    bottom = row_j == 0
    side_y, side_w = jnp.full(shape, ny_all[1], jnp.float32), jnp.full(shape, wy_all[1], jnp.float32)
    for n in range(1, tile_y):
        side_y = jnp.where(row_i == n, ny_all[1 + n], side_y)
        side_w = jnp.where(row_i == n, wy_all[1 + n], side_w)
    ghost_x = jnp.where(bottom, nx, nx_all[0])
    ghost_y = jnp.where(bottom, py, side_y)
    ghost = jnp.where(bottom, wx, side_w) * wz * float(-time_step / WEIGHTS[3])
    ghost_factors = [ghost * pair for pair in pairs(2.0 / ghost_x, 2.0 / ghost_y, iz)]
    field = [[[None] * 4 for b in range(4)] for a in range(4)]
    for n in range(4):
        for c in range(4):
            from_x = jnp.zeros(shape, jnp.float32)
            for m in range(tile_y):
                place = m * tile_y + last_j
                from_x = jnp.where(row == place, roll_rows(ph[0, n, c], place - m), from_x)
            put(field, 3, n, c, from_x)
            put(field, n, 3, c, ph[1, n, c])
    for kind, column in enumerate(columns(field, ghost_factors, three)):
        total = hess_ref[kind] + jnp.where(bottom, column[0, 3], 0.0)
        total = total + jnp.where(bottom, up_x_shift(column[3, 3]), 0.0)
        for m in range(tile_y):
            place = m * tile_y + last_j
            total = total + jnp.where(row == m, roll_rows(column[3, 0], m - place), 0.0)
            if m < last_j:
                total = total + jnp.where(row == m + 1, roll_rows(column[3, 3], m + 1 - place), 0.0)
        hess_ref[kind] = total

    inverse = 1.0 / ((nx + px) * (ny + py) * (nz + pz))
    for copy in rims:
        copy.wait()
    for kind in range(6):
        total = hess_ref[kind]
        from_x = roll_rows(rxr[kind // tile_x], -tile_y * (kind % tile_x))
        total = total + jnp.where(row_i == 0, from_x, 0.0)
        from_y = roll_rows(ryr[kind // tile_y], -(kind % tile_y))
        total = total + jnp.where(row_j == 0, from_y, 0.0)
        total = total + jnp.where(row == 0, roll_rows(rdr[...], -kind), 0.0)
        hess_ref[kind] = total * inverse


def emit(adv_ref, hess_ref, adv_out, hess_out, sem):
    copies = [
        pltpu.make_async_copy(adv_ref, adv_out, sem.at[0]),
        pltpu.make_async_copy(hess_ref, hess_out, sem.at[1]),
    ]
    for copy in copies:
        copy.start()
    for copy in copies:
        copy.wait()


def solution(mesh):
    sizes = (mesh.shape["gx"], mesh.shape["gy"])

    def local(conserved, troubled_list, widths_x, widths_y, widths_z, speed_x, speed_y, speed_z):
        tile_x, tile_y, column = conserved.shape[4:]
        rows = tile_x * tile_y
        f32 = jnp.float32
        vmem = pl.BlockSpec(memory_space=pltpu.VMEM)
        whole = pl.BlockSpec(memory_space=pl.ANY)
        full = (5, 4, 4, 4, rows, column)
        nodal = (4, 4, 4, rows, column)
        x_face = (2, 5, 4, rows, column)
        y_face = (2, 5, 4, 4 // tile_y, rows, column)
        groups = 4 * (4 // tile_y)
        x_late = (2, 5, 4 // tile_y, rows, column)
        y_late = (2, 5, groups - groups // tile_x, rows, column)
        herald = (4, 5, 16 // rows, rows, column)
        x_rim = (-(-6 // tile_x), rows, column)
        y_rim = (-(-6 // tile_y), rows, column)
        advanced, hessian = pl.pallas_call(
            functools.partial(kernel, tile_x, tile_y, sizes),
            out_shape=(
                pltpu.VMEM(full, f32),
                pltpu.VMEM((6, rows, column), f32),
            ),
            in_specs=[whole] * 9,
            out_specs=(vmem, vmem),
            scratch_shapes=[
                pltpu.VMEM((1, troubled_list.shape[0]), jnp.int32),
                pltpu.SMEM(widths_x.shape, f32),
                pltpu.SMEM(widths_y.shape, f32),
                pltpu.VMEM((1, column), f32),
                pltpu.SMEM(speed_x.shape, f32),
                pltpu.SMEM(speed_y.shape, f32),
                pltpu.VMEM((1, column), f32),
                pltpu.VMEM(full, f32),
                pltpu.VMEM(nodal, f32),
                pltpu.VMEM(nodal, f32),
                pltpu.VMEM(nodal, f32),
                pltpu.VMEM((8, 4, 4, rows, column), f32),
                pltpu.VMEM((5, 4, 4, rows, column), f32),
                pltpu.VMEM((2, 4, 4, rows, column), f32),
                pltpu.VMEM((GEO, rows, column), f32),
                pltpu.VMEM((4, 5, 4, 4, 1, column), f32),
                pltpu.VMEM((4, 5, 4, 4, 1, column), f32),
                pltpu.VMEM(herald, f32),
                pltpu.VMEM(x_late, f32),
                pltpu.VMEM(x_late, f32),
                pltpu.VMEM(y_late, f32),
                pltpu.VMEM(y_late, f32),
                pltpu.VMEM(x_face, f32),
                pltpu.VMEM(x_face, f32),
                pltpu.VMEM(y_face, f32),
                pltpu.VMEM(y_face, f32),
                pltpu.VMEM(x_rim, f32),
                pltpu.VMEM(x_rim, f32),
                pltpu.VMEM(y_rim, f32),
                pltpu.VMEM(y_rim, f32),
                pltpu.VMEM((rows, column), f32),
                pltpu.VMEM((rows, column), f32),
                pltpu.SemaphoreType.DMA((15,)),
                pltpu.SemaphoreType.DMA((11,)),
                pltpu.SemaphoreType.DMA((11,)),
            ],
            compiler_params=pltpu.CompilerParams(collective_id=0, has_side_effects=True),
        )(
            conserved.reshape(full),
            conserved.reshape(full[:5] + (1, column)),
            troubled_list.reshape(1, -1),
            widths_x,
            widths_y,
            widths_z.reshape(1, -1),
            speed_x,
            speed_y,
            speed_z.reshape(1, -1),
        )
        advanced = pltpu.with_memory_space_constraint(advanced, pltpu.VMEM)
        hessian = pltpu.with_memory_space_constraint(hessian, pltpu.VMEM)
        advanced, hessian = pl.pallas_call(
            emit,
            out_shape=(
                jax.ShapeDtypeStruct(full, f32),
                jax.ShapeDtypeStruct((6, rows, column), f32),
            ),
            in_specs=[whole, whole],
            out_specs=(whole, whole),
            scratch_shapes=[pltpu.SemaphoreType.DMA((2,))],
        )(advanced, hessian)
        return advanced.reshape(conserved.shape), hessian.reshape(6, tile_x, tile_y, column)

    in_specs = (
        P(None, None, None, None, "gx", "gy", None),
        P(("gx", "gy")),
        P(),
        P(),
        P(),
        P(),
        P(),
        P(),
    )
    out_specs = (P(None, None, None, None, "gx", "gy", None), P(None, "gx", "gy", None))
    return jax.shard_map(local, mesh=mesh, in_specs=in_specs, out_specs=out_specs, check_vma=False)
```

```python
import functools

import jax
import jax.numpy as jnp
import numpy as np
from jax import lax
from jax.experimental import pallas as pl
from jax.experimental.pallas import tpu as pltpu
from jax.sharding import PartitionSpec as P

MESH = pl.DeviceIdType.MESH
time_step = 0.05
gamma_ratio = 1.4


def lgl_tables():
    nodes = np.array([-1.0, -1.0 / np.sqrt(5.0), 1.0 / np.sqrt(5.0), 1.0])
    weights = np.array([1.0 / 6.0, 5.0 / 6.0, 5.0 / 6.0, 1.0 / 6.0])
    barycentric = np.ones(4)
    for row_a in range(4):
        for row_b in range(4):
            if row_a != row_b:
                barycentric[row_a] = barycentric[row_a] / (nodes[row_a] - nodes[row_b])
    deriv = np.zeros((4, 4))
    for row_a in range(4):
        for row_b in range(4):
            if row_a != row_b:
                deriv[row_a, row_b] = (
                    barycentric[row_b] / barycentric[row_a] / (nodes[row_a] - nodes[row_b])
                )
    for row_a in range(4):
        deriv[row_a, row_a] = -np.sum(deriv[row_a])
    return (nodes, weights, deriv)


NODES, WEIGHTS, DERIV = lgl_tables()
SPEED, INTER, SCALE, FACE = 0, 12, 21, 27
RATIO, MASK, GEO = 33, 34, 35
ALL, DENSITY, REST = (0, 1, 2, 3, 4), (0,), (1, 2, 3, 4)


def primitives(state):
    inverse = 1.0 / state[0]
    square = state[1] * state[1] + state[2] * state[2] + state[3] * state[3]
    pressure = (gamma_ratio - 1.0) * (state[4] - 0.5 * square * inverse)
    ratio = gamma_ratio * pressure * inverse
    return inverse, pressure, ratio * lax.rsqrt(ratio)


def twice_flux(low, p_low, c_low, u_low, high, p_high, c_high, u_high, direction, speed):
    rel_low = u_low - speed
    rel_high = u_high - speed
    fastest = jnp.maximum(jnp.abs(rel_low) + c_low, jnp.abs(rel_high) + c_high)
    left = rel_low + fastest
    right = rel_high - fastest
    flux = [low[v] * left + high[v] * right for v in range(5)]
    flux[direction + 1] = flux[direction + 1] + (p_low + p_high)
    flux[4] = flux[4] + (p_low * u_low + p_high * u_high)
    return flux


def dg_table():
    lifted = DERIV.copy()
    lifted[0, 0] += 1.0 / WEIGHTS[0]
    lifted[3, 3] -= 1.0 / WEIGHTS[3]
    return np.cumsum(2.0 * WEIGHTS[:, None] * lifted, axis=0)


SUBCELL = dg_table()


def dg_fluxes(values):
    outer, inner = values[0] + values[3], values[1] + values[2]
    step = inner - outer
    even = outer + float(0.5 * (SUBCELL[0, 1] + SUBCELL[2, 1])) * step
    middle = outer + float(SUBCELL[1, 1]) * step
    odd = float(0.5 * (SUBCELL[0, 0] - SUBCELL[2, 0])) * (values[0] - values[3])
    odd = odd + float(0.5 * (SUBCELL[0, 1] - SUBCELL[2, 1])) * (values[1] - values[2])
    return even + odd, middle, even - odd


def wave_weights(u_low, c_low, u_high, c_high, speed):
    rel_low = u_low - speed
    rel_high = u_high - speed
    fastest = jnp.maximum(jnp.abs(rel_low) + c_low, jnp.abs(rel_high) + c_high)
    return rel_low + fastest, rel_high - fastest


def kernel(
    tile_x,
    tile_y,
    sizes,
    cons_hbm,
    rows_hbm,
    list_hbm,
    wx_hbm,
    wy_hbm,
    wz_hbm,
    sx_hbm,
    sy_hbm,
    sz_hbm,
    out,
    hess_ref,
    list_ref,
    wx_ref,
    wy_ref,
    wz_ref,
    sx_ref,
    sy_ref,
    sz_ref,
    state,
    inv_s,
    pres_s,
    sound_s,
    zl,
    zst,
    ph,
    geo,
    cs,
    cr,
    theirs,
    lxs,
    lxr,
    lys,
    lyr,
    xs,
    xr,
    ys,
    yr,
    rxs,
    rxr,
    rys,
    ryr,
    rds,
    rdr,
    io_sem,
    send_sem,
    recv_sem,
):
    size_x, size_y = sizes
    rows = tile_x * tile_y
    lanes = state.shape[-1]
    me_x, me_y = lax.axis_index("gx"), lax.axis_index("gy")
    up_x, down_x = lax.rem(me_x + 1, size_x), lax.rem(me_x + size_x - 1, size_x)
    up_y, down_y = lax.rem(me_y + 1, size_y), lax.rem(me_y + size_y - 1, size_y)

    barrier = pltpu.get_barrier_semaphore()
    partners = ((me_x, down_y), (me_x, up_y), (down_x, me_y), (up_x, me_y), (down_x, down_y))
    for partner in partners:
        pl.semaphore_signal(barrier, inc=1, device_id=partner, device_id_type=MESH)
    small = [
        pltpu.make_async_copy(src, dst, io_sem.at[4 + n])
        for n, (src, dst) in enumerate(
            (
                (wx_hbm, wx_ref),
                (wy_hbm, wy_ref),
                (sx_hbm, sx_ref),
                (sy_hbm, sy_ref),
                (wz_hbm, wz_ref),
                (sz_hbm, sz_ref),
                (list_hbm, list_ref),
            )
        )
    ]
    last_i, last_j = tile_x - 1, tile_y - 1
    early = ((0, 0, last_j), (0, 1, rows - 1), (1, 0, rows - tile_y), (1, 1, rows - 1))

    picks = []
    for slot, (d, side, place) in enumerate(early):
        view = rows_hbm.at[:, 3 * side, :, :, place] if d == 0 else rows_hbm.at[:, :, 3 * side, :, place]
        picks.append(pltpu.make_async_copy(view, cs.at[slot], io_sem.at[11 + slot]))
    for slot in (3, 1):
        picks[slot].start()
    loads = [pltpu.make_async_copy(cons_hbm.at[:, a], state.at[:, a], io_sem.at[a]) for a in range(4)]
    for a in (0, 3, 1, 2):
        loads[a].start()
    for slot in (2, 0):
        picks[slot].start()
    for copy in small:
        copy.start()

    shape = (rows, lanes)
    row = lax.broadcasted_iota(jnp.int32, shape, 0)
    row_i, row_j = row // tile_y, row % tile_y

    def roll_rows(value, shift):
        shift = shift % rows
        return value if shift == 0 else pltpu.roll(value, shift, 0)

    def roll_lanes(value, shift):
        return pltpu.roll(value, shift % lanes, 1)

    def pack_x(q, carry):
        for v in range(5):
            for side, node, first in ((0, 0, 0), (1, 3, rows - tile_y)):
                packed = None
                for c in range(4):
                    part = roll_rows(state[v, node, q, c], tile_y * c - first)
                    packed = part if packed is None else jnp.where(row_i == c, part, packed)
                xs[side, v, q] = packed
        return carry

    def pack_y(q, carry):
        for v in range(5):
            for side, node, first in ((0, 0, 0), (1, 3, tile_y - 1)):
                for group in range(4 // tile_y):
                    packed = None
                    for c in range(tile_y):
                        part = roll_rows(state[v, q, node, group * tile_y + c], c - first)
                        packed = part if packed is None else jnp.where(row_j == c, part, packed)
                    ys[side, v, q, group] = packed
        return carry

    def early_node(group, sub):
        return (group * rows + sub) // 4, sub % 4

    def packed_rows(ref, slot, v, group):
        return ref[slot, v, group * (rows // 4) : (group + 1) * (rows // 4)].reshape(shape)

    def remote(src, dst, slot, device):
        return pltpu.make_async_remote_copy(
            src_ref=src,
            dst_ref=dst,
            send_sem=send_sem.at[slot],
            recv_sem=recv_sem.at[slot],
            device_id=device,
            device_id_type=MESH,
        )

    ring_end = jnp.logical_or(me_x == size_x - 1, me_y == size_y - 1)
    heralds = [
        remote(cs.at[2], cr.at[3], 9, (me_x, down_y)),
        remote(cs.at[3], cr.at[2], 10, (me_x, up_y)),
        remote(cs.at[0], cr.at[1], 7, (down_x, me_y)),
        remote(cs.at[1], cr.at[0], 8, (up_x, me_y)),
    ]

    def send_early():
        pl.semaphore_wait(barrier, len(partners))
        for slot, copy in ((3, heralds[1]), (1, heralds[3]), (2, heralds[0]), (0, heralds[2])):
            picks[slot].wait()
            copy.start()

    work_first = jnp.logical_and(me_y == 0, me_x != size_x - 1)
    pack_first = jnp.logical_and(me_y == size_y - 1, me_x != size_x - 1)
    pl.when(jnp.logical_not(jnp.logical_or(work_first, pack_first)))(send_early)
    for copy in small:
        copy.wait()

    def along(ref, start, total, tile, index):
        values = [ref[lax.rem(start + total + i, total)] for i in range(-1, tile + 1)]

        def pick(offset):
            vector = jnp.full(shape, values[1 + offset], jnp.float32)
            for i in range(1, tile):
                vector = jnp.where(index == i, values[1 + offset + i], vector)
            return vector

        return values, pick(-1), pick(0), pick(1)

    total_x, total_y = size_x * tile_x, size_y * tile_y
    wx_all, wx_p, wx, _ = along(wx_ref, me_x * tile_x, total_x, tile_x, row_i)
    wy_all, wy_p, wy, _ = along(wy_ref, me_y * tile_y, total_y, tile_y, row_j)
    sx_all, sx_p, sx, sx_n = along(sx_ref, me_x * tile_x, total_x, tile_x, row_i)
    sy_all, sy_p, sy, sy_n = along(sy_ref, me_y * tile_y, total_y, tile_y, row_j)
    nx_all = [wx_all[i] + time_step * (sx_all[i + 1] - sx_all[i]) for i in range(tile_x + 1)]
    ny_all = [wy_all[i] + time_step * (sy_all[i + 1] - sy_all[i]) for i in range(tile_y + 1)]
    wz = jnp.broadcast_to(wz_ref[...], shape)
    sz = jnp.broadcast_to(sz_ref[...], shape)
    sz_n = roll_lanes(sz, -1)
    nx, ny, nz = (
        wx + time_step * (sx_n - sx),
        wy + time_step * (sy_n - sy),
        wz + time_step * (sz_n - sz),
    )
    px, py = wx_p + time_step * (sx - sx_p), wy_p + time_step * (sy - sy_p)
    pz = roll_lanes(nz, 1)
    mass = nx * ny * nz
    ratio = wx * wy * wz / mass
    geo[RATIO] = ratio
    for d, (width, low, high) in enumerate(((wx, sx, sx_n), (wy, sy, sy_n), (wz, sz, sz_n))):
        for a in range(4):
            geo[SPEED + 4 * d + a] = low * float((1.0 - NODES[a]) / 2.0) + high * float(
                (1.0 + NODES[a]) / 2.0
            )
        for q, xi in enumerate((-5.0 / 6.0, 0.0, 5.0 / 6.0)):
            geo[INTER + 3 * d + q] = low * ((1.0 - xi) / 2.0) + high * ((1.0 + xi) / 2.0)
        geo[FACE + 2 * d] = low
        geo[FACE + 2 * d + 1] = high
        kappa = -time_step * ratio / width
        geo[SCALE + 2 * d] = kappa * float(1.0 / WEIGHTS[0])
        geo[SCALE + 2 * d + 1] = kappa * float(1.0 / WEIGHTS[1])

    entries = list_ref[...]
    count = entries.shape[-1]
    in_row = jnp.where(
        lax.broadcasted_iota(jnp.int32, (rows, count), 0) == entries // lanes, 1.0, 0.0
    )
    in_lane = jnp.where(
        lax.broadcasted_iota(jnp.int32, (lanes, count), 0) == entries % lanes, 1.0, 0.0
    )
    geo[MASK] = lax.dot_general(
        in_row, in_lane, (((1,), (1,)), ((), ())), preferred_element_type=jnp.float32
    )

    def prepare(a, carry):
        for b in range(4):
            for c in range(4):
                inverse, pressure, sound = primitives([state[v, a, b, c] for v in range(5)])
                inv_s[a, b, c] = inverse
                pres_s[a, b, c] = pressure
                sound_s[a, b, c] = sound
            zl[0, a, b] = roll_lanes(state[0, a, b, 3], 1)
            zl[3, a, b] = roll_lanes(state[3, a, b, 3] * inverse, 1)
            zl[5, a, b] = roll_lanes(sound, 1)
        return carry


    def interior(d, parts, first, second):
        def at(n):
            return ((n, first, second), (first, n, second), (first, second, n))[d]

        mask = geo[MASK] > 0.5
        sound = [sound_s[at(n)] for n in range(4)]
        normal = [state[(d + 1,) + at(n)] * inv_s[at(n)] for n in range(4)]
        weights = [
            wave_weights(normal[q], sound[q], normal[q + 1], sound[q + 1], geo[INTER + 3 * d + q])
            for q in range(3)
        ]
        relative = [normal[n] - geo[SPEED + 4 * d + n] for n in range(4)]
        if parts != DENSITY:
            pressure = [pres_s[at(n)] for n in range(4)]
            work = [pressure[n] * normal[n] for n in range(4)]
        if d == 2:
            behind = zl[3, first, second]
            star_left, star_right = wave_weights(
                behind, zl[5, first, second], normal[0], sound[0], geo[FACE + 4]
            )
            if parts != DENSITY:
                push = zl[6, first, second]
        for v in parts:
            value = [state[(v,) + at(n)] for n in range(4)]
            flux = [value[n] * relative[n] for n in range(4)]
            inner = [value[q] * weights[q][0] + value[q + 1] * weights[q][1] for q in range(3)]
            if d == 2:
                if v == 3:
                    rolled = zl[7, first, second]
                else:
                    rolled = zl[v, first, second]
                star = rolled * star_left + value[0] * star_right
            extra = pressure if v == d + 1 else work if v == 4 else None
            if extra is not None:
                flux = [flux[n] + extra[n] for n in range(4)]
                inner = [inner[q] + (extra[q] + extra[q + 1]) for q in range(3)]
            if d == 2:
                if v == 3:
                    star = star + (push + pressure[0])
                if v == 4:
                    star = star + (push * behind + work[0])
                zst[v, first, second] = star
            smooth = dg_fluxes(flux)
            chosen = [jnp.where(mask, inner[q], smooth[q]) for q in range(3)]
            head = chosen[0] - star if d == 2 else chosen[0]
            change = [head, chosen[1] - chosen[0], chosen[2] - chosen[1], -chosen[2]]
            for n in range(4):
                where = (v,) + at(n)
                scale = geo[SCALE + 2 * d + (0 if n in (0, 3) else 1)]
                if d == 0:
                    base = geo[RATIO] * value[n]
                else:
                    base = out[where]
                out[where] = base + scale * change[n]

    def lines(d, parts, width):
        def body(index, carry):
            for step in range(width):
                interior(d, parts, index // (4 // width), index % (4 // width) * width + step)
            return carry

        lax.fori_loop(0, 16 // width, body, 0)

    def above(v, a):
        for b in range(4):
            out[v, a, b, 3] = out[v, a, b, 3] + geo[SCALE + 4] * roll_lanes(zst[v, a, b], -1)


    def paired(body):
        def two(index, carry):
            return body(2 * index + 1, body(2 * index, carry))

        lax.fori_loop(0, 2, two, 0)

    def spots(d, q, c):
        return ((0, q, c), (3, q, c)) if d == 0 else ((q, 0, c), (q, 3, c))

    def inside(d, q, carry):
        shift = (tile_y, 1)[d]
        edge = (row_i, row_j)[d]
        for c in range(4):
            low, high = spots(d, q, c)
            left, right = wave_weights(
                roll_rows(state[(d + 1,) + high] * inv_s[high], shift),
                roll_rows(sound_s[high], shift),
                state[(d + 1,) + low] * inv_s[low],
                sound_s[low],
                geo[FACE + 2 * d],
            )
            star = roll_rows(state[(0,) + high], shift) * left + state[(0,) + low] * right
            star = jnp.where(edge > 0, star, 0.0)
            scale = geo[SCALE + 2 * d]
            out[(0,) + low] = out[(0,) + low] - scale * star
            out[(0,) + high] = out[(0,) + high] + scale * roll_rows(star, -shift)
        return carry


    def first_density():
        lax.fori_loop(0, 4, prepare, 0)
        for d in range(3):
            lines(d, DENSITY, 4)
        for a in range(4):
            above(0, a)
        for d in range(2):
            lax.fori_loop(0, 4, functools.partial(inside, d), 0)

    for a in (0, 3, 1, 2):
        loads[a].wait()

    faces = [
        remote(lys.at[0], lyr.at[1], 2, (me_x, down_y)),
        remote(lys.at[1], lyr.at[0], 3, (me_x, up_y)),
        remote(lxs.at[0], lxr.at[1], 0, (down_x, me_y)),
        remote(lxs.at[1], lxr.at[0], 1, (up_x, me_y)),
    ]
    halves = 4 // tile_y
    groups = 4 * halves
    kept = groups - groups // tile_x
    free_y, free_x = row_i == last_i, row_j == last_j

    def group_of(ref, side, v, k):
        return ref[side, v, k // halves, k % halves]

    def squeeze_y(v, carry):
        for side in range(2):
            for k in range(kept):
                source, piece = kept + k // last_i, k % last_i
                moved = roll_rows(group_of(ys, side, v, source), rows - tile_y - piece * tile_y)
                lys[side, v, k] = jnp.where(free_y, moved, group_of(ys, side, v, k))
        return carry

    def squeeze_x(v, carry):
        for side in range(2):
            for k in range(4 // tile_y):
                moved = roll_rows(xs[side, v, tile_y * k + 1], last_j)
                lxs[side, v, k] = jnp.where(free_x, moved, xs[side, v, tile_y * k])
        return carry

    pl.when(work_first)(first_density)
    lax.fori_loop(0, 4, pack_y, 0)
    lax.fori_loop(0, 5, squeeze_y, 0)
    lax.fori_loop(0, 4, pack_x, 0)
    lax.fori_loop(0, 5, squeeze_x, 0)
    pl.when(jnp.logical_or(work_first, pack_first))(send_early)

    def send_y():
        faces[0].start()
        faces[1].start()

    held_back = jnp.logical_and(me_x == size_x - 1, me_y != size_y - 1)
    pl.when(jnp.logical_not(held_back))(send_y)
    faces[2].start()
    faces[3].start()

    pl.when(jnp.logical_not(work_first))(first_density)

    second = DERIV @ DERIV
    ends = (0, 3)

    def combine(coefficients, values):
        total = None
        for n in range(4):
            if values[n] is not None:
                term = float(coefficients[n]) * values[n]
                total = term if total is None else total + term
        return total

    def columns(density, factors, wanted):
        along_x = {
            (p, b, c): combine(DERIV[p], [density[a][b][c] for a in range(4)])
            for p in ends
            for b in range(4)
            for c in range(4)
            if b in ends or c in ends
        }
        along_y = {
            (a, q, c): combine(DERIV[q], [density[a][b][c] for b in range(4)])
            for q in ends
            for a in ends
            for c in range(4)
        }

        def corner(kind, p, q, r):
            if kind == 0:
                return combine(second[p], [density[a][q][r] for a in range(4)])
            if kind == 1:
                return combine(second[q], [density[p][b][r] for b in range(4)])
            if kind == 2:
                return combine(second[r], [density[p][q][c] for c in range(4)])
            if kind == 3:
                return combine(DERIV[q], [along_x[p, b, r] for b in range(4)])
            if kind == 4:
                return combine(DERIV[r], [along_x[p, q, c] for c in range(4)])
            return combine(DERIV[r], [along_y[p, q, c] for c in range(4)])

        found = []
        for kind in range(6):
            column = {}
            for p, q in wanted:
                low, high = corner(kind, p, q, 0), corner(kind, p, q, 3)
                column[p, q] = factors[kind] * low + roll_lanes(factors[kind] * high, 1)
            found.append(column)
        return found

    def pairs(jx, jy, jz):
        return (jx * jx, jy * jy, jz * jz, jx * jy, jx * jz, jy * jz)

    ix, iy, iz = 2.0 / nx, 2.0 / ny, 2.0 / nz
    factors = [mass * pair for pair in pairs(ix, iy, iz)]

    def up_y_shift(value):
        return jnp.where(row_j == 0, 0.0, roll_rows(value, 1))

    def up_x_shift(value):
        return jnp.where(row_i == 0, 0.0, roll_rows(value, tile_y))

    three = ((0, 3), (3, 0), (3, 3))
    density = [[[out[0, a, b, c] for c in range(4)] for b in range(4)] for a in range(4)]
    x_rim, y_rim = [None] * -(-6 // tile_x), [None] * -(-6 // tile_y)
    d_rim = None
    for kind, column in enumerate(columns(density, factors, three)):
        high_x = column[3, 0] + up_y_shift(column[3, 3])
        slot, place = kind // tile_x, kind % tile_x
        part = roll_rows(high_x, tile_y * place - (rows - tile_y))
        x_rim[slot] = part if place == 0 else jnp.where(row_i == place, part, x_rim[slot])
        rim = column[0, 3] + up_x_shift(column[3, 3])
        slot, place = kind // tile_y, kind % tile_y
        part = roll_rows(rim, place - last_j)
        y_rim[slot] = part if place == 0 else jnp.where(row_j == place, part, y_rim[slot])
        part = roll_rows(column[3, 3], kind - (rows - 1))
        d_rim = part if kind == 0 else jnp.where(row == kind, part, d_rim)
    for slot, value in enumerate(x_rim):
        rxs[slot] = value
    for slot, value in enumerate(y_rim):
        rys[slot] = value
    rds[...] = d_rim
    rims = [
        remote(rds, rdr, 6, (up_x, up_y)),
        remote(rys, ryr, 5, (me_x, up_y)),
        remote(rxs, rxr, 4, (up_x, me_y)),
    ]
    rims[0].start()
    pl.when(held_back)(send_y)

    def behind_rest(a, carry):
        for b in range(4):
            zl[1, a, b] = roll_lanes(state[1, a, b, 3], 1)
            zl[2, a, b] = roll_lanes(state[2, a, b, 3], 1)
            zl[7, a, b] = roll_lanes(state[3, a, b, 3], 1)
            zl[4, a, b] = roll_lanes(state[4, a, b, 3], 1)
            zl[6, a, b] = roll_lanes(pres_s[a, b, 3], 1)
        return carry

    def above_rest(a, carry):
        for v in REST:
            above(v, a)
        return carry

    def rest():
        lax.fori_loop(0, 4, behind_rest, 0)
        for d in range(3):
            lines(d, REST, 2)
        lax.fori_loop(0, 4, above_rest, 0)

    pl.when(jnp.logical_not(ring_end))(rest)

    row_up_x, row_low_x, row_under_x = 3, last_j, last_j - 1
    row_up_y, row_low_y, row_under_y = rows - 1, rows - tile_y, rows - tile_y - 1
    is_x = row <= row_up_x
    lower = jnp.logical_or(row == row_low_x, row == row_low_y)
    part_x = jnp.where(row == row_under_x, nx_all[0], jnp.where(row == row_low_x, nx_all[1], nx_all[tile_x]))
    part_y = jnp.where(row == row_under_y, ny_all[0], jnp.where(row == row_low_y, ny_all[1], ny_all[tile_y]))
    across = jnp.where(is_x, wy_all[tile_y], wx_all[tile_x])
    part = jnp.where(lower, 1.0, -1.0) * across * wz * float(time_step / WEIGHTS[3])
    part_factors = [part * pair for pair in pairs(2.0 / part_x, 2.0 / part_y, iz)]

    def waves(ref, slot, group, keep):
        d = early[slot][0]
        fields = [packed_rows(ref, slot, v, group) for v in range(5)]
        if keep:
            for v in range(5):
                theirs[slot, v, group] = fields[v]
        inverse, _, sound = primitives(fields)
        return fields[0], fields[d + 1] * inverse, sound

    def own_waves(d):
        return [[waves(cs, 2 * d + side, group, False) for group in range(16 // rows)] for side in range(2)]

    def face_stars(slot, mine):
        d, side, place = early[slot]
        found = []
        for group in range(16 // rows):
            own, other = mine[side][group], waves(cr, slot, group, True)
            low, high = (other, own) if side == 0 else (own, other)
            speed = geo[FACE + 2 * d + side, place : place + 1]
            left, right = wave_weights(low[1], low[2], high[1], high[2], speed)
            found.append(low[0] * left + high[0] * right)
        return found

    def put(field, a, b, c, value):
        old = field[a][b][c]
        field[a][b][c] = value if old is None else old + value

    def part_field(d, mine):
        field = [[[None] * 4 for b in range(4)] for a in range(4)]
        lows, ups = face_stars(2 * d, mine), face_stars(2 * d + 1, mine)
        up_row, low_row = (row_up_x, row_up_y)[d], (row_low_x, row_low_y)[d]
        under_row = (row_under_x, row_under_y)[d]
        for group in range(16 // rows):
            for sub in range(rows):
                q, c = early_node(group, sub)
                top, floor = ((3, q, c), (0, q, c)) if d == 0 else ((q, 3, c), (q, 0, c))
                value = jnp.where(row == up_row, roll_rows(ups[group], up_row - sub), 0.0)
                below = roll_rows(lows[group], under_row - sub)
                put(field, *top, jnp.where(row == under_row, below, value))
                low = roll_rows(lows[group], low_row - sub)
                put(field, *floor, jnp.where(row == low_row, low, 0.0))
        return field

    def y_part():
        mine = own_waves(0)
        heralds[2].wait()
        heralds[3].wait()
        y_rim = [None] * -(-6 // tile_y)
        for kind, column in enumerate(columns(part_field(0, mine), part_factors, ((0, 3), (3, 3)))):
            near = jnp.where(row == last_j, column[0, 3] + roll_rows(column[3, 3], 1), 0.0)
            near = jnp.where(row == last_j + tile_y, roll_rows(column[3, 3], tile_y), near)
            rim = jnp.where(row == rows - 1, roll_rows(column[0, 3], rows - 1 - row_up_x), near)
            slot, place = kind // tile_y, kind % tile_y
            part = roll_rows(rim, place - last_j)
            y_rim[slot] = part if place == 0 else jnp.where(row_j == place, part, y_rim[slot])
        for slot, value in enumerate(y_rim):
            rys[slot] = rys[slot] + value
        rims[1].start()

    def x_part():
        mine = own_waves(1)
        heralds[0].wait()
        heralds[1].wait()
        x_rim = [None] * -(-6 // tile_x)
        for kind, column in enumerate(columns(part_field(1, mine), part_factors, ((3, 0), (3, 3)))):
            high_x = column[3, 0] + roll_rows(column[3, 3], 1)
            slot, place = kind // tile_x, kind % tile_x
            part = roll_rows(high_x, tile_y * place - (rows - tile_y))
            x_rim[slot] = part if place == 0 else jnp.where(row_i == place, part, x_rim[slot])
        for slot, value in enumerate(x_rim):
            rxs[slot] = rxs[slot] + value
        rims[2].start()

    first_x = me_x == size_x - 1
    pl.when(first_x)(x_part)
    y_part()
    pl.when(jnp.logical_not(first_x))(x_part)
    pl.when(ring_end)(rest)

    def surface(d, q, carry):
        shift = (tile_y, 1)[d]
        edge, last = ((row_i, last_i), (row_j, last_j))[d]
        speed = geo[FACE + 2 * d]
        top_speed = geo[FACE + 2 * d + 1, rows - 1 : rows]
        scale = geo[SCALE + 2 * d]
        tops = []
        for group in range(1 if d == 0 else 4 // tile_y):
            if d == 0:
                own = [xs[1, v, q] for v in range(5)]
                other = [xr[1, v, q] for v in range(5)]
            else:
                own = [ys[1, v, q, group] for v in range(5)]
                other = [yr[1, v, q, group] for v in range(5)]
            own_inverse, own_pressure, own_sound = primitives(own)
            inverse, pressure, sound = primitives(other)
            tops.append(
                twice_flux(
                    own,
                    own_pressure,
                    own_sound,
                    own[d + 1] * own_inverse,
                    other,
                    pressure,
                    sound,
                    other[d + 1] * inverse,
                    d,
                    top_speed,
                )
            )
        for c in range(4):
            low, high = spots(d, q, c)
            own = [state[(v,) + low] for v in range(5)]
            other = []
            for v in range(5):
                if d == 0:
                    halo = roll_rows(xr[0, v, q], -tile_y * c)
                else:
                    halo = roll_rows(yr[0, v, q, c // tile_y], -(c % tile_y))
                moved = roll_rows(state[(v,) + high], shift)
                other.append(jnp.where(edge == 0, halo, moved))
            inverse, pressure, sound = primitives(other)
            star = twice_flux(
                other,
                pressure,
                sound,
                other[d + 1] * inverse,
                own,
                pres_s[low],
                sound_s[low],
                own[d + 1] * inv_s[low],
                d,
                speed,
            )
            for v in range(5):
                if d == 0:
                    top = roll_rows(tops[0][v], rows - tile_y - tile_y * c)
                else:
                    top = roll_rows(tops[c // tile_y][v], tile_y - 1 - c % tile_y)
                if v == 0:
                    down = jnp.where(edge == 0, star[v], 0.0)
                    up = jnp.where(edge == last, top, 0.0)
                    ph[d, q, c] = down
                else:
                    down = star[v]
                    up = jnp.where(edge == last, top, roll_rows(star[v], -shift))
                out[(v,) + low] = out[(v,) + low] - scale * down
                out[(v,) + high] = out[(v,) + high] + scale * up
        return carry

    def spread_x(v, carry):
        for side in range(2):
            for q in range(4):
                k = q // tile_y
                value = lxr[side, v, k]
                if q % tile_y:
                    value = roll_rows(value, -last_j)
                for c in range(4):
                    place, sub = tile_y * c + last_j, (q * 4 + c) % rows
                    first = roll_rows(theirs[side, v, q * 4 // rows], place - sub)
                    value = jnp.where(row == place, first, value)
                xr[side, v, q] = value
        return carry

    def spread_y(v, carry):
        for side in range(2):
            for k in range(groups):
                if k < kept:
                    value = lyr[side, v, k]
                else:
                    value = None
                    for piece in range(last_i):
                        part = lyr[side, v, (k - kept) * last_i + piece]
                        part = roll_rows(part, piece * tile_y - (rows - tile_y))
                        value = part if value is None else jnp.where(row_i == piece, part, value)
                first = theirs[2 + side, v, k // tile_x]
                first = roll_rows(first, rows - tile_y - (k % tile_x) * tile_y)
                yr[side, v, k // halves, k % halves] = jnp.where(free_y, first, value)
        return carry

    faces[2].wait()
    faces[3].wait()
    lax.fori_loop(0, 5, spread_x, 0)
    paired(functools.partial(surface, 0))
    faces[0].wait()
    faces[1].wait()
    lax.fori_loop(0, 5, spread_y, 0)
    paired(functools.partial(surface, 1))

    density = [[[out[0, a, b, c] for c in range(4)] for b in range(4)] for a in range(4)]
    for kind, column in enumerate(columns(density, factors, ((0, 0), (0, 3), (3, 0), (3, 3)))):
        low_x = column[0, 0] + up_y_shift(column[0, 3])
        high_x = column[3, 0] + up_y_shift(column[3, 3])
        hess_ref[kind] = low_x + up_x_shift(high_x)

    bottom = row_j == 0
    side_y, side_w = jnp.full(shape, ny_all[1], jnp.float32), jnp.full(shape, wy_all[1], jnp.float32)
    for n in range(1, tile_y):
        side_y = jnp.where(row_i == n, ny_all[1 + n], side_y)
        side_w = jnp.where(row_i == n, wy_all[1 + n], side_w)
    ghost_x = jnp.where(bottom, nx, nx_all[0])
    ghost_y = jnp.where(bottom, py, side_y)
    ghost = jnp.where(bottom, wx, side_w) * wz * float(-time_step / WEIGHTS[3])
    ghost_factors = [ghost * pair for pair in pairs(2.0 / ghost_x, 2.0 / ghost_y, iz)]
    field = [[[None] * 4 for b in range(4)] for a in range(4)]
    for n in range(4):
        for c in range(4):
            from_x = jnp.zeros(shape, jnp.float32)
            for m in range(tile_y):
                place = m * tile_y + last_j
                from_x = jnp.where(row == place, roll_rows(ph[0, n, c], place - m), from_x)
            put(field, 3, n, c, from_x)
            put(field, n, 3, c, ph[1, n, c])
    for kind, column in enumerate(columns(field, ghost_factors, three)):
        total = hess_ref[kind] + jnp.where(bottom, column[0, 3], 0.0)
        total = total + jnp.where(bottom, up_x_shift(column[3, 3]), 0.0)
        for m in range(tile_y):
            place = m * tile_y + last_j
            total = total + jnp.where(row == m, roll_rows(column[3, 0], m - place), 0.0)
            if m < last_j:
                total = total + jnp.where(row == m + 1, roll_rows(column[3, 3], m + 1 - place), 0.0)
        hess_ref[kind] = total

    inverse = 1.0 / ((nx + px) * (ny + py) * (nz + pz))
    for copy in rims:
        copy.wait()
    for kind in range(6):
        total = hess_ref[kind]
        from_x = roll_rows(rxr[kind // tile_x], -tile_y * (kind % tile_x))
        total = total + jnp.where(row_i == 0, from_x, 0.0)
        from_y = roll_rows(ryr[kind // tile_y], -(kind % tile_y))
        total = total + jnp.where(row_j == 0, from_y, 0.0)
        total = total + jnp.where(row == 0, roll_rows(rdr[...], -kind), 0.0)
        hess_ref[kind] = total * inverse


def emit(adv_ref, hess_ref, adv_out, hess_out, sem):
    copies = [
        pltpu.make_async_copy(adv_ref, adv_out, sem.at[0]),
        pltpu.make_async_copy(hess_ref, hess_out, sem.at[1]),
    ]
    for copy in copies:
        copy.start()
    for copy in copies:
        copy.wait()


def solution(mesh):
    sizes = (mesh.shape["gx"], mesh.shape["gy"])

    def local(conserved, troubled_list, widths_x, widths_y, widths_z, speed_x, speed_y, speed_z):
        tile_x, tile_y, column = conserved.shape[4:]
        rows = tile_x * tile_y
        f32 = jnp.float32
        vmem = pl.BlockSpec(memory_space=pltpu.VMEM)
        whole = pl.BlockSpec(memory_space=pl.ANY)
        full = (5, 4, 4, 4, rows, column)
        nodal = (4, 4, 4, rows, column)
        x_face = (2, 5, 4, rows, column)
        y_face = (2, 5, 4, 4 // tile_y, rows, column)
        groups = 4 * (4 // tile_y)
        x_late = (2, 5, 4 // tile_y, rows, column)
        y_late = (2, 5, groups - groups // tile_x, rows, column)
        herald = (4, 5, 16 // rows, rows, column)
        x_rim = (-(-6 // tile_x), rows, column)
        y_rim = (-(-6 // tile_y), rows, column)
        advanced, hessian = pl.pallas_call(
            functools.partial(kernel, tile_x, tile_y, sizes),
            out_shape=(
                pltpu.VMEM(full, f32),
                pltpu.VMEM((6, rows, column), f32),
            ),
            in_specs=[whole] * 9,
            out_specs=(vmem, vmem),
            scratch_shapes=[
                pltpu.VMEM((1, troubled_list.shape[0]), jnp.int32),
                pltpu.SMEM(widths_x.shape, f32),
                pltpu.SMEM(widths_y.shape, f32),
                pltpu.VMEM((1, column), f32),
                pltpu.SMEM(speed_x.shape, f32),
                pltpu.SMEM(speed_y.shape, f32),
                pltpu.VMEM((1, column), f32),
                pltpu.VMEM(full, f32),
                pltpu.VMEM(nodal, f32),
                pltpu.VMEM(nodal, f32),
                pltpu.VMEM(nodal, f32),
                pltpu.VMEM((8, 4, 4, rows, column), f32),
                pltpu.VMEM((5, 4, 4, rows, column), f32),
                pltpu.VMEM((2, 4, 4, rows, column), f32),
                pltpu.VMEM((GEO, rows, column), f32),
                pltpu.VMEM((4, 5, 4, 4, 1, column), f32),
                pltpu.VMEM((4, 5, 4, 4, 1, column), f32),
                pltpu.VMEM(herald, f32),
                pltpu.VMEM(x_late, f32),
                pltpu.VMEM(x_late, f32),
                pltpu.VMEM(y_late, f32),
                pltpu.VMEM(y_late, f32),
                pltpu.VMEM(x_face, f32),
                pltpu.VMEM(x_face, f32),
                pltpu.VMEM(y_face, f32),
                pltpu.VMEM(y_face, f32),
                pltpu.VMEM(x_rim, f32),
                pltpu.VMEM(x_rim, f32),
                pltpu.VMEM(y_rim, f32),
                pltpu.VMEM(y_rim, f32),
                pltpu.VMEM((rows, column), f32),
                pltpu.VMEM((rows, column), f32),
                pltpu.SemaphoreType.DMA((15,)),
                pltpu.SemaphoreType.DMA((11,)),
                pltpu.SemaphoreType.DMA((11,)),
            ],
            compiler_params=pltpu.CompilerParams(collective_id=0, has_side_effects=True),
        )(
            conserved.reshape(full),
            conserved.reshape(full[:5] + (1, column)),
            troubled_list.reshape(1, -1),
            widths_x,
            widths_y,
            widths_z.reshape(1, -1),
            speed_x,
            speed_y,
            speed_z.reshape(1, -1),
        )
        advanced = pltpu.with_memory_space_constraint(advanced, pltpu.VMEM)
        hessian = pltpu.with_memory_space_constraint(hessian, pltpu.VMEM)
        advanced, hessian = pl.pallas_call(
            emit,
            out_shape=(
                jax.ShapeDtypeStruct(full, f32),
                jax.ShapeDtypeStruct((6, rows, column), f32),
            ),
            in_specs=[whole, whole],
            out_specs=(whole, whole),
            scratch_shapes=[pltpu.SemaphoreType.DMA((2,))],
        )(advanced, hessian)
        return advanced.reshape(conserved.shape), hessian.reshape(6, tile_x, tile_y, column)

    in_specs = (
        P(None, None, None, None, "gx", "gy", None),
        P(("gx", "gy")),
        P(),
        P(),
        P(),
        P(),
        P(),
        P(),
    )
    out_specs = (P(None, None, None, None, "gx", "gy", None), P(None, "gx", "gy", None))
    return jax.shard_map(local, mesh=mesh, in_specs=in_specs, out_specs=out_specs, check_vma=False)
```
